256 devices in a mesh: chan: 2 (over core), ens: 16 (over y, z_lo), lat: 8 (over z_hi, x).
Axes of the slice: x: 4, y: 4, z: 8 (z_hi: 2, z_lo: 4; z = z_hi * 4 + z_lo), core: 2. Of those that a mesh axis runs over, the one named last changes fastest.
Arguments:
- model_outputs: bfloat16 [16, 2, 720, 1440], P('ens', 'chan', 'lat'), may hold values from -340 to 340
- verifying_truth: bfloat16 [2, 720, 1440], P('chan', 'lat', 'ens'), may hold values from -250 to 250
Outputs:
- scaled_gradient: float32 [16, 2, 720, 1440], P('ens', 'chan', 'lat')
- ensemble_loss: float32 [], replicated
The draws below stay inside these ranges and needn't reach their ends.
All inputs are finite; a program needn't handle non-finite values.
Results may differ from the reference program's by a relative error of at most 0.02.
The reference program's roundings to bfloat16 on the way count: a program that leaves them out, or rounds other values in their place, can miss the bound.
Values may be sent and summed in bfloat16 or wider, within the bound.
A program may use at most 64 MiB of HBM per device.

```python
import math
import jax
import jax.numpy as jnp
from jax import lax

PARALLEL_LINES = 720
AZIMUTH_STEPS = 1440
DEGREE_CUTOFF = 384
LAYER_TOTAL = 2
MEMBERS = 16


def smooth_waves(key, count):
    key_amp, key_phase = jax.random.split(key)
    amplitude = jax.random.uniform(key_amp, (count, 8, 4), jnp.float32, -1.0, 1.0) * 0.25
    phases = jax.random.uniform(key_phase, (count, 8, 4), jnp.float32, -math.pi, math.pi)
    longitude = 2.0 * math.pi * jnp.arange(AZIMUTH_STEPS, dtype=jnp.float32) / AZIMUTH_STEPS
    wavenumbers = jnp.arange(8, dtype=jnp.float32)
    waves = amplitude[..., None] * jnp.cos(wavenumbers[None, :, None, None] * longitude[None, None, None, :] + phases[..., None])
    colatitude = math.pi * (jnp.arange(PARALLEL_LINES, dtype=jnp.float32) + 0.5) / PARALLEL_LINES
    powers = jnp.cos(colatitude)[None, :] ** jnp.arange(4, dtype=jnp.float32)[:, None]
    return jnp.einsum('ckqn,qj->cjn', waves, powers)


def truth_parts(key):
    keys = jax.random.split(jax.random.fold_in(key, 11), 4)
    chan_scale = 0.3 * jnp.exp(math.log(10.0) * (jnp.arange(LAYER_TOTAL, dtype=jnp.float32) + jax.random.uniform(keys[0], (LAYER_TOTAL,))) / LAYER_TOTAL)
    lat_factor = 1.0 + 2.0 * (jnp.arange(PARALLEL_LINES, dtype=jnp.float32) + jax.random.uniform(keys[1], (PARALLEL_LINES,))) / PARALLEL_LINES
    smooth = smooth_waves(keys[2], LAYER_TOTAL)
    rough = jax.random.truncated_normal(keys[3], -5.0, 5.0, (LAYER_TOTAL, PARALLEL_LINES, AZIMUTH_STEPS), jnp.float32)
    scaling = chan_scale[:, None, None] * lat_factor[None, :, None]
    return (scaling, scaling * (rough + 1.5 * smooth))


def draw_verifying_truth(key, part):
    scaling, field = truth_parts(key)
    return field.astype(jnp.bfloat16)


def draw_model_outputs(key, part):
    scaling, field = truth_parts(key)
    key_noise, key_wave = jax.random.split(jax.random.fold_in(key, 23))
    noise = jax.random.truncated_normal(key_noise, -5.0, 5.0, (MEMBERS, LAYER_TOTAL, PARALLEL_LINES, AZIMUTH_STEPS), jnp.float32)
    wobble = smooth_waves(key_wave, MEMBERS * LAYER_TOTAL).reshape(MEMBERS, LAYER_TOTAL, PARALLEL_LINES, AZIMUTH_STEPS)
    return (field[None] + scaling[None] * (0.6 * noise + 0.8 * wobble)).astype(jnp.bfloat16)


def setup_inputs(seed: int = 0) -> dict:
    streams_of = jax.random.split(jax.random.key(seed), 3)
    return {
        "model_outputs": draw_model_outputs(jax.random.fold_in(streams_of[2], 71), 0),
        "verifying_truth": draw_verifying_truth(jax.random.fold_in(streams_of[2], 71), 0),
    }


SOFTENING_EPS = 0.25
SPECTRAL_WEIGHT = 0.1

def dft_table():
    longitude = jnp.arange(AZIMUTH_STEPS, dtype=jnp.int32)[:, None]
    wavenumber = jnp.arange(DEGREE_CUTOFF, dtype=jnp.int32)[None, :]
    phase = (longitude * wavenumber % AZIMUTH_STEPS).astype(jnp.float32) * (2.0 * math.pi / AZIMUTH_STEPS)
    stacked = jnp.stack([jnp.cos(phase), -jnp.sin(phase)], axis=-1)
    return stacked.reshape(AZIMUTH_STEPS, 2 * DEGREE_CUTOFF).astype(jnp.bfloat16)

def lat_rows(first_row, count):
    rows_index = (first_row + jnp.arange(count, dtype=jnp.int32)).astype(jnp.float32)
    colatitude = math.pi * (rows_index + 0.5) / PARALLEL_LINES
    return (jnp.cos(colatitude), jnp.sin(colatitude))

def seed_log(order_values):
    factors = jnp.arange(1, DEGREE_CUTOFF + 1, dtype=jnp.int32).astype(jnp.float32)[None, :]
    summands = jnp.where(factors <= order_values[:, None], jnp.log1p(-0.5 / factors), 0.0)
    return 0.5 * jnp.log(order_values + 0.5) + 0.5 * lax.optimization_barrier(jnp.sum(summands, axis=1))

def legendre_table(order_values, cos_lat, sin_lat):
    order_col = order_values[:, None]
    start_log = seed_log(order_values)[:, None] + order_col * jnp.log(sin_lat)[None, :]
    cos_row = cos_lat[None, :]
    state_shape = (order_values.shape[0], cos_lat.shape[0])

    def recur(carry, degree_index):
        latest, before, log_scale = carry
        degree = degree_index.astype(jnp.float32)
        growing = degree > order_col
        denominator = jnp.where(growing, degree * degree - order_col * order_col, 1.0)
        leading = jnp.sqrt(jnp.maximum(4.0 * degree * degree - 1.0, 0.0) / denominator)
        trailing = jnp.sqrt(jnp.maximum(((degree - 1.0) ** 2 - order_col * order_col) * (2.0 * degree + 1.0) / ((2.0 * degree - 3.0) * denominator), 0.0))
        advanced = leading * cos_row * latest - trailing * before
        next_latest = jnp.where(growing, advanced, latest)
        next_before = jnp.where(growing, latest, before)
        largest = jnp.maximum(jnp.abs(next_latest), jnp.abs(next_before))
        next_latest = next_latest / largest
        next_before = next_before / largest
        next_log = log_scale + jnp.log(largest)
        value = jnp.where(degree >= order_col, next_latest * jnp.exp(next_log), 0.0)
        return ((next_latest, next_before, next_log), value)
    initial = (jnp.ones(state_shape, cos_lat.dtype), jnp.zeros(state_shape, cos_lat.dtype), start_log)
    unused, stacked = lax.scan(recur, initial, jnp.arange(DEGREE_CUTOFF, dtype=jnp.int32), unroll=16)
    legendre = jnp.transpose(stacked, (1, 2, 0))
    weights = math.pi / PARALLEL_LINES * sin_lat
    return (weights[None, :, None] * legendre).astype(jnp.bfloat16)

def coefficient_parts(expansion_terms, azimuth_wavenumber, prediction_draws):
    degree = jnp.arange(DEGREE_CUTOFF, dtype=jnp.int32).astype(jnp.float32)
    retained = (degree >= azimuth_wavenumber).astype(jnp.float32)
    draw_stack = expansion_terms[:prediction_draws]
    pivot_term = expansion_terms[prediction_draws:]
    observed_gap = draw_stack - pivot_term
    observed_length = jnp.sqrt(observed_gap[:, :, 0] ** 2 + observed_gap[:, :, 1] ** 2 + SOFTENING_EPS ** 2)
    couple_gap = draw_stack[:, None] - draw_stack[None]
    couple_length = jnp.sqrt(couple_gap[:, :, :, 0] ** 2 + couple_gap[:, :, :, 1] ** 2 + SOFTENING_EPS ** 2)
    power_score = lax.optimization_barrier(jnp.sum(observed_length, axis=0)) - (lax.optimization_barrier(jnp.sum(couple_length, axis=(0, 1))) - prediction_draws * SOFTENING_EPS) / (2.0 * (prediction_draws - 1))
    penalty_piece = jnp.sum(retained * power_score)
    step_downhill = observed_gap / observed_length[:, :, None] - lax.optimization_barrier(jnp.sum(couple_gap / couple_length[:, :, :, None], axis=1)) / (prediction_draws - 1)
    scale_factor = SPECTRAL_WEIGHT * PARALLEL_LINES * AZIMUTH_STEPS / (DEGREE_CUTOFF * (DEGREE_CUTOFF + 1) / 2)
    upstream_grad = (scale_factor * retained * step_downhill).astype(jnp.bfloat16)
    return (penalty_piece, upstream_grad)

def reference(model_outputs, verifying_truth):
    prediction_draws = model_outputs.shape[0]
    globe_degree_table = dft_table()
    cos_lat, sin_lat = lat_rows(0, PARALLEL_LINES)
    draw_azimuth_spectra = jnp.dot(model_outputs.reshape(-1, AZIMUTH_STEPS), globe_degree_table, preferred_element_type=jnp.float32).astype(jnp.bfloat16)
    target_azimuth_spectra = jnp.dot(verifying_truth.reshape(-1, AZIMUTH_STEPS), globe_degree_table, preferred_element_type=jnp.float32).astype(jnp.bfloat16)
    azimuth_spectra = jnp.concatenate([draw_azimuth_spectra.reshape(prediction_draws, LAYER_TOTAL, PARALLEL_LINES, DEGREE_CUTOFF, 2), target_azimuth_spectra.reshape(1, LAYER_TOTAL, PARALLEL_LINES, DEGREE_CUTOFF, 2)], axis=0)
    azimuth_spectra = jnp.transpose(azimuth_spectra, (3, 0, 1, 4, 2)).reshape(DEGREE_CUTOFF, (prediction_draws + 1) * LAYER_TOTAL * 2, PARALLEL_LINES)
    orders = jnp.arange(DEGREE_CUTOFF, dtype=jnp.int32).astype(jnp.float32)

    def per_order(packed):
        azimuth_wavenumber, order_lines = packed
        scaled_result = legendre_table(azimuth_wavenumber[None], cos_lat, sin_lat)[0]
        expansion_terms = jnp.dot(order_lines, scaled_result, preferred_element_type=jnp.float32).reshape(prediction_draws + 1, LAYER_TOTAL, 2, DEGREE_CUTOFF)
        penalty_piece, upstream_grad = coefficient_parts(expansion_terms, azimuth_wavenumber, prediction_draws)
        backward_map = jnp.dot(upstream_grad.reshape(-1, DEGREE_CUTOFF), scaled_result.T, preferred_element_type=jnp.float32).astype(jnp.bfloat16)
        return (penalty_piece, backward_map)
    losses, backward_map = lax.map(per_order, (orders, azimuth_spectra))
    backward_map = jnp.transpose(backward_map.reshape(DEGREE_CUTOFF, prediction_draws, LAYER_TOTAL, 2, PARALLEL_LINES), (1, 2, 4, 0, 3)).reshape(-1, 2 * DEGREE_CUTOFF)
    coefficient_slope = jnp.dot(backward_map, globe_degree_table.T, preferred_element_type=jnp.float32).reshape(prediction_draws, LAYER_TOTAL, PARALLEL_LINES, AZIMUTH_STEPS)
    gridded_quantity = model_outputs.astype(jnp.float32)
    target = verifying_truth.astype(jnp.float32)
    line_factor = sin_lat[None, :, None]

    def per_member(single_draw):
        observed_polarity = jnp.sign(single_draw - target)
        observed_magnitude = jnp.sum(line_factor * jnp.abs(single_draw - target))

        def add_into(position, running):
            pair_gap = single_draw - gridded_quantity[position]
            return (running[0] + jnp.sign(pair_gap), running[1] + jnp.sum(line_factor * jnp.abs(pair_gap)))
        polarity_accum, couple_magnitude = lax.fori_loop(0, prediction_draws, add_into, (jnp.zeros_like(single_draw), jnp.zeros((), jnp.float32)))
        tally_numbers = ((prediction_draws - 1) * observed_polarity - polarity_accum).astype(jnp.bfloat16)
        return (tally_numbers, observed_magnitude, couple_magnitude)
    tally_numbers, observed_magnitude, couple_magnitude = lax.map(per_member, gridded_quantity)
    nodal_penalty = (jnp.sum(observed_magnitude) - jnp.sum(couple_magnitude) / (2.0 * (prediction_draws - 1))) / (PARALLEL_LINES * AZIMUTH_STEPS)
    slope_result = line_factor[None] * tally_numbers.astype(jnp.float32) / (prediction_draws - 1) + coefficient_slope
    ensemble_loss = nodal_penalty + SPECTRAL_WEIGHT / (DEGREE_CUTOFF * (DEGREE_CUTOFF + 1) / 2) * jnp.sum(losses)
    return (slope_result, ensemble_loss)
```

```python
import functools
import math

import jax
import jax.numpy as jnp
from jax import lax
from jax.experimental import pallas as pl
from jax.experimental.pallas import tpu as pltpu
from jax.sharding import PartitionSpec as P

PARALLEL_LINES = 720
AZIMUTH_STEPS = 1440
DEGREE_CUTOFF = 384
SOFTENING_EPS = 0.25
SPECTRAL_WEIGHT = 0.1

MEMBERS = 16
BANDS = 8
GROUPS = MEMBERS * BANDS
ORDERS = DEGREE_CUTOFF // GROUPS
BAND_ROWS = PARALLEL_LINES // BANDS
LON_BLOCK = AZIMUTH_STEPS // MEMBERS
ROW_GROUPS = 15
GROUP_ROWS = 6
LANES = 128
LON_CHUNKS = 12
LON_PADDED = LON_CHUNKS * LANES
SPECTRAL_ROWS = GROUPS * 8
BLOCK = 16

VMEM = pltpu.VMEM
F32 = jnp.float32
BF16 = jnp.bfloat16


def params(**kw):
    return pltpu.CompilerParams(vmem_limit_bytes=48 << 20, **kw)


def iota(shape, dim):
    return lax.broadcasted_iota(jnp.int32, shape, dim)


def cos_sin(steps):
    quarter = jnp.floor(steps * (1.0 / 360.0) + 0.5)
    rest = (steps - 360.0 * quarter) * (2.0 * math.pi / AZIMUTH_STEPS)
    quadrant = quarter - 4.0 * jnp.floor(quarter * 0.25)
    square = rest * rest
    sine = rest * (
        1.0
        + square
        * (-1.0 / 6.0 + square * (1.0 / 120.0 + square * (-1.0 / 5040.0 + square * (1.0 / 362880.0))))
    )
    cosine = 1.0 + square * (
        -0.5
        + square
        * (1.0 / 24.0 + square * (-1.0 / 720.0 + square * (1.0 / 40320.0 - square * (1.0 / 3628800.0))))
    )
    odd = (quadrant == 1.0) | (quadrant == 3.0)
    cos_part = jnp.where(odd, sine, cosine)
    sin_part = jnp.where(odd, cosine, sine)
    cos_part = jnp.where((quadrant == 1.0) | (quadrant == 2.0), -cos_part, cos_part)
    sin_part = jnp.where(quadrant >= 2.0, -sin_part, sin_part)
    return cos_part, sin_part


def dft_kernel(out_ref):
    def body(block, carry):
        row = block * BLOCK + iota((BLOCK, LANES), 0)
        lane = iota((BLOCK, LANES), 1)
        part = row & 7
        order = (ORDERS * (row >> 3) + (part >> 1)).astype(F32)
        turn = (360 * (part & 1)).astype(F32)
        cosine, sine = cos_sin(order * lane.astype(F32) + turn)
        cosine = jnp.where(part < 2 * ORDERS, cosine, 0.0)
        sine = jnp.where(part < 2 * ORDERS, sine, 0.0)
        cos_step, sin_step = cos_sin(order * float(LANES))
        rows = pl.ds(pl.multiple_of(block * BLOCK, BLOCK), BLOCK)
        for chunk in range(LON_CHUNKS):
            value = cosine
            if chunk == LON_CHUNKS - 1:
                value = jnp.where(lane < AZIMUTH_STEPS - LANES * chunk, value, 0.0)
            out_ref[rows, LANES * chunk : LANES * (chunk + 1)] = value.astype(BF16)
            cosine, sine = (
                cosine * cos_step - sine * sin_step,
                sine * cos_step + cosine * sin_step,
            )
        return carry

    lax.fori_loop(0, SPECTRAL_ROWS // BLOCK, body, 0)


def dft_table():
    return pl.pallas_call(
        dft_kernel,
        out_shape=jax.ShapeDtypeStruct((SPECTRAL_ROWS, LON_PADDED), BF16),
        out_specs=pl.BlockSpec(memory_space=VMEM),
        compiler_params=params(),
        cost_estimate=pl.CostEstimate(flops=20_000_000, bytes_accessed=3 << 20, transcendentals=0),
    )()


def lat_rows(rows_index):
    colatitude = math.pi * (rows_index.astype(F32) + 0.5) / PARALLEL_LINES
    return (jnp.cos(colatitude), jnp.sin(colatitude))


def seed_log(order_values):
    factors = jnp.arange(1, DEGREE_CUTOFF + 1, dtype=jnp.int32).astype(F32)[None, :]
    summands = jnp.where(factors <= order_values[:, None], jnp.log1p(-0.5 / factors), 0.0)
    return 0.5 * jnp.log(order_values + 0.5) + 0.5 * jnp.sum(summands, axis=1)


def recurrence(order_values):
    degree = jnp.arange(DEGREE_CUTOFF, dtype=jnp.int32).astype(F32)[None, :]
    order = order_values[:, None]
    growing = degree > order
    denominator = jnp.where(growing, degree * degree - order * order, 1.0)
    leading = jnp.sqrt(jnp.maximum(4.0 * degree * degree - 1.0, 0.0) / denominator)
    trailing = jnp.sqrt(
        jnp.maximum(
            ((degree - 1.0) ** 2 - order * order)
            * (2.0 * degree + 1.0)
            / ((2.0 * degree - 3.0) * denominator),
            0.0,
        )
    )
    zero = jnp.zeros_like(leading)
    return jnp.concatenate(
        [
            jnp.where(growing, leading, zero),
            jnp.where(growing, trailing, zero),
            (degree == order).astype(F32),
        ],
        axis=0,
    )


def legendre_kernel(coef_ref, cos_ref, weight_ref, start_ref, out_ref, table_ref):
    cos_lat = cos_ref[...]
    weight = weight_ref[...]

    def body(block, carry):
        state = list(carry)
        for step in range(BLOCK):
            degree = block * BLOCK + step
            for index in range(ORDERS):
                latest, before, log_scale, factor = state[4 * index : 4 * index + 4]
                leading = coef_ref[index, degree]
                trailing = coef_ref[ORDERS + index, degree]
                begin = coef_ref[2 * ORDERS + index, degree]
                advanced = (leading * cos_lat) * latest + (begin - trailing * before)
                row = (index * DEGREE_CUTOFF + degree) * 8
                table_ref[pl.ds(pl.multiple_of(row, 8), 8), :] = advanced * factor
                state[4 * index : 4 * index + 4] = [advanced, latest, log_scale, factor]
        for index in range(ORDERS):
            latest, before, log_scale, factor = state[4 * index : 4 * index + 4]
            largest = jnp.maximum(jnp.abs(latest), jnp.abs(before))
            largest = jnp.where(largest > 0.0, largest, 1.0)
            shrink = 1.0 / largest
            log_scale = log_scale + jnp.log(largest)
            state[4 * index : 4 * index + 4] = [
                latest * shrink,
                before * shrink,
                log_scale,
                jnp.exp(log_scale) * weight,
            ]
        return tuple(state)

    state = []
    for index in range(ORDERS):
        start = start_ref[8 * index : 8 * index + 8, :]
        state += [jnp.zeros((8, LANES), F32), jnp.zeros((8, LANES), F32), start, jnp.exp(start) * weight]
    lax.fori_loop(0, DEGREE_CUTOFF // BLOCK, body, tuple(state))
    for index in range(ORDERS):
        for band in range(BANDS):
            rows = table_ref[pl.ds(index * DEGREE_CUTOFF * 8 + band, DEGREE_CUTOFF, stride=8), :]
            out_ref[index, :, LANES * band : LANES * (band + 1)] = rows.astype(BF16)


def legendre_table(order_values):
    lane = jnp.arange(LANES, dtype=jnp.int32)[None, :]
    band = jnp.arange(BANDS, dtype=jnp.int32)[:, None]
    valid = ((lane >> 3) < ROW_GROUPS) & ((lane & 7) < GROUP_ROWS)
    row = jnp.where(valid, BAND_ROWS * band + GROUP_ROWS * (lane >> 3) + (lane & 7), 0)
    cos_lat, sin_lat = lat_rows(row)
    weight = jnp.where(valid, math.pi / PARALLEL_LINES * sin_lat, 0.0)
    start = seed_log(order_values)[:, None, None] + order_values[:, None, None] * jnp.log(sin_lat)[None]
    return pl.pallas_call(
        legendre_kernel,
        out_shape=jax.ShapeDtypeStruct((ORDERS, DEGREE_CUTOFF, BANDS * LANES), BF16),
        in_specs=[pl.BlockSpec(memory_space=pltpu.SMEM)] + [pl.BlockSpec(memory_space=VMEM)] * 3,
        out_specs=pl.BlockSpec(memory_space=VMEM),
        scratch_shapes=[VMEM((ORDERS * DEGREE_CUTOFF * 8, LANES), F32)],
        compiler_params=params(),
        cost_estimate=pl.CostEstimate(flops=20_000_000, bytes_accessed=3 << 20, transcendentals=0),
    )(recurrence(order_values), cos_lat, weight, start.reshape(8 * ORDERS, LANES))


def truth_rows(message_ref):
    lane = iota((8, LANES), 1)
    base = AZIMUTH_STEPS - (LON_CHUNKS - 1) * LANES
    chunks = [jnp.zeros((8, LANES), F32) for _ in range(LON_CHUNKS)]
    for pair in range(MEMBERS // 2):
        both = message_ref[16 * pair : 16 * pair + 16, LON_PADDED - LANES :].astype(F32)
        for half in range(2):
            first = LON_BLOCK * (2 * pair + half)
            value = both[8 * half : 8 * half + 8]
            shift = (first - base) % LANES
            if shift:
                value = pltpu.roll(value, shift, 1)
            for chunk in range(first // LANES, (first + LON_BLOCK - 1) // LANES + 1):
                place = lane + chunk * LANES
                inside = (place >= first) & (place < first + LON_BLOCK)
                chunks[chunk] = jnp.where(inside, value, chunks[chunk])
    return chunks


def fourier_kernel(table_ref, own_ref, message_ref, out_ref, field_ref):
    field_ref[0:112, :] = own_ref[0:112, :]
    truth = truth_rows(message_ref)
    for chunk in range(LON_CHUNKS):
        lanes = slice(LANES * chunk, LANES * (chunk + 1))
        last = own_ref[112:128, lanes].astype(F32)[0:8]
        field_ref[112:128, lanes] = jnp.concatenate([last, truth[chunk]], axis=0).astype(BF16)
    for block in range(4):
        rows = slice(256 * block, 256 * (block + 1))
        out_ref[rows, :] = lax.dot_general(
            table_ref[rows, :],
            field_ref[...],
            (((1,), (1,)), ((), ())),
            preferred_element_type=F32,
        ).astype(BF16)


def fourier(table, own, message):
    return pl.pallas_call(
        fourier_kernel,
        out_shape=jax.ShapeDtypeStruct((SPECTRAL_ROWS, LANES), BF16),
        in_specs=[pl.BlockSpec(memory_space=VMEM)] * 3,
        out_specs=pl.BlockSpec(memory_space=VMEM),
        scratch_shapes=[VMEM((LANES, LON_PADDED), BF16)],
        compiler_params=params(),
        cost_estimate=pl.CostEstimate(flops=400_000_000, bytes_accessed=4 << 20, transcendentals=0),
    )(table, own, message)


def grid_kernel(message_ref, weight_ref, out_ref, loss_ref, truth_ref):
    for chunk, value in enumerate(truth_rows(message_ref)):
        truth_ref[:, LANES * chunk : LANES * (chunk + 1)] = value
    weight = weight_ref[...]
    lane = iota((8, LANES), 1)

    def body(chunk, total):
        lanes = pl.ds(pl.multiple_of(chunk * LANES, LANES), LANES)
        draws = []
        for pair in range(MEMBERS // 2):
            both = message_ref[16 * pair : 16 * pair + 16, lanes].astype(F32)
            draws += [both[0:8], both[8:16]]
        target = truth_ref[:, lanes]
        counts = [None] * MEMBERS
        for i in range(MEMBERS):
            for k in range(i + 1, MEMBERS):
                above = jnp.where(draws[i] > draws[k], 1.0, 0.0)
                turn = jnp.where(draws[i] < draws[k], -1.0, above)
                counts[i] = turn if counts[i] is None else counts[i] + turn
                counts[k] = -turn if counts[k] is None else counts[k] - turn
        spread = jnp.zeros((8, LANES), F32)
        pulls = []
        for i in range(MEMBERS):
            gap = draws[i] - target
            above = jnp.where(draws[i] > target, float(MEMBERS - 1), 0.0)
            side = jnp.where(draws[i] < target, -float(MEMBERS - 1), above)
            pulls.append(side - counts[i])
            spread = spread + (jnp.abs(gap) - (draws[i] * counts[i]) * (1.0 / (MEMBERS - 1)))
        for pair in range(MEMBERS // 2):
            both = jnp.concatenate([pulls[2 * pair], pulls[2 * pair + 1]], axis=0)
            out_ref[16 * pair : 16 * pair + 16, lanes] = both.astype(BF16)
        return total + jnp.where(lane + chunk * LANES < AZIMUTH_STEPS, spread, 0.0)

    total = lax.fori_loop(0, LON_CHUNKS, body, jnp.zeros((8, LANES), F32))
    loss_ref[...] = total * weight


def grid_counts(message, weight):
    return pl.pallas_call(
        grid_kernel,
        out_shape=(
            jax.ShapeDtypeStruct((LANES, LON_PADDED), BF16),
            jax.ShapeDtypeStruct((8, LANES), F32),
        ),
        in_specs=[pl.BlockSpec(memory_space=VMEM)] * 2,
        out_specs=(pl.BlockSpec(memory_space=VMEM), pl.BlockSpec(memory_space=VMEM)),
        scratch_shapes=[VMEM((8, LON_PADDED), F32)],
        compiler_params=params(),
        cost_estimate=pl.CostEstimate(flops=40_000_000, bytes_accessed=1 << 20, transcendentals=0),
    )(message, weight)


def spectral_kernel(first_ref, modes_ref, table_ref, grid_ref, out_ref, wide_ref, lhs_ref):
    draws = MEMBERS
    scale = SPECTRAL_WEIGHT * PARALLEL_LINES * AZIMUTH_STEPS / (DEGREE_CUTOFF * (DEGREE_CUTOFF + 1) / 2)
    lane = iota((64, LANES), 1)
    target = jnp.zeros((64, LANES), F32)
    for member in range(draws):
        value = modes_ref[64 * member : 64 * member + 64, :].astype(F32)
        wide_ref[64 * member : 64 * member + 64, :] = value
        if member < ROW_GROUPS:
            moved = pltpu.roll(value, (8 * member + 8) % LANES, 1)
            target = jnp.where((lane >> 3) == member, moved, target)
    loss = jnp.zeros((1, DEGREE_CUTOFF), F32)
    degree = iota((1, DEGREE_CUTOFF), 1)
    pad = jnp.zeros((14, LANES), F32)
    grads = []
    for index in range(ORDERS):
        for band in range(BANDS):
            lanes = slice(LANES * band, LANES * (band + 1))
            parts = [
                wide_ref[pl.ds(8 * band + 2 * index + r, draws, stride=64), :] for r in range(2)
            ]
            aims = [target[8 * band + 2 * index + r : 8 * band + 2 * index + r + 1, :] for r in range(2)]
            lhs_ref[index, :, lanes] = jnp.concatenate(parts + aims + [pad], axis=0).astype(BF16)
        terms = lax.dot_general(
            lhs_ref[index],
            table_ref[index],
            (((1,), (1,)), ((), ())),
            preferred_element_type=F32,
        )
        real, imag = terms[0:draws], terms[draws : 2 * draws]
        real_aim, imag_aim = terms[2 * draws : 2 * draws + 1], terms[2 * draws + 1 : 2 * draws + 2]
        gap_real, gap_imag = real - real_aim, imag - imag_aim
        square = gap_real * gap_real + gap_imag * gap_imag + SOFTENING_EPS**2
        inverse = lax.rsqrt(square)
        near = square * inverse
        step_real, step_imag = gap_real * inverse, gap_imag * inverse
        pair = jnp.zeros_like(real)
        pull_real, pull_imag = jnp.zeros_like(real), jnp.zeros_like(real)
        for other in range(draws):
            gap_real, gap_imag = real - real[other : other + 1], imag - imag[other : other + 1]
            square = gap_real * gap_real + gap_imag * gap_imag + SOFTENING_EPS**2
            inverse = lax.rsqrt(square)
            pair = pair + square * inverse
            pull_real = pull_real + gap_real * inverse
            pull_imag = pull_imag + gap_imag * inverse
        kept = degree >= first_ref[0] + index
        score = jnp.sum(near, axis=0, keepdims=True) - (
            jnp.sum(pair, axis=0, keepdims=True) - draws * SOFTENING_EPS
        ) / (2.0 * (draws - 1))
        loss = loss + jnp.where(kept, score, 0.0)
        down = jnp.concatenate(
            [step_real - pull_real / (draws - 1), step_imag - pull_imag / (draws - 1)], axis=0
        )
        grad = jnp.where(kept, scale * down, 0.0).astype(BF16)
        back = jnp.dot(grad, table_ref[index], preferred_element_type=F32)
        for band in range(BANDS):
            for r in range(2):
                wide_ref[pl.ds(8 * band + 2 * index + r, draws, stride=64), :] = back[
                    draws * r : draws * (r + 1), LANES * band : LANES * (band + 1)
                ]
    local = jnp.sum(jnp.sum(grid_ref[...], axis=0, keepdims=True), axis=1, keepdims=True) / (
        PARALLEL_LINES * AZIMUTH_STEPS
    ) + SPECTRAL_WEIGHT / (DEGREE_CUTOFF * (DEGREE_CUTOFF + 1) / 2) * jnp.sum(loss, axis=1, keepdims=True)
    high = local.astype(BF16).astype(F32)
    middle = (local - high).astype(BF16).astype(F32)
    low = local - high - middle
    row = iota((BLOCK, LANES), 0) & 7
    column = iota((BLOCK, LANES), 1)
    spare = jnp.where(column == LANES - 8, high, jnp.where(column == LANES - 7, middle, low))
    carries = (row == 0) & (column >= LANES - 8) & (column < LANES - 5)
    for block in range(SPECTRAL_ROWS // BLOCK):
        value = wide_ref[BLOCK * block : BLOCK * (block + 1), :]
        value = jnp.where(row < 2 * ORDERS, value, 0.0)
        out_ref[BLOCK * block : BLOCK * (block + 1), :] = jnp.where(carries, spare, value).astype(BF16)


def spectral(first, modes, table, grid_loss):
    return pl.pallas_call(
        spectral_kernel,
        out_shape=jax.ShapeDtypeStruct((SPECTRAL_ROWS, LANES), BF16),
        in_specs=[pl.BlockSpec(memory_space=pltpu.SMEM)] + [pl.BlockSpec(memory_space=VMEM)] * 3,
        out_specs=pl.BlockSpec(memory_space=VMEM),
        scratch_shapes=[
            VMEM((SPECTRAL_ROWS, LANES), F32),
            VMEM((ORDERS, 48, BANDS * LANES), BF16),
        ],
        compiler_params=params(),
        cost_estimate=pl.CostEstimate(flops=200_000_000, bytes_accessed=3 << 20, transcendentals=0),
    )(first, modes, table, grid_loss)


def final_kernel(table_ref, modes_ref, counts_ref, weight_ref, out_ref):
    for chunk in range(LON_CHUNKS):
        lanes = slice(LANES * chunk, LANES * (chunk + 1))
        width = min(LANES, AZIMUTH_STEPS - LANES * chunk)
        wave = lax.dot_general(
            modes_ref[...],
            table_ref[:, lanes],
            (((0,), (0,)), ((), ())),
            preferred_element_type=F32,
        )
        total = weight_ref[...] * counts_ref[:, lanes].astype(F32) + wave
        for group in range(ROW_GROUPS):
            out_ref[GROUP_ROWS * group : GROUP_ROWS * (group + 1), LANES * chunk : LANES * chunk + width] = total[
                8 * group : 8 * group + GROUP_ROWS, 0:width
            ]


def final(table, modes, counts, weight):
    return pl.pallas_call(
        final_kernel,
        out_shape=jax.ShapeDtypeStruct((BAND_ROWS, AZIMUTH_STEPS), F32),
        in_specs=[pl.BlockSpec(memory_space=VMEM)] * 4,
        out_specs=pl.BlockSpec(memory_space=VMEM),
        compiler_params=params(),
        cost_estimate=pl.CostEstimate(flops=400_000_000, bytes_accessed=4 << 20, transcendentals=0),
    )(table, modes, counts, weight)


def local(model_outputs, verifying_truth):
    ens_index = lax.axis_index("ens")
    lat_index = lax.axis_index("lat")
    own = model_outputs.reshape(ROW_GROUPS, GROUP_ROWS, AZIMUTH_STEPS)
    target = verifying_truth.reshape(ROW_GROUPS, GROUP_ROWS, LON_BLOCK)
    outgoing = jnp.concatenate([own, target], axis=2)
    outgoing = jnp.pad(
        outgoing,
        ((0, 1), (0, 8 - GROUP_ROWS), (0, LON_PADDED - AZIMUTH_STEPS - LON_BLOCK)),
    )
    message = lax.all_to_all(outgoing, "ens", split_axis=0, concat_axis=0, tiled=True)
    message = message.reshape(LANES, LON_PADDED)

    table = dft_table()
    first = ORDERS * (ens_index * BANDS + lat_index)
    orders = (first + jnp.arange(ORDERS, dtype=jnp.int32)).astype(F32)
    legendre = legendre_table(orders)

    modes = fourier(table, outgoing.reshape(LANES, LON_PADDED), message)
    modes = lax.all_to_all(
        modes.reshape(GROUPS, 8, LANES), ("ens", "lat"), split_axis=0, concat_axis=0, tiled=True
    ).reshape(SPECTRAL_ROWS, LANES)

    part = jnp.arange(8, dtype=jnp.int32)
    grid_row = BAND_ROWS * lat_index + GROUP_ROWS * ens_index + part
    grid_valid = (part < GROUP_ROWS) & (ens_index < ROW_GROUPS)
    grid_weight = jnp.where(grid_valid, lat_rows(grid_row)[1], 0.0)
    counts, grid_loss = grid_counts(message, jnp.broadcast_to(grid_weight[:, None], (8, LANES)))
    counts = lax.all_to_all(
        counts.reshape(MEMBERS, 8, LON_PADDED), "ens", split_axis=0, concat_axis=0, tiled=True
    ).reshape(LANES, LON_PADDED)

    back = spectral(first.reshape(1).astype(jnp.int32), modes, legendre, grid_loss)
    back = lax.all_to_all(
        back.reshape(GROUPS, 8, LANES), ("ens", "lat"), split_axis=0, concat_axis=0, tiled=True
    )
    shared = jnp.sum(back[:, 0, LANES - 8 : LANES - 5].astype(F32))
    other = lax.ppermute(shared, "chan", [(0, 1), (1, 0)])

    row = jnp.arange(LANES, dtype=jnp.int32)
    band_row = BAND_ROWS * lat_index + GROUP_ROWS * (row >> 3) + (row & 7)
    weight = lat_rows(band_row)[1] / (MEMBERS - 1)
    weight = jnp.broadcast_to(weight[:, None], (LANES, LANES))
    slope = final(table, back.reshape(SPECTRAL_ROWS, LANES), counts, weight)
    return (slope[None, None], shared + other)


def solution(mesh):
    return jax.shard_map(
        local,
        mesh=mesh,
        in_specs=(P("ens", "chan", "lat", None), P("chan", "lat", "ens")),
        out_specs=(P("ens", "chan", "lat", None), P()),
        check_vma=False,
    )
```

```python
import functools
import math

import jax
import jax.numpy as jnp
from jax import lax
from jax.experimental import pallas as pl
from jax.experimental.pallas import tpu as pltpu
from jax.sharding import PartitionSpec as P

PARALLEL_LINES = 720
AZIMUTH_STEPS = 1440
DEGREE_CUTOFF = 384
SOFTENING_EPS = 0.25
SPECTRAL_WEIGHT = 0.1

MEMBERS = 16
BANDS = 8
GROUPS = MEMBERS * BANDS
ORDERS = DEGREE_CUTOFF // GROUPS
BAND_ROWS = PARALLEL_LINES // BANDS
LON_BLOCK = AZIMUTH_STEPS // MEMBERS
ROW_GROUPS = 15
GROUP_ROWS = 6
LANES = 128
LON_CHUNKS = 12
LON_PADDED = LON_CHUNKS * LANES
SPECTRAL_ROWS = GROUPS * 8
BLOCK = 16

VMEM = pltpu.VMEM
MESH = pl.DeviceIdType.MESH
F32 = jnp.float32
BF16 = jnp.bfloat16


def params(**kw):
    return pltpu.CompilerParams(vmem_limit_bytes=48 << 20, **kw)


def iota(shape, dim):
    return lax.broadcasted_iota(jnp.int32, shape, dim)


def cos_sin(steps):
    quarter = jnp.floor(steps * (1.0 / 360.0) + 0.5)
    rest = (steps - 360.0 * quarter) * (2.0 * math.pi / AZIMUTH_STEPS)
    quadrant = quarter - 4.0 * jnp.floor(quarter * 0.25)
    square = rest * rest
    sine = rest * (
        1.0
        + square
        * (-1.0 / 6.0 + square * (1.0 / 120.0 + square * (-1.0 / 5040.0 + square * (1.0 / 362880.0))))
    )
    cosine = 1.0 + square * (
        -0.5
        + square
        * (1.0 / 24.0 + square * (-1.0 / 720.0 + square * (1.0 / 40320.0 - square * (1.0 / 3628800.0))))
    )
    odd = (quadrant == 1.0) | (quadrant == 3.0)
    cos_part = jnp.where(odd, sine, cosine)
    sin_part = jnp.where(odd, cosine, sine)
    cos_part = jnp.where((quadrant == 1.0) | (quadrant == 2.0), -cos_part, cos_part)
    sin_part = jnp.where(quadrant >= 2.0, -sin_part, sin_part)
    return cos_part, sin_part


def fill_dft(out_ref):
    def body(block, carry):
        row = block * BLOCK + iota((BLOCK, LANES), 0)
        lane = iota((BLOCK, LANES), 1)
        part = row & 7
        order = (ORDERS * (row >> 3) + (part >> 1)).astype(F32)
        turn = (360 * (part & 1)).astype(F32)
        cosine, sine = cos_sin(order * lane.astype(F32) + turn)
        cosine = jnp.where(part < 2 * ORDERS, cosine, 0.0)
        sine = jnp.where(part < 2 * ORDERS, sine, 0.0)
        cos_step, sin_step = cos_sin(order * float(LANES))
        rows = pl.ds(pl.multiple_of(block * BLOCK, BLOCK), BLOCK)
        for chunk in range(LON_CHUNKS):
            value = cosine
            if chunk == LON_CHUNKS - 1:
                value = jnp.where(lane < AZIMUTH_STEPS - LANES * chunk, value, 0.0)
            out_ref[rows, LANES * chunk : LANES * (chunk + 1)] = value.astype(BF16)
            cosine, sine = (
                cosine * cos_step - sine * sin_step,
                sine * cos_step + cosine * sin_step,
            )
        return carry

    lax.fori_loop(0, SPECTRAL_ROWS // BLOCK, body, 0)


def fill_recurrence(first, out_ref):
    order = (first + iota((8, DEGREE_CUTOFF), 0)).astype(F32)
    degree = iota((8, DEGREE_CUTOFF), 1).astype(F32)
    growing = degree > order
    denominator = jnp.where(growing, degree * degree - order * order, 1.0)
    leading = jnp.sqrt(jnp.maximum(4.0 * degree * degree - 1.0, 0.0) / denominator)
    trailing = jnp.sqrt(
        jnp.maximum(
            ((degree - 1.0) * (degree - 1.0) - order * order)
            * (2.0 * degree + 1.0)
            / ((2.0 * degree - 3.0) * denominator),
            0.0,
        )
    )
    out_ref[0:8, :] = jnp.where(growing, leading, 0.0)
    out_ref[8:16, :] = jnp.where(growing, trailing, 0.0)


def seed_logs(first):
    order = (first + iota((8, DEGREE_CUTOFF), 0)).astype(F32)
    factor = (1 + iota((8, DEGREE_CUTOFF), 1)).astype(F32)
    summands = jnp.where(factor <= order, jnp.log(1.0 - 0.5 / factor), 0.0)
    return 0.5 * jnp.log(order[:, 0:1] + 0.5) + 0.5 * jnp.sum(summands, axis=1, keepdims=True)


def fill_legendre(first, coef_ref, table_ref, out_ref):
    band, lane = iota((8, LANES), 0), iota((8, LANES), 1)
    group, part = lane >> 3, lane & 7
    valid = (group < ROW_GROUPS) & (part < GROUP_ROWS)
    row = jnp.where(valid, BAND_ROWS * band + GROUP_ROWS * group + part, 0)
    cos_lat, sin_lat = cos_sin(row.astype(F32) + 0.5)
    weight = jnp.where(valid, math.pi / PARALLEL_LINES * sin_lat, 0.0)
    log_sin = jnp.log(sin_lat)
    seeds = seed_logs(first)

    def body(block, carry):
        state = list(carry)
        for step in range(BLOCK):
            degree = block * BLOCK + step
            for index in range(ORDERS):
                latest, before, log_scale, factor = state[4 * index : 4 * index + 4]
                leading = coef_ref[index, degree]
                trailing = coef_ref[8 + index, degree]
                begin = jnp.where(degree == first + index, 1.0, 0.0)
                advanced = (leading * cos_lat) * latest + (begin - trailing * before)
                row = (index * DEGREE_CUTOFF + degree) * 8
                table_ref[pl.ds(pl.multiple_of(row, 8), 8), :] = advanced * factor
                state[4 * index : 4 * index + 4] = [advanced, latest, log_scale, factor]
        for index in range(ORDERS):
            latest, before, log_scale, factor = state[4 * index : 4 * index + 4]
            largest = jnp.maximum(jnp.abs(latest), jnp.abs(before))
            largest = jnp.where(largest > 0.0, largest, 1.0)
            shrink = 1.0 / largest
            log_scale = log_scale + jnp.log(largest)
            state[4 * index : 4 * index + 4] = [
                latest * shrink,
                before * shrink,
                log_scale,
                jnp.exp(log_scale) * weight,
            ]
        return tuple(state)

    state = []
    for index in range(ORDERS):
        order = jnp.broadcast_to((first + index).astype(F32), (8, LANES))
        start = jnp.broadcast_to(seeds[index : index + 1, :], (8, LANES)) + order * log_sin
        state += [jnp.zeros((8, LANES), F32), jnp.zeros((8, LANES), F32), start, jnp.exp(start) * weight]
    lax.fori_loop(0, DEGREE_CUTOFF // BLOCK, body, tuple(state))
    for index in range(ORDERS):
        for band in range(BANDS):
            rows = table_ref[pl.ds(index * DEGREE_CUTOFF * 8 + band, DEGREE_CUTOFF, stride=8), :]
            out_ref[index, :, LANES * band : LANES * (band + 1)] = rows.astype(BF16)


def fill_truth(blocks_ref, out_ref):
    lane = iota((8, LANES), 1)
    chunks = [jnp.zeros((8, LANES), F32) for _ in range(LON_CHUNKS)]
    for block in range(MEMBERS):
        first = LON_BLOCK * block
        value = blocks_ref[block].astype(F32)
        shift = first % LANES
        if shift:
            value = pltpu.roll(value, shift, 1)
        for chunk in range(first // LANES, (first + LON_BLOCK - 1) // LANES + 1):
            place = lane + chunk * LANES
            inside = (place >= first) & (place < first + LON_BLOCK)
            chunks[chunk] = jnp.where(inside, value, chunks[chunk])
    for chunk in range(LON_CHUNKS):
        out_ref[:, LANES * chunk : LANES * (chunk + 1)] = chunks[chunk]


def grid_stage(ens, lat, draws_ref, truth_ref, counts_ref):
    row, lane = iota((8, LANES), 0), iota((8, LANES), 1)
    line = (BAND_ROWS * lat + GROUP_ROWS * ens + row).astype(F32)
    weight = jnp.where((row < GROUP_ROWS) & (ens < ROW_GROUPS), cos_sin(line + 0.5)[1], 0.0)

    def body(chunk, total):
        lanes = pl.ds(pl.multiple_of(chunk * LANES, LANES), LANES)
        draws = [draws_ref[i, :, lanes].astype(F32) for i in range(MEMBERS)]
        target = truth_ref[:, lanes]
        counts = [None] * MEMBERS
        for i in range(MEMBERS):
            for k in range(i + 1, MEMBERS):
                above = jnp.where(draws[i] > draws[k], 1.0, 0.0)
                turn = jnp.where(draws[i] < draws[k], -1.0, above)
                counts[i] = turn if counts[i] is None else counts[i] + turn
                counts[k] = -turn if counts[k] is None else counts[k] - turn
        spread = jnp.zeros((8, LANES), F32)
        for i in range(MEMBERS):
            gap = draws[i] - target
            above = jnp.where(draws[i] > target, float(MEMBERS - 1), 0.0)
            side = jnp.where(draws[i] < target, -float(MEMBERS - 1), above)
            counts_ref[i, :, lanes] = (side - counts[i]).astype(BF16)
            spread = spread + (jnp.abs(gap) - (draws[i] * counts[i]) * (1.0 / (MEMBERS - 1)))
        return total + jnp.where(lane + chunk * LANES < AZIMUTH_STEPS, spread, 0.0)

    return weight * lax.fori_loop(0, LON_CHUNKS, body, jnp.zeros((8, LANES), F32))


def spectral_stage(first, grid_loss, modes_ref, table_ref, out_ref, wide_ref, lhs_ref):
    draws = MEMBERS
    scale = SPECTRAL_WEIGHT * PARALLEL_LINES * AZIMUTH_STEPS / (DEGREE_CUTOFF * (DEGREE_CUTOFF + 1) / 2)
    lane = iota((64, LANES), 1)
    target = jnp.zeros((64, LANES), F32)
    for member in range(draws):
        value = modes_ref[8 * member : 8 * member + 8].astype(F32).reshape(64, LANES)
        wide_ref[64 * member : 64 * member + 64, :] = value
        if member < ROW_GROUPS:
            moved = pltpu.roll(value, (8 * member + 8) % LANES, 1)
            target = jnp.where((lane >> 3) == member, moved, target)
    loss = jnp.zeros((1, DEGREE_CUTOFF), F32)
    degree = iota((1, DEGREE_CUTOFF), 1)
    pad = jnp.zeros((14, LANES), F32)
    for index in range(ORDERS):
        for band in range(BANDS):
            lanes = slice(LANES * band, LANES * (band + 1))
            parts = [
                wide_ref[pl.ds(8 * band + 2 * index + r, draws, stride=64), :] for r in range(2)
            ]
            aims = [target[8 * band + 2 * index + r : 8 * band + 2 * index + r + 1, :] for r in range(2)]
            lhs_ref[index, :, lanes] = jnp.concatenate(parts + aims + [pad], axis=0).astype(BF16)
        terms = lax.dot_general(
            lhs_ref[index],
            table_ref[index],
            (((1,), (1,)), ((), ())),
            preferred_element_type=F32,
        )
        real, imag = terms[0:draws], terms[draws : 2 * draws]
        real_aim, imag_aim = terms[2 * draws : 2 * draws + 1], terms[2 * draws + 1 : 2 * draws + 2]
        gap_real, gap_imag = real - real_aim, imag - imag_aim
        square = gap_real * gap_real + gap_imag * gap_imag + SOFTENING_EPS**2
        inverse = lax.rsqrt(square)
        near = square * inverse
        step_real, step_imag = gap_real * inverse, gap_imag * inverse
        pair = jnp.zeros_like(real)
        pull_real, pull_imag = jnp.zeros_like(real), jnp.zeros_like(real)
        for other in range(draws):
            gap_real, gap_imag = real - real[other : other + 1], imag - imag[other : other + 1]
            square = gap_real * gap_real + gap_imag * gap_imag + SOFTENING_EPS**2
            inverse = lax.rsqrt(square)
            pair = pair + square * inverse
            pull_real = pull_real + gap_real * inverse
            pull_imag = pull_imag + gap_imag * inverse
        kept = degree >= first + index
        score = jnp.sum(near, axis=0, keepdims=True) - (
            jnp.sum(pair, axis=0, keepdims=True) - draws * SOFTENING_EPS
        ) / (2.0 * (draws - 1))
        loss = loss + jnp.where(kept, score, 0.0)
        down = jnp.concatenate(
            [step_real - pull_real / (draws - 1), step_imag - pull_imag / (draws - 1)], axis=0
        )
        grad = jnp.where(kept, scale * down, 0.0).astype(BF16)
        back = jnp.dot(grad, table_ref[index], preferred_element_type=F32)
        for band in range(BANDS):
            for r in range(2):
                wide_ref[pl.ds(8 * band + 2 * index + r, draws, stride=64), :] = back[
                    draws * r : draws * (r + 1), LANES * band : LANES * (band + 1)
                ]
    local = jnp.sum(jnp.sum(grid_loss, axis=0, keepdims=True), axis=1, keepdims=True) / (
        PARALLEL_LINES * AZIMUTH_STEPS
    ) + SPECTRAL_WEIGHT / (DEGREE_CUTOFF * (DEGREE_CUTOFF + 1) / 2) * jnp.sum(loss, axis=1, keepdims=True)
    high = local.astype(BF16).astype(F32)
    middle = (local - high).astype(BF16).astype(F32)
    low = local - high - middle
    row = iota((BLOCK, LANES), 0) & 7
    column = iota((BLOCK, LANES), 1)
    spare = jnp.where(column == LANES - 8, high, jnp.where(column == LANES - 7, middle, low))
    carries = (row == 0) & (column >= LANES - 8) & (column < LANES - 5)
    for block in range(SPECTRAL_ROWS // BLOCK):
        value = wide_ref[BLOCK * block : BLOCK * (block + 1), :]
        value = jnp.where(row < 2 * ORDERS, value, 0.0)
        value = jnp.where(carries, spare, value)
        out_ref[2 * block : 2 * block + 2] = value.reshape(2, 8, LANES).astype(BF16)


def exchange_kernel(
    own_ref,
    truth_in_ref,
    dft_ref,
    back_in_ref,
    counts_in_ref,
    loss_ref,
    wide_own_ref,
    rows_out_ref,
    rows_in_ref,
    blocks_out_ref,
    blocks_in_ref,
    truth_ref,
    field_ref,
    modes_out_ref,
    modes_in_ref,
    coef_vector_ref,
    coef_ref,
    table_ref,
    legendre_ref,
    counts_out_ref,
    back_out_ref,
    wide_ref,
    lhs_ref,
    send_sem,
    recv_sem,
    local_sem,
):
    chan, ens, lat = lax.axis_index("chan"), lax.axis_index("ens"), lax.axis_index("lat")
    mine = ens * BANDS + lat
    first = ORDERS * mine

    barrier = pltpu.get_barrier_semaphore()

    def greet(step, carry):
        peer = lax.rem(mine + step, GROUPS)
        pl.semaphore_signal(
            barrier,
            inc=1,
            device_id=(chan, lax.div(peer, BANDS), lax.rem(peer, BANDS)),
            device_id_type=MESH,
        )
        return carry

    lax.fori_loop(1, GROUPS, greet, 0)

    def copy(source, target, kind, peer_ens, peer_lat):
        return pltpu.make_async_remote_copy(
            src_ref=source,
            dst_ref=target,
            send_sem=send_sem.at[kind],
            recv_sem=recv_sem.at[kind],
            device_id=(chan, peer_ens, peer_lat),
            device_id_type=MESH,
        )

    def to_members(source, target, kind):
        def body(step, carry):
            peer = lax.rem(ens + step, MEMBERS)
            copy(source.at[peer], target.at[ens], kind, peer, lat).start()
            return carry

        lax.fori_loop(1, MEMBERS, body, 0)
        target[ens] = source[ens]

    def to_groups(source, target, kind, block):
        def body(step, carry):
            peer = block * 32 + lax.rem(mine + step, 32)

            @pl.when(peer != mine)
            def _():
                copy(source.at[peer], target.at[mine], kind, lax.div(peer, BANDS), lax.rem(peer, BANDS)).start()

            return carry

        lax.fori_loop(0, 32, body, 0)

    def all_of(source, target, kind, count):
        return copy(source.at[pl.ds(0, count)], target.at[pl.ds(0, count)], kind, ens, lat)

    wide_own_ref[88:96, :] = jnp.zeros((8, LON_PADDED), F32)
    wide_own_ref[:, LON_PADDED - LANES :] = jnp.zeros((96, LANES), F32)
    wide_own_ref[0:BAND_ROWS, 0:LON_BLOCK] = truth_in_ref[...].astype(F32)
    for group in range(ROW_GROUPS):
        blocks_out_ref[group] = wide_own_ref[GROUP_ROWS * group : GROUP_ROWS * group + 8, 0:LANES].astype(BF16)
    blocks_out_ref[ROW_GROUPS] = jnp.zeros((8, LANES), BF16)
    wide_own_ref[0:BAND_ROWS, 0:AZIMUTH_STEPS] = own_ref[...].astype(F32)
    for group in range(ROW_GROUPS):
        rows_out_ref[group] = wide_own_ref[GROUP_ROWS * group : GROUP_ROWS * group + 8, :].astype(BF16)
    rows_out_ref[ROW_GROUPS] = jnp.zeros((8, LON_PADDED), BF16)

    pl.semaphore_wait(barrier, GROUPS - 1)
    to_members(blocks_out_ref, blocks_in_ref, 0)
    to_members(rows_out_ref, rows_in_ref, 1)

    fill_recurrence(first, coef_vector_ref)
    coef_copy = pltpu.make_async_copy(coef_vector_ref, coef_ref, local_sem)
    coef_copy.start()
    for pair in range(7):
        both = [
            wide_own_ref[GROUP_ROWS * group : GROUP_ROWS * group + 8, :] for group in (2 * pair, 2 * pair + 1)
        ]
        field_ref[16 * pair : 16 * pair + 16, :] = jnp.concatenate(both, axis=0).astype(BF16)
    fill_dft(dft_ref)

    all_of(blocks_out_ref, blocks_in_ref, 0, MEMBERS - 1).wait_recv()
    fill_truth(blocks_in_ref, truth_ref)
    both = [wide_own_ref[84:92, :], truth_ref[...]]
    field_ref[112:128, :] = jnp.concatenate(both, axis=0).astype(BF16)

    def fourier(step, carry):
        block = lax.rem(lax.div(mine, 32) + step, 4)
        modes = lax.dot_general(
            dft_ref[pl.ds(pl.multiple_of(block * 256, 256), 256), :],
            field_ref[...],
            (((1,), (1,)), ((), ())),
            preferred_element_type=F32,
        )
        modes_out_ref[pl.ds(block * 32, 32)] = modes.reshape(32, 8, LANES).astype(BF16)
        to_groups(modes_out_ref, modes_in_ref, 2, block)
        return carry

    lax.fori_loop(0, 4, fourier, 0)
    modes_in_ref[mine] = modes_out_ref[mine]

    coef_copy.wait()
    fill_legendre(first, coef_ref, table_ref, legendre_ref)

    all_of(rows_out_ref, rows_in_ref, 1, MEMBERS - 1).wait_recv()
    grid_loss = grid_stage(ens, lat, rows_in_ref, truth_ref, counts_out_ref)
    to_members(counts_out_ref, counts_in_ref, 3)

    all_of(modes_out_ref, modes_in_ref, 2, GROUPS - 1).wait_recv()
    spectral_stage(first, grid_loss, modes_in_ref, legendre_ref, back_out_ref, wide_ref, lhs_ref)

    def give_back(step, carry):
        to_groups(back_out_ref, back_in_ref, 4, lax.rem(lax.div(mine, 32) + step, 4))
        return carry

    lax.fori_loop(0, 4, give_back, 0)
    back_in_ref[mine] = back_out_ref[mine]

    all_of(counts_out_ref, counts_in_ref, 3, MEMBERS - 1).wait_recv()
    all_of(back_out_ref, back_in_ref, 4, GROUPS - 1).wait_recv()
    total = jnp.zeros((8, LANES), F32)
    for block in range(16):
        total = total + jnp.sum(back_in_ref[8 * block : 8 * block + 8].astype(F32), axis=0)
    row, column = iota((8, LANES), 0), iota((8, LANES), 1)
    total = jnp.where((row == 0) & (column >= LANES - 8) & (column < LANES - 5), total, 0.0)
    loss_ref[...] = jnp.sum(jnp.sum(total, axis=0, keepdims=True), axis=1, keepdims=True)

    all_of(blocks_out_ref, blocks_in_ref, 0, MEMBERS - 1).wait_send()
    all_of(rows_out_ref, rows_in_ref, 1, MEMBERS - 1).wait_send()
    all_of(modes_out_ref, modes_in_ref, 2, GROUPS - 1).wait_send()
    all_of(counts_out_ref, counts_in_ref, 3, MEMBERS - 1).wait_send()
    all_of(back_out_ref, back_in_ref, 4, GROUPS - 1).wait_send()


def exchange(own, target):
    rows = (MEMBERS, 8, LON_PADDED)
    blocks = (MEMBERS, 8, LANES)
    modes = (GROUPS, 8, LANES)
    return pl.pallas_call(
        exchange_kernel,
        out_shape=(
            jax.ShapeDtypeStruct((SPECTRAL_ROWS, LON_PADDED), BF16),
            jax.ShapeDtypeStruct(modes, BF16),
            jax.ShapeDtypeStruct(rows, BF16),
            jax.ShapeDtypeStruct((1, 1), F32),
        ),
        in_specs=[pl.BlockSpec(memory_space=VMEM)] * 2,
        out_specs=tuple([pl.BlockSpec(memory_space=VMEM)] * 4),
        scratch_shapes=[
            VMEM((96, LON_PADDED), F32),
            VMEM(rows, BF16),
            VMEM(rows, BF16),
            VMEM(blocks, BF16),
            VMEM(blocks, BF16),
            VMEM((8, LON_PADDED), F32),
            VMEM((LANES, LON_PADDED), BF16),
            VMEM(modes, BF16),
            VMEM(modes, BF16),
            VMEM((16, DEGREE_CUTOFF), F32),
            pltpu.SMEM((16, DEGREE_CUTOFF), F32),
            VMEM((ORDERS * DEGREE_CUTOFF * 8, LANES), F32),
            VMEM((ORDERS, DEGREE_CUTOFF, BANDS * LANES), BF16),
            VMEM(rows, BF16),
            VMEM(modes, BF16),
            VMEM((SPECTRAL_ROWS, LANES), F32),
            VMEM((ORDERS, 48, BANDS * LANES), BF16),
            pltpu.SemaphoreType.DMA((5,)),
            pltpu.SemaphoreType.DMA((5,)),
            pltpu.SemaphoreType.DMA,
        ],
        compiler_params=params(collective_id=0, has_side_effects=True),
        cost_estimate=pl.CostEstimate(flops=800_000_000, bytes_accessed=8 << 20, transcendentals=0),
    )(own, target)


def final_kernel(table_ref, modes_ref, counts_ref, out_ref):
    row = iota((LANES, LANES), 0)
    line = BAND_ROWS * lax.axis_index("lat") + GROUP_ROWS * (row >> 3) + (row & 7)
    weight = cos_sin(line.astype(F32) + 0.5)[1] / (MEMBERS - 1)
    for chunk in range(LON_CHUNKS):
        lanes = slice(LANES * chunk, LANES * (chunk + 1))
        width = min(LANES, AZIMUTH_STEPS - LANES * chunk)
        wave = lax.dot_general(
            modes_ref[...],
            table_ref[:, lanes],
            (((0,), (0,)), ((), ())),
            preferred_element_type=F32,
        )
        total = weight * counts_ref[:, lanes].astype(F32) + wave
        for group in range(ROW_GROUPS):
            out_ref[
                GROUP_ROWS * group : GROUP_ROWS * (group + 1), 0, LANES * chunk : LANES * chunk + width
            ] = total[8 * group : 8 * group + GROUP_ROWS, 0:width]


def final(table, modes, counts):
    return pl.pallas_call(
        final_kernel,
        out_shape=jax.ShapeDtypeStruct((BAND_ROWS, 1, AZIMUTH_STEPS), F32),
        in_specs=[pl.BlockSpec(memory_space=VMEM)] * 3,
        out_specs=pl.BlockSpec(memory_space=VMEM),
        compiler_params=params(),
        cost_estimate=pl.CostEstimate(flops=400_000_000, bytes_accessed=4 << 20, transcendentals=0),
    )(table, modes, counts)


def local(model_outputs, verifying_truth):
    table, back, counts, shared = exchange(model_outputs[0, 0], verifying_truth[0])
    other = lax.ppermute(shared, "chan", [(0, 1), (1, 0)])
    slope = final(table, back.reshape(SPECTRAL_ROWS, LANES), counts.reshape(LANES, LON_PADDED))
    return (slope.reshape(1, 1, BAND_ROWS, AZIMUTH_STEPS), (shared + other)[0, 0])


def solution(mesh):
    return jax.shard_map(
        local,
        mesh=mesh,
        in_specs=(P("ens", "chan", "lat", None), P("chan", "lat", "ens")),
        out_specs=(P("ens", "chan", "lat", None), P()),
        check_vma=False,
    )
```

```python
import functools
import math

import jax
import jax.numpy as jnp
from jax import lax
from jax.experimental import pallas as pl
from jax.experimental.pallas import tpu as pltpu
from jax.sharding import PartitionSpec as P

PARALLEL_LINES = 720
AZIMUTH_STEPS = 1440
DEGREE_CUTOFF = 384
SOFTENING_EPS = 0.25
SPECTRAL_WEIGHT = 0.1

MEMBERS = 16
BANDS = 8
GROUPS = MEMBERS * BANDS
ORDERS = DEGREE_CUTOFF // GROUPS
BAND_ROWS = PARALLEL_LINES // BANDS
LON_BLOCK = AZIMUTH_STEPS // MEMBERS
ROW_GROUPS = 15
GROUP_ROWS = 6
LANES = 128
LON_CHUNKS = 12
LON_PADDED = LON_CHUNKS * LANES
SPECTRAL_ROWS = 2 * DEGREE_CUTOFF
BLOCK = 16
DFT_BLOCK = 64
PACKED_ROWS = GROUP_ROWS * LON_CHUNKS
PACKED_TILES = PACKED_ROWS // 8
PARTS = 2 * ORDERS

VMEM = pltpu.VMEM
MESH = pl.DeviceIdType.MESH
F32 = jnp.float32
BF16 = jnp.bfloat16


def params(**kw):
    return pltpu.CompilerParams(vmem_limit_bytes=48 << 20, **kw)


def iota(shape, dim):
    return lax.broadcasted_iota(jnp.int32, shape, dim)


def cos_sin(steps):
    quarter = jnp.floor(steps * (1.0 / 360.0) + 0.5)
    rest = (steps - 360.0 * quarter) * (2.0 * math.pi / AZIMUTH_STEPS)
    quadrant = quarter - 4.0 * jnp.floor(quarter * 0.25)
    square = rest * rest
    sine = rest * (
        1.0
        + square
        * (-1.0 / 6.0 + square * (1.0 / 120.0 + square * (-1.0 / 5040.0 + square * (1.0 / 362880.0))))
    )
    cosine = 1.0 + square * (
        -0.5
        + square
        * (1.0 / 24.0 + square * (-1.0 / 720.0 + square * (1.0 / 40320.0 - square * (1.0 / 3628800.0))))
    )
    odd = (quadrant == 1.0) | (quadrant == 3.0)
    cos_part = jnp.where(odd, sine, cosine)
    sin_part = jnp.where(odd, cosine, sine)
    cos_part = jnp.where((quadrant == 1.0) | (quadrant == 2.0), -cos_part, cos_part)
    sin_part = jnp.where(quadrant >= 2.0, -sin_part, sin_part)
    return cos_part, sin_part


def fill_dft(out_ref):
    def body(block, carry):
        row = block * DFT_BLOCK + iota((DFT_BLOCK, LANES), 0)
        lane = iota((DFT_BLOCK, LANES), 1)
        order = (row >> 1).astype(F32)
        turn = (360 * (row & 1)).astype(F32)
        cosine, sine = cos_sin(order * lane.astype(F32) + turn)
        cos_step, sin_step = cos_sin(order * float(LANES))
        rows = pl.ds(pl.multiple_of(block * DFT_BLOCK, DFT_BLOCK), DFT_BLOCK)
        for chunk in range(LON_CHUNKS):
            value = cosine
            if chunk == LON_CHUNKS - 1:
                value = jnp.where(lane < AZIMUTH_STEPS - LANES * chunk, value, 0.0)
            out_ref[rows, LANES * chunk : LANES * (chunk + 1)] = value.astype(BF16)
            cosine, sine = (
                cosine * cos_step - sine * sin_step,
                sine * cos_step + cosine * sin_step,
            )
        return carry

    lax.fori_loop(0, SPECTRAL_ROWS // DFT_BLOCK, body, 0)


def fill_recurrence(first, out_ref):
    order = (first + iota((8, DEGREE_CUTOFF), 0)).astype(F32)
    degree = iota((8, DEGREE_CUTOFF), 1).astype(F32)
    growing = degree > order
    denominator = jnp.where(growing, degree * degree - order * order, 1.0)
    leading = jnp.sqrt(jnp.maximum(4.0 * degree * degree - 1.0, 0.0) / denominator)
    trailing = jnp.sqrt(
        jnp.maximum(
            ((degree - 1.0) * (degree - 1.0) - order * order)
            * (2.0 * degree + 1.0)
            / ((2.0 * degree - 3.0) * denominator),
            0.0,
        )
    )
    out_ref[0:8, :] = jnp.where(growing, leading, 0.0)
    out_ref[8:16, :] = jnp.where(growing, trailing, 0.0)


def seed_logs(first):
    order = (first + iota((8, DEGREE_CUTOFF), 0)).astype(F32)
    factor = (1 + iota((8, DEGREE_CUTOFF), 1)).astype(F32)
    summands = jnp.where(factor <= order, jnp.log(1.0 - 0.5 / factor), 0.0)
    return 0.5 * jnp.log(order[:, 0:1] + 0.5) + 0.5 * jnp.sum(summands, axis=1, keepdims=True)


def fill_legendre(first, coef_ref, table_ref, out_ref):
    band, lane = iota((8, LANES), 0), iota((8, LANES), 1)
    group, part = lane >> 3, lane & 7
    valid = (group < ROW_GROUPS) & (part < GROUP_ROWS)
    row = jnp.where(valid, BAND_ROWS * band + GROUP_ROWS * group + part, 0)
    cos_lat, sin_lat = cos_sin(row.astype(F32) + 0.5)
    weight = jnp.where(valid, math.pi / PARALLEL_LINES * sin_lat, 0.0)
    log_sin = jnp.log(sin_lat)
    seeds = seed_logs(first)

    def body(block, carry):
        state = list(carry)
        for step in range(BLOCK):
            degree = block * BLOCK + step
            for index in range(ORDERS):
                latest, before, log_scale, factor = state[4 * index : 4 * index + 4]
                leading = coef_ref[index, degree]
                trailing = coef_ref[8 + index, degree]
                begin = jnp.where(degree == first + index, 1.0, 0.0)
                advanced = (leading * cos_lat) * latest + (begin - trailing * before)
                row = (index * DEGREE_CUTOFF + degree) * 8
                table_ref[pl.ds(pl.multiple_of(row, 8), 8), :] = advanced * factor
                state[4 * index : 4 * index + 4] = [advanced, latest, log_scale, factor]
        for index in range(ORDERS):
            latest, before, log_scale, factor = state[4 * index : 4 * index + 4]
            largest = jnp.maximum(jnp.abs(latest), jnp.abs(before))
            largest = jnp.where(largest > 0.0, largest, 1.0)
            shrink = 1.0 / largest
            log_scale = log_scale + jnp.log(largest)
            state[4 * index : 4 * index + 4] = [
                latest * shrink,
                before * shrink,
                log_scale,
                jnp.exp(log_scale) * weight,
            ]
        return tuple(state)

    state = []
    for index in range(ORDERS):
        order = jnp.broadcast_to((first + index).astype(F32), (8, LANES))
        start = jnp.broadcast_to(seeds[index : index + 1, :], (8, LANES)) + order * log_sin
        state += [jnp.zeros((8, LANES), F32), jnp.zeros((8, LANES), F32), start, jnp.exp(start) * weight]
    lax.fori_loop(0, DEGREE_CUTOFF // BLOCK, body, tuple(state))
    for index in range(ORDERS):
        for band in range(BANDS):
            rows = table_ref[pl.ds(index * DEGREE_CUTOFF * 8 + band, DEGREE_CUTOFF, stride=8), :]
            out_ref[index, :, LANES * band : LANES * (band + 1)] = rows.astype(BF16)


def fill_truth(blocks_ref, out_ref, packed_ref):
    lane = iota((8, LANES), 1)
    chunks = [jnp.zeros((8, LANES), F32) for _ in range(LON_CHUNKS)]
    for block in range(MEMBERS):
        first = LON_BLOCK * block
        value = blocks_ref[block].astype(F32)
        shift = first % LANES
        if shift:
            value = pltpu.roll(value, shift, 1)
        for chunk in range(first // LANES, (first + LON_BLOCK - 1) // LANES + 1):
            place = lane + chunk * LANES
            inside = (place >= first) & (place < first + LON_BLOCK)
            chunks[chunk] = jnp.where(inside, value, chunks[chunk])
    for chunk in range(LON_CHUNKS):
        out_ref[:, LANES * chunk : LANES * (chunk + 1)] = chunks[chunk]
        packed_ref[GROUP_ROWS * chunk : GROUP_ROWS * (chunk + 1), :] = chunks[chunk][0:GROUP_ROWS]


def grid_stage(ens, lat, draws_ref, truth_ref, counts_ref):
    row, lane = iota((8, LANES), 0), iota((8, LANES), 1)

    def body(tile, total):
        place = 8 * tile + row
        chunk = (place * 43) >> 8
        part = place - GROUP_ROWS * chunk
        line = (BAND_ROWS * lat + GROUP_ROWS * ens + part).astype(F32)
        kept = (lane + chunk * LANES < AZIMUTH_STEPS) & (ens < ROW_GROUPS)
        weight = jnp.where(kept, cos_sin(line + 0.5)[1], 0.0)
        draws = [draws_ref[i, tile].astype(F32) for i in range(MEMBERS)]
        target = truth_ref[pl.ds(pl.multiple_of(8 * tile, 8), 8), :]
        counts = [None] * MEMBERS
        for i in range(MEMBERS):
            for k in range(i + 1, MEMBERS):
                above = jnp.where(draws[i] > draws[k], 1.0, 0.0)
                turn = jnp.where(draws[i] < draws[k], -1.0, above)
                counts[i] = turn if counts[i] is None else counts[i] + turn
                counts[k] = -turn if counts[k] is None else counts[k] - turn
        spread = jnp.zeros((8, LANES), F32)
        for i in range(MEMBERS):
            gap = draws[i] - target
            above = jnp.where(draws[i] > target, float(MEMBERS - 1), 0.0)
            side = jnp.where(draws[i] < target, -float(MEMBERS - 1), above)
            counts_ref[i, tile] = (side - counts[i]).astype(BF16)
            spread = spread + (jnp.abs(gap) - (draws[i] * counts[i]) * (1.0 / (MEMBERS - 1)))
        return total + jnp.where(kept, weight * spread, 0.0)

    return lax.fori_loop(0, PACKED_TILES, body, jnp.zeros((8, LANES), F32))


def spectral_stage(first, grid_loss, modes_ref, table_ref, out_ref, wide_ref, lhs_ref):
    draws = MEMBERS
    scale = SPECTRAL_WEIGHT * PARALLEL_LINES * AZIMUTH_STEPS / (DEGREE_CUTOFF * (DEGREE_CUTOFF + 1) / 2)
    held = BANDS * PARTS
    lane = iota((held, LANES), 1)
    target = jnp.zeros((held, LANES), F32)
    for member in range(draws):
        value = modes_ref[8 * member : 8 * member + 8].astype(F32).reshape(held, LANES)
        wide_ref[held * member : held * (member + 1), :] = value
        if member < ROW_GROUPS:
            moved = pltpu.roll(value, (8 * member + 8) % LANES, 1)
            target = jnp.where((lane >> 3) == member, moved, target)
    loss = jnp.zeros((1, DEGREE_CUTOFF), F32)
    degree = iota((1, DEGREE_CUTOFF), 1)
    pad = jnp.zeros((14, LANES), F32)
    for index in range(ORDERS):
        for band in range(BANDS):
            lanes = slice(LANES * band, LANES * (band + 1))
            parts = [
                wide_ref[pl.ds(PARTS * band + 2 * index + r, draws, stride=held), :] for r in range(2)
            ]
            aim = PARTS * band + 2 * index
            aims = [target[aim + r : aim + r + 1, :] for r in range(2)]
            lhs_ref[index, :, lanes] = jnp.concatenate(parts + aims + [pad], axis=0).astype(BF16)
        terms = lax.dot_general(
            lhs_ref[index],
            table_ref[index],
            (((1,), (1,)), ((), ())),
            preferred_element_type=F32,
        )
        real, imag = terms[0:draws], terms[draws : 2 * draws]
        real_aim, imag_aim = terms[2 * draws : 2 * draws + 1], terms[2 * draws + 1 : 2 * draws + 2]
        gap_real, gap_imag = real - real_aim, imag - imag_aim
        square = gap_real * gap_real + gap_imag * gap_imag + SOFTENING_EPS**2
        inverse = lax.rsqrt(square)
        near = square * inverse
        step_real, step_imag = gap_real * inverse, gap_imag * inverse
        pair = jnp.zeros_like(real)
        pull_real, pull_imag = jnp.zeros_like(real), jnp.zeros_like(real)
        for other in range(draws):
            gap_real, gap_imag = real - real[other : other + 1], imag - imag[other : other + 1]
            square = gap_real * gap_real + gap_imag * gap_imag + SOFTENING_EPS**2
            inverse = lax.rsqrt(square)
            pair = pair + square * inverse
            pull_real = pull_real + gap_real * inverse
            pull_imag = pull_imag + gap_imag * inverse
        kept = degree >= first + index
        score = jnp.sum(near, axis=0, keepdims=True) - (
            jnp.sum(pair, axis=0, keepdims=True) - draws * SOFTENING_EPS
        ) / (2.0 * (draws - 1))
        loss = loss + jnp.where(kept, score, 0.0)
        down = jnp.concatenate(
            [step_real - pull_real / (draws - 1), step_imag - pull_imag / (draws - 1)], axis=0
        )
        grad = jnp.where(kept, scale * down, 0.0).astype(BF16)
        back = jnp.dot(grad, table_ref[index], preferred_element_type=F32)
        for band in range(BANDS):
            for r in range(2):
                wide_ref[pl.ds(PARTS * band + 2 * index + r, draws, stride=held), :] = back[
                    draws * r : draws * (r + 1), LANES * band : LANES * (band + 1)
                ]
    local = jnp.sum(jnp.sum(grid_loss, axis=0, keepdims=True), axis=1, keepdims=True) / (
        PARALLEL_LINES * AZIMUTH_STEPS
    ) + SPECTRAL_WEIGHT / (DEGREE_CUTOFF * (DEGREE_CUTOFF + 1) / 2) * jnp.sum(loss, axis=1, keepdims=True)
    high = local.astype(BF16).astype(F32)
    middle = (local - high).astype(BF16).astype(F32)
    low = local - high - middle
    row = iota((BANDS, ORDERS, 2, LANES), 1) + iota((BANDS, ORDERS, 2, LANES), 2)
    column = iota((BANDS, ORDERS, 2, LANES), 3)
    high, middle, low = (v.reshape(1, 1, 1, 1) for v in (high, middle, low))
    spare = jnp.where(column == LANES - 8, high, jnp.where(column == LANES - 7, middle, low))
    carries = (row == 0) & (column >= LANES - 8) & (column < LANES - 5)
    for member in range(draws):
        value = wide_ref[held * member : held * (member + 1), :].reshape(BANDS, ORDERS, 2, LANES)
        value = jnp.where(carries, spare, value)
        out_ref[BANDS * member : BANDS * (member + 1)] = value.astype(BF16)


def exchange_kernel(
    own_hbm_ref,
    truth_hbm_ref,
    dft_ref,
    back_in_ref,
    counts_in_ref,
    loss_ref,
    own_ref,
    truth_in_ref,
    packed_ref,
    truth_packed_ref,
    wide_own_ref,
    rows_out_ref,
    rows_in_ref,
    blocks_out_ref,
    blocks_in_ref,
    truth_ref,
    field_ref,
    modes_out_ref,
    modes_in_ref,
    coef_vector_ref,
    coef_ref,
    table_ref,
    legendre_ref,
    counts_out_ref,
    back_out_ref,
    wide_ref,
    lhs_ref,
    send_sem,
    recv_sem,
    local_sem,
):
    chan, ens, lat = lax.axis_index("chan"), lax.axis_index("ens"), lax.axis_index("lat")
    mine = ens * BANDS + lat
    first = ORDERS * mine
    truth_copy = pltpu.make_async_copy(truth_hbm_ref, truth_in_ref, local_sem.at[0])
    truth_copy.start()
    own_copy = pltpu.make_async_copy(own_hbm_ref, own_ref, local_sem.at[1])
    own_copy.start()

    barrier = pltpu.get_barrier_semaphore()

    def greet(step, carry):
        peer = lax.rem(mine + step, GROUPS)
        pl.semaphore_signal(
            barrier,
            inc=1,
            device_id=(chan, lax.div(peer, BANDS), lax.rem(peer, BANDS)),
            device_id_type=MESH,
        )
        return carry

    lax.fori_loop(1, GROUPS, greet, 0)

    def copy(source, target, kind, peer_ens, peer_lat):
        return pltpu.make_async_remote_copy(
            src_ref=source,
            dst_ref=target,
            send_sem=send_sem.at[kind],
            recv_sem=recv_sem.at[kind],
            device_id=(chan, peer_ens, peer_lat),
            device_id_type=MESH,
        )

    def to_members(source, target, kind):
        def body(step, carry):
            peer = lax.rem(ens + step, MEMBERS)
            copy(source.at[peer], target.at[ens], kind, peer, lat).start()
            return carry

        lax.fori_loop(1, MEMBERS, body, 0)
        target[ens] = source[ens]

    def to_groups(source, target, kind, block):
        def body(step, carry):
            peer = block * 32 + lax.rem(mine + step, 32)

            @pl.when(peer != mine)
            def _():
                copy(source.at[peer], target.at[mine], kind, lax.div(peer, BANDS), lax.rem(peer, BANDS)).start()

            return carry

        lax.fori_loop(0, 32, body, 0)

    def all_of(source, target, kind, count):
        return copy(source.at[pl.ds(0, count)], target.at[pl.ds(0, count)], kind, ens, lat)

    wide_own_ref[88:96, :] = jnp.zeros((8, LON_PADDED), F32)
    wide_own_ref[:, LON_PADDED - LANES :] = jnp.zeros((96, LANES), F32)
    truth_copy.wait()
    wide_own_ref[0:BAND_ROWS, 0:LON_BLOCK] = truth_in_ref[...].astype(F32)
    for group in range(ROW_GROUPS):
        blocks_out_ref[group] = wide_own_ref[GROUP_ROWS * group : GROUP_ROWS * group + 8, 0:LANES].astype(BF16)
    blocks_out_ref[ROW_GROUPS] = jnp.zeros((8, LANES), BF16)
    pl.semaphore_wait(barrier, GROUPS - 1)
    to_members(blocks_out_ref, blocks_in_ref, 0)

    own_copy.wait()
    wide_own_ref[0:BAND_ROWS, 0:AZIMUTH_STEPS] = own_ref[...].astype(F32)
    for group in range(ROW_GROUPS):
        for chunk in range(LON_CHUNKS):
            packed_ref[GROUP_ROWS * chunk : GROUP_ROWS * (chunk + 1), :] = wide_own_ref[
                GROUP_ROWS * group : GROUP_ROWS * (group + 1), LANES * chunk : LANES * (chunk + 1)
            ]
        rows_out_ref[group] = packed_ref[...].reshape(PACKED_TILES, 8, LANES).astype(BF16)
    rows_out_ref[ROW_GROUPS] = jnp.zeros((PACKED_TILES, 8, LANES), BF16)
    to_members(rows_out_ref, rows_in_ref, 1)

    fill_recurrence(first, coef_vector_ref)
    coef_copy = pltpu.make_async_copy(coef_vector_ref, coef_ref, local_sem.at[2])
    coef_copy.start()
    for pair in range(7):
        both = [
            wide_own_ref[GROUP_ROWS * group : GROUP_ROWS * group + 8, :] for group in (2 * pair, 2 * pair + 1)
        ]
        field_ref[16 * pair : 16 * pair + 16, :] = jnp.concatenate(both, axis=0).astype(BF16)
    fill_dft(dft_ref)

    all_of(blocks_out_ref, blocks_in_ref, 0, MEMBERS - 1).wait_recv()
    fill_truth(blocks_in_ref, truth_ref, truth_packed_ref)
    both = [wide_own_ref[84:92, :], truth_ref[...]]
    field_ref[112:128, :] = jnp.concatenate(both, axis=0).astype(BF16)

    def fourier(step, carry):
        block = lax.rem(lax.div(mine, 32) + step, 4)
        modes = lax.dot_general(
            dft_ref[pl.ds(pl.multiple_of(block * 192, 192), 192), :],
            field_ref[...],
            (((1,), (1,)), ((), ())),
            preferred_element_type=F32,
        )
        modes_out_ref[pl.ds(block * 32, 32)] = modes.reshape(32, ORDERS, 2, LANES).astype(BF16)
        to_groups(modes_out_ref, modes_in_ref, 2, block)
        return carry

    lax.fori_loop(0, 4, fourier, 0)
    modes_in_ref[mine] = modes_out_ref[mine]

    coef_copy.wait()
    fill_legendre(first, coef_ref, table_ref, legendre_ref)

    all_of(rows_out_ref, rows_in_ref, 1, MEMBERS - 1).wait_recv()
    grid_loss = grid_stage(ens, lat, rows_in_ref, truth_packed_ref, counts_out_ref)
    to_members(counts_out_ref, counts_in_ref, 3)

    all_of(modes_out_ref, modes_in_ref, 2, GROUPS - 1).wait_recv()
    spectral_stage(first, grid_loss, modes_in_ref, legendre_ref, back_out_ref, wide_ref, lhs_ref)

    def give_back(step, carry):
        to_groups(back_out_ref, back_in_ref, 4, lax.rem(lax.div(mine, 32) + step, 4))
        return carry

    lax.fori_loop(0, 4, give_back, 0)
    back_in_ref[mine] = back_out_ref[mine]

    all_of(counts_out_ref, counts_in_ref, 3, MEMBERS - 1).wait_recv()
    all_of(back_out_ref, back_in_ref, 4, GROUPS - 1).wait_recv()
    total = jnp.zeros((2, LANES), F32)
    for block in range(16):
        total = total + jnp.sum(back_in_ref[8 * block : 8 * block + 8, 0].astype(F32), axis=0)
    row, column = iota((2, LANES), 0), iota((2, LANES), 1)
    total = jnp.where((row == 0) & (column >= LANES - 8) & (column < LANES - 5), total, 0.0)
    loss_ref[...] = jnp.sum(jnp.sum(total, axis=0, keepdims=True), axis=1, keepdims=True)

    all_of(blocks_out_ref, blocks_in_ref, 0, MEMBERS - 1).wait_send()
    all_of(rows_out_ref, rows_in_ref, 1, MEMBERS - 1).wait_send()
    all_of(modes_out_ref, modes_in_ref, 2, GROUPS - 1).wait_send()
    all_of(counts_out_ref, counts_in_ref, 3, MEMBERS - 1).wait_send()
    all_of(back_out_ref, back_in_ref, 4, GROUPS - 1).wait_send()


def exchange(own, target):
    rows = (MEMBERS, PACKED_TILES, 8, LANES)
    blocks = (MEMBERS, 8, LANES)
    modes = (GROUPS, ORDERS, 2, LANES)
    return pl.pallas_call(
        exchange_kernel,
        out_shape=(
            jax.ShapeDtypeStruct((SPECTRAL_ROWS, LON_PADDED), BF16),
            jax.ShapeDtypeStruct(modes, BF16),
            jax.ShapeDtypeStruct(rows, BF16),
            jax.ShapeDtypeStruct((1, 1), F32),
        ),
        in_specs=[pl.BlockSpec(memory_space=pltpu.HBM)] * 2,
        out_specs=tuple([pl.BlockSpec(memory_space=VMEM)] * 4),
        scratch_shapes=[
            VMEM((BAND_ROWS, AZIMUTH_STEPS), BF16),
            VMEM((BAND_ROWS, LON_BLOCK), BF16),
            VMEM((PACKED_ROWS, LANES), F32),
            VMEM((PACKED_ROWS, LANES), F32),
            VMEM((96, LON_PADDED), F32),
            VMEM(rows, BF16),
            VMEM(rows, BF16),
            VMEM(blocks, BF16),
            VMEM(blocks, BF16),
            VMEM((8, LON_PADDED), F32),
            VMEM((LANES, LON_PADDED), BF16),
            VMEM(modes, BF16),
            VMEM(modes, BF16),
            VMEM((16, DEGREE_CUTOFF), F32),
            pltpu.SMEM((16, DEGREE_CUTOFF), F32),
            VMEM((ORDERS * DEGREE_CUTOFF * 8, LANES), F32),
            VMEM((ORDERS, DEGREE_CUTOFF, BANDS * LANES), BF16),
            VMEM(rows, BF16),
            VMEM(modes, BF16),
            VMEM((SPECTRAL_ROWS, LANES), F32),
            VMEM((ORDERS, 48, BANDS * LANES), BF16),
            pltpu.SemaphoreType.DMA((5,)),
            pltpu.SemaphoreType.DMA((5,)),
            pltpu.SemaphoreType.DMA((3,)),
        ],
        compiler_params=params(collective_id=0, has_side_effects=True),
        cost_estimate=pl.CostEstimate(flops=800_000_000, bytes_accessed=8 << 20, transcendentals=0),
    )(own, target)


def final_kernel(table_ref, modes_ref, counts_ref, out_ref, packed_ref):
    row = iota((LANES, LANES), 0)
    line = BAND_ROWS * lax.axis_index("lat") + GROUP_ROWS * (row >> 3) + (row & 7)
    weight = cos_sin(line.astype(F32) + 0.5)[1] / (MEMBERS - 1)
    for group in range(ROW_GROUPS):
        packed_ref[PACKED_ROWS * group : PACKED_ROWS * (group + 1), :] = (
            counts_ref[group].astype(F32).reshape(PACKED_ROWS, LANES)
        )
    for chunk in range(LON_CHUNKS):
        lanes = slice(LANES * chunk, LANES * (chunk + 1))
        width = min(LANES, AZIMUTH_STEPS - LANES * chunk)
        wave = lax.dot_general(
            modes_ref[...],
            table_ref[:, lanes],
            (((0,), (0,)), ((), ())),
            preferred_element_type=F32,
        )
        for group in range(ROW_GROUPS):
            first = PACKED_ROWS * group + GROUP_ROWS * chunk
            rows = slice(8 * group, 8 * group + GROUP_ROWS)
            total = weight[rows] * packed_ref[first : first + GROUP_ROWS, :] + wave[rows]
            out_ref[
                GROUP_ROWS * group : GROUP_ROWS * (group + 1), 0, LANES * chunk : LANES * chunk + width
            ] = total[:, 0:width]


def final(table, modes, counts):
    return pl.pallas_call(
        final_kernel,
        out_shape=jax.ShapeDtypeStruct((BAND_ROWS, 1, AZIMUTH_STEPS), F32),
        in_specs=[pl.BlockSpec(memory_space=VMEM)] * 3,
        out_specs=pl.BlockSpec(memory_space=VMEM),
        scratch_shapes=[VMEM((ROW_GROUPS * PACKED_ROWS, LANES), F32)],
        compiler_params=params(),
        cost_estimate=pl.CostEstimate(flops=400_000_000, bytes_accessed=4 << 20, transcendentals=0),
    )(table, modes, counts)


def local(model_outputs, verifying_truth):
    table, back, counts, shared = exchange(model_outputs[0, 0], verifying_truth[0])
    other = lax.ppermute(shared, "chan", [(0, 1), (1, 0)])
    slope = final(table, back.reshape(SPECTRAL_ROWS, LANES), counts)
    return (slope.reshape(1, 1, BAND_ROWS, AZIMUTH_STEPS), (shared + other)[0, 0])


def solution(mesh):
    return jax.shard_map(
        local,
        mesh=mesh,
        in_specs=(P("ens", "chan", "lat", None), P("chan", "lat", "ens")),
        out_specs=(P("ens", "chan", "lat", None), P()),
        check_vma=False,
    )
```

```python
import functools
import math

import jax
import jax.numpy as jnp
from jax import lax
from jax.experimental import pallas as pl
from jax.experimental.pallas import tpu as pltpu
from jax.sharding import PartitionSpec as P

PARALLEL_LINES = 720
AZIMUTH_STEPS = 1440
DEGREE_CUTOFF = 384
SOFTENING_EPS = 0.25
SPECTRAL_WEIGHT = 0.1

MEMBERS = 16
BANDS = 8
GROUPS = MEMBERS * BANDS
ORDERS = DEGREE_CUTOFF // GROUPS
BAND_ROWS = PARALLEL_LINES // BANDS
LON_BLOCK = AZIMUTH_STEPS // MEMBERS
ROW_GROUPS = 15
GROUP_ROWS = 6
LANES = 128
LON_CHUNKS = 12
LON_PADDED = LON_CHUNKS * LANES
SPECTRAL_ROWS = 2 * DEGREE_CUTOFF
BLOCK = 16
DFT_BLOCK = 64
PACKED_ROWS = GROUP_ROWS * LON_CHUNKS
PACKED_TILES = PACKED_ROWS // 8
PARTS = 2 * ORDERS
FAR_FIRST = (2, 1, 3, 0)

VMEM = pltpu.VMEM
MESH = pl.DeviceIdType.MESH
F32 = jnp.float32
BF16 = jnp.bfloat16


def params(**kw):
    return pltpu.CompilerParams(vmem_limit_bytes=48 << 20, **kw)


def iota(shape, dim):
    return lax.broadcasted_iota(jnp.int32, shape, dim)


def cos_sin(steps):
    quarter = jnp.floor(steps * (1.0 / 360.0) + 0.5)
    rest = (steps - 360.0 * quarter) * (2.0 * math.pi / AZIMUTH_STEPS)
    quadrant = quarter - 4.0 * jnp.floor(quarter * 0.25)
    square = rest * rest
    sine = rest * (
        1.0
        + square
        * (-1.0 / 6.0 + square * (1.0 / 120.0 + square * (-1.0 / 5040.0 + square * (1.0 / 362880.0))))
    )
    cosine = 1.0 + square * (
        -0.5
        + square
        * (1.0 / 24.0 + square * (-1.0 / 720.0 + square * (1.0 / 40320.0 - square * (1.0 / 3628800.0))))
    )
    odd = (quadrant == 1.0) | (quadrant == 3.0)
    cos_part = jnp.where(odd, sine, cosine)
    sin_part = jnp.where(odd, cosine, sine)
    cos_part = jnp.where((quadrant == 1.0) | (quadrant == 2.0), -cos_part, cos_part)
    sin_part = jnp.where(quadrant >= 2.0, -sin_part, sin_part)
    return cos_part, sin_part


def fill_dft(out_ref):
    def body(block, carry):
        row = block * DFT_BLOCK + iota((DFT_BLOCK, LANES), 0)
        lane = iota((DFT_BLOCK, LANES), 1)
        order = (row >> 1).astype(F32)
        turn = (360 * (row & 1)).astype(F32)
        cosine, sine = cos_sin(order * lane.astype(F32) + turn)
        cos_step, sin_step = cos_sin(order * float(LANES))
        rows = pl.ds(pl.multiple_of(block * DFT_BLOCK, DFT_BLOCK), DFT_BLOCK)
        for chunk in range(LON_CHUNKS):
            value = cosine
            if chunk == LON_CHUNKS - 1:
                value = jnp.where(lane < AZIMUTH_STEPS - LANES * chunk, value, 0.0)
            out_ref[rows, LANES * chunk : LANES * (chunk + 1)] = value.astype(BF16)
            cosine, sine = (
                cosine * cos_step - sine * sin_step,
                sine * cos_step + cosine * sin_step,
            )
        return carry

    lax.fori_loop(0, SPECTRAL_ROWS // DFT_BLOCK, body, 0)


def fill_recurrence(first, out_ref):
    order = (first + iota((8, DEGREE_CUTOFF), 0)).astype(F32)
    degree = iota((8, DEGREE_CUTOFF), 1).astype(F32)
    growing = degree > order
    denominator = jnp.where(growing, degree * degree - order * order, 1.0)
    leading = jnp.sqrt(jnp.maximum(4.0 * degree * degree - 1.0, 0.0) / denominator)
    trailing = jnp.sqrt(
        jnp.maximum(
            ((degree - 1.0) * (degree - 1.0) - order * order)
            * (2.0 * degree + 1.0)
            / ((2.0 * degree - 3.0) * denominator),
            0.0,
        )
    )
    out_ref[0:8, :] = jnp.where(growing, leading, 0.0)
    out_ref[8:16, :] = jnp.where(growing, trailing, 0.0)


def seed_logs(first):
    order = (first + iota((8, DEGREE_CUTOFF), 0)).astype(F32)
    factor = (1 + iota((8, DEGREE_CUTOFF), 1)).astype(F32)
    summands = jnp.where(factor <= order, jnp.log(1.0 - 0.5 / factor), 0.0)
    return 0.5 * jnp.log(order[:, 0:1] + 0.5) + 0.5 * jnp.sum(summands, axis=1, keepdims=True)


def fill_legendre(first, coef_ref, table_ref, out_ref):
    band, lane = iota((8, LANES), 0), iota((8, LANES), 1)
    group, part = lane >> 3, lane & 7
    valid = (group < ROW_GROUPS) & (part < GROUP_ROWS)
    row = jnp.where(valid, BAND_ROWS * band + GROUP_ROWS * group + part, 0)
    cos_lat, sin_lat = cos_sin(row.astype(F32) + 0.5)
    weight = jnp.where(valid, math.pi / PARALLEL_LINES * sin_lat, 0.0)
    log_sin = jnp.log(sin_lat)
    seeds = seed_logs(first)

    def body(block, carry):
        state = list(carry)
        for step in range(BLOCK):
            degree = block * BLOCK + step
            for index in range(ORDERS):
                latest, before, log_scale, factor = state[4 * index : 4 * index + 4]
                leading = coef_ref[index, degree]
                trailing = coef_ref[8 + index, degree]
                begin = jnp.where(degree == first + index, 1.0, 0.0)
                advanced = (leading * cos_lat) * latest + (begin - trailing * before)
                row = (index * DEGREE_CUTOFF + degree) * 8
                table_ref[pl.ds(pl.multiple_of(row, 8), 8), :] = advanced * factor
                state[4 * index : 4 * index + 4] = [advanced, latest, log_scale, factor]
        for index in range(ORDERS):
            latest, before, log_scale, factor = state[4 * index : 4 * index + 4]
            largest = jnp.maximum(jnp.abs(latest), jnp.abs(before))
            largest = jnp.where(largest > 0.0, largest, 1.0)
            shrink = 1.0 / largest
            log_scale = log_scale + jnp.log(largest)
            state[4 * index : 4 * index + 4] = [
                latest * shrink,
                before * shrink,
                log_scale,
                jnp.exp(log_scale) * weight,
            ]
        return tuple(state)

    state = []
    for index in range(ORDERS):
        order = jnp.broadcast_to((first + index).astype(F32), (8, LANES))
        start = jnp.broadcast_to(seeds[index : index + 1, :], (8, LANES)) + order * log_sin
        state += [jnp.zeros((8, LANES), F32), jnp.zeros((8, LANES), F32), start, jnp.exp(start) * weight]
    lax.fori_loop(0, DEGREE_CUTOFF // BLOCK, body, tuple(state))
    for index in range(ORDERS):
        for band in range(BANDS):
            rows = table_ref[pl.ds(index * DEGREE_CUTOFF * 8 + band, DEGREE_CUTOFF, stride=8), :]
            out_ref[index, :, LANES * band : LANES * (band + 1)] = rows.astype(BF16)


def fill_truth(blocks_ref, out_ref, packed_ref):
    lane = iota((8, LANES), 1)
    chunks = [jnp.zeros((8, LANES), F32) for _ in range(LON_CHUNKS)]
    for block in range(MEMBERS):
        first = LON_BLOCK * block
        value = blocks_ref[block].astype(F32)
        shift = first % LANES
        if shift:
            value = pltpu.roll(value, shift, 1)
        for chunk in range(first // LANES, (first + LON_BLOCK - 1) // LANES + 1):
            place = lane + chunk * LANES
            inside = (place >= first) & (place < first + LON_BLOCK)
            chunks[chunk] = jnp.where(inside, value, chunks[chunk])
    for chunk in range(LON_CHUNKS):
        out_ref[:, LANES * chunk : LANES * (chunk + 1)] = chunks[chunk]
        packed_ref[GROUP_ROWS * chunk : GROUP_ROWS * (chunk + 1), :] = chunks[chunk][0:GROUP_ROWS]


def grid_stage(ens, lat, draws_ref, truth_ref, counts_ref):
    row, lane = iota((8, LANES), 0), iota((8, LANES), 1)

    def body(tile, total):
        place = 8 * tile + row
        chunk = (place * 43) >> 8
        part = place - GROUP_ROWS * chunk
        line = (BAND_ROWS * lat + GROUP_ROWS * ens + part).astype(F32)
        kept = (lane + chunk * LANES < AZIMUTH_STEPS) & (ens < ROW_GROUPS)
        weight = jnp.where(kept, cos_sin(line + 0.5)[1], 0.0)
        draws = [draws_ref[i, tile].astype(F32) for i in range(MEMBERS)]
        target = truth_ref[pl.ds(pl.multiple_of(8 * tile, 8), 8), :]
        counts = [None] * MEMBERS
        for i in range(MEMBERS):
            for k in range(i + 1, MEMBERS):
                above = jnp.where(draws[i] > draws[k], 1.0, 0.0)
                turn = jnp.where(draws[i] < draws[k], -1.0, above)
                counts[i] = turn if counts[i] is None else counts[i] + turn
                counts[k] = -turn if counts[k] is None else counts[k] - turn
        spread = jnp.zeros((8, LANES), F32)
        for i in range(MEMBERS):
            gap = draws[i] - target
            above = jnp.where(draws[i] > target, float(MEMBERS - 1), 0.0)
            side = jnp.where(draws[i] < target, -float(MEMBERS - 1), above)
            counts_ref[i, tile] = (side - counts[i]).astype(BF16)
            spread = spread + (jnp.abs(gap) - (draws[i] * counts[i]) * (1.0 / (MEMBERS - 1)))
        return total + jnp.where(kept, weight * spread, 0.0)

    return lax.fori_loop(0, PACKED_TILES, body, jnp.zeros((8, LANES), F32))


def spectral_stage(first, grid_loss, modes_ref, table_ref, wide_ref, lhs_ref):
    draws = MEMBERS
    scale = SPECTRAL_WEIGHT * PARALLEL_LINES * AZIMUTH_STEPS / (DEGREE_CUTOFF * (DEGREE_CUTOFF + 1) / 2)
    held = BANDS * PARTS
    lane = iota((held, LANES), 1)
    target = jnp.zeros((held, LANES), F32)
    for member in range(draws):
        value = modes_ref[8 * member : 8 * member + 8].astype(F32).reshape(held, LANES)
        wide_ref[held * member : held * (member + 1), :] = value
        if member < ROW_GROUPS:
            moved = pltpu.roll(value, (8 * member + 8) % LANES, 1)
            target = jnp.where((lane >> 3) == member, moved, target)
    loss = jnp.zeros((1, DEGREE_CUTOFF), F32)
    degree = iota((1, DEGREE_CUTOFF), 1)
    pad = jnp.zeros((14, LANES), F32)
    for index in range(ORDERS):
        for band in range(BANDS):
            lanes = slice(LANES * band, LANES * (band + 1))
            parts = [
                wide_ref[pl.ds(PARTS * band + 2 * index + r, draws, stride=held), :] for r in range(2)
            ]
            aim = PARTS * band + 2 * index
            aims = [target[aim + r : aim + r + 1, :] for r in range(2)]
            lhs_ref[index, :, lanes] = jnp.concatenate(parts + aims + [pad], axis=0).astype(BF16)
        terms = lax.dot_general(
            lhs_ref[index],
            table_ref[index],
            (((1,), (1,)), ((), ())),
            preferred_element_type=F32,
        )
        real, imag = terms[0:draws], terms[draws : 2 * draws]
        real_aim, imag_aim = terms[2 * draws : 2 * draws + 1], terms[2 * draws + 1 : 2 * draws + 2]
        gap_real, gap_imag = real - real_aim, imag - imag_aim
        square = gap_real * gap_real + gap_imag * gap_imag + SOFTENING_EPS**2
        inverse = lax.rsqrt(square)
        near = square * inverse
        step_real, step_imag = gap_real * inverse, gap_imag * inverse
        pair = jnp.zeros_like(real)
        pull_real, pull_imag = jnp.zeros_like(real), jnp.zeros_like(real)
        for other in range(draws):
            gap_real, gap_imag = real - real[other : other + 1], imag - imag[other : other + 1]
            square = gap_real * gap_real + gap_imag * gap_imag + SOFTENING_EPS**2
            inverse = lax.rsqrt(square)
            pair = pair + square * inverse
            pull_real = pull_real + gap_real * inverse
            pull_imag = pull_imag + gap_imag * inverse
        kept = degree >= first + index
        score = jnp.sum(near, axis=0, keepdims=True) - (
            jnp.sum(pair, axis=0, keepdims=True) - draws * SOFTENING_EPS
        ) / (2.0 * (draws - 1))
        loss = loss + jnp.where(kept, score, 0.0)
        down = jnp.concatenate(
            [step_real - pull_real / (draws - 1), step_imag - pull_imag / (draws - 1)], axis=0
        )
        grad = jnp.where(kept, scale * down, 0.0).astype(BF16)
        back = jnp.dot(grad, table_ref[index], preferred_element_type=F32)
        for band in range(BANDS):
            for r in range(2):
                wide_ref[pl.ds(PARTS * band + 2 * index + r, draws, stride=held), :] = back[
                    draws * r : draws * (r + 1), LANES * band : LANES * (band + 1)
                ]
    local = jnp.sum(jnp.sum(grid_loss, axis=0, keepdims=True), axis=1, keepdims=True) / (
        PARALLEL_LINES * AZIMUTH_STEPS
    ) + SPECTRAL_WEIGHT / (DEGREE_CUTOFF * (DEGREE_CUTOFF + 1) / 2) * jnp.sum(loss, axis=1, keepdims=True)
    high = local.astype(BF16).astype(F32)
    middle = (local - high).astype(BF16).astype(F32)
    low = local - high - middle
    row = iota((BANDS, ORDERS, 2, LANES), 1) + iota((BANDS, ORDERS, 2, LANES), 2)
    column = iota((BANDS, ORDERS, 2, LANES), 3)
    high, middle, low = (v.reshape(1, 1, 1, 1) for v in (high, middle, low))
    spare = jnp.where(column == LANES - 8, high, jnp.where(column == LANES - 7, middle, low))
    carries = (row == 0) & (column >= LANES - 8) & (column < LANES - 5)
    return spare, carries


def exchange_kernel(
    own_hbm_ref,
    truth_hbm_ref,
    dft_ref,
    back_in_ref,
    counts_in_ref,
    loss_ref,
    own_ref,
    truth_in_ref,
    packed_ref,
    truth_packed_ref,
    wide_own_ref,
    rows_out_ref,
    rows_in_ref,
    blocks_out_ref,
    blocks_in_ref,
    truth_ref,
    field_ref,
    modes_out_ref,
    modes_in_ref,
    coef_vector_ref,
    coef_ref,
    table_ref,
    legendre_ref,
    counts_out_ref,
    back_out_ref,
    wide_ref,
    lhs_ref,
    send_sem,
    recv_sem,
    local_sem,
):
    chan, ens, lat = lax.axis_index("chan"), lax.axis_index("ens"), lax.axis_index("lat")
    mine = ens * BANDS + lat
    first = ORDERS * mine
    y, x = lax.div(ens, 4), lax.rem(lat, 4)
    z = lax.div(lat, 4) * 4 + lax.rem(ens, 4)
    truth_copy = pltpu.make_async_copy(truth_hbm_ref, truth_in_ref, local_sem.at[0])
    truth_copy.start()
    own_copy = pltpu.make_async_copy(own_hbm_ref, own_ref, local_sem.at[1])
    own_copy.start()

    barrier = pltpu.get_barrier_semaphore()

    def greet(step, carry):
        peer = lax.rem(mine + step, GROUPS)
        pl.semaphore_signal(
            barrier,
            inc=1,
            device_id=(chan, lax.div(peer, BANDS), lax.rem(peer, BANDS)),
            device_id_type=MESH,
        )
        return carry

    lax.fori_loop(1, GROUPS, greet, 0)

    def copy(source, target, kind, peer_ens, peer_lat):
        return pltpu.make_async_remote_copy(
            src_ref=source,
            dst_ref=target,
            send_sem=send_sem.at[kind],
            recv_sem=recv_sem.at[kind],
            device_id=(chan, peer_ens, peer_lat),
            device_id_type=MESH,
        )

    def to_members(source, target, kind):
        def body(step, carry):
            peer_y = lax.rem(y + FAR_FIRST[0] + lax.div(step, 4), 4)
            peer = peer_y * 4 + lax.rem(ens + 2 + step, 4)

            @pl.when(peer != ens)
            def _():
                copy(source.at[peer], target.at[ens], kind, peer, lat).start()

            return carry

        lax.fori_loop(0, MEMBERS, body, 0)
        target[ens] = source[ens]

    def to_groups(source, target, kind, y_step):
        peer_y = lax.rem(y + y_step, 4)

        def send(z_step, x_step):
            peer_z, peer_x = lax.rem(z + z_step, 8), lax.rem(x + x_step, 4)
            peer_ens = peer_y * 4 + lax.rem(peer_z, 4)
            peer_lat = lax.div(peer_z, 4) * 4 + peer_x
            copy(
                source.at[peer_ens * BANDS + peer_lat], target.at[mine], kind, peer_ens, peer_lat
            ).start()

        def body(step, carry):
            z_step = 4 + lax.div(step + 1, 2) * (1 - 2 * lax.rem(step, 2))
            for x_step in FAR_FIRST:
                send(z_step, x_step)
            return carry

        lax.fori_loop(0, 8 if y_step else 7, body, 0)
        if y_step == 0:
            for x_step in FAR_FIRST[:3]:
                send(0, x_step)

    def all_of(source, target, kind, count):
        return copy(source.at[pl.ds(0, count)], target.at[pl.ds(0, count)], kind, ens, lat)

    wide_own_ref[88:96, :] = jnp.zeros((8, LON_PADDED), F32)
    wide_own_ref[:, LON_PADDED - LANES :] = jnp.zeros((96, LANES), F32)
    truth_copy.wait()
    wide_own_ref[0:BAND_ROWS, 0:LON_BLOCK] = truth_in_ref[...].astype(F32)
    for group in range(ROW_GROUPS):
        blocks_out_ref[group] = wide_own_ref[GROUP_ROWS * group : GROUP_ROWS * group + 8, 0:LANES].astype(BF16)
    blocks_out_ref[ROW_GROUPS] = jnp.zeros((8, LANES), BF16)

    own_copy.wait()
    wide_own_ref[0:BAND_ROWS, 0:AZIMUTH_STEPS] = own_ref[...].astype(F32)
    for group in range(ROW_GROUPS):
        for chunk in range(LON_CHUNKS):
            packed_ref[GROUP_ROWS * chunk : GROUP_ROWS * (chunk + 1), :] = wide_own_ref[
                GROUP_ROWS * group : GROUP_ROWS * (group + 1), LANES * chunk : LANES * (chunk + 1)
            ]
        rows_out_ref[group] = packed_ref[...].reshape(PACKED_TILES, 8, LANES).astype(BF16)
    rows_out_ref[ROW_GROUPS] = jnp.zeros((PACKED_TILES, 8, LANES), BF16)

    fill_recurrence(first, coef_vector_ref)
    coef_copy = pltpu.make_async_copy(coef_vector_ref, coef_ref, local_sem.at[2])
    coef_copy.start()
    for pair in range(7):
        both = [
            wide_own_ref[GROUP_ROWS * group : GROUP_ROWS * group + 8, :] for group in (2 * pair, 2 * pair + 1)
        ]
        field_ref[16 * pair : 16 * pair + 16, :] = jnp.concatenate(both, axis=0).astype(BF16)
    fill_dft(dft_ref)

    pl.semaphore_wait(barrier, GROUPS - 1)
    to_members(blocks_out_ref, blocks_in_ref, 0)
    to_members(rows_out_ref, rows_in_ref, 1)

    all_of(blocks_out_ref, blocks_in_ref, 0, MEMBERS - 1).wait_recv()
    fill_truth(blocks_in_ref, truth_ref, truth_packed_ref)
    both = [wide_own_ref[84:92, :], truth_ref[...]]
    field_ref[112:128, :] = jnp.concatenate(both, axis=0).astype(BF16)

    for y_step in FAR_FIRST:
        block = lax.rem(y + y_step, 4)
        modes = lax.dot_general(
            dft_ref[pl.ds(pl.multiple_of(block * 192, 192), 192), :],
            field_ref[...],
            (((1,), (1,)), ((), ())),
            preferred_element_type=F32,
        )
        modes_out_ref[pl.ds(block * 32, 32)] = modes.reshape(32, ORDERS, 2, LANES).astype(BF16)
        to_groups(modes_out_ref, modes_in_ref, 2, y_step)
    modes_in_ref[mine] = modes_out_ref[mine]

    coef_copy.wait()
    fill_legendre(first, coef_ref, table_ref, legendre_ref)

    all_of(rows_out_ref, rows_in_ref, 1, MEMBERS - 1).wait_recv()
    grid_loss = grid_stage(ens, lat, rows_in_ref, truth_packed_ref, counts_out_ref)
    to_members(counts_out_ref, counts_in_ref, 3)

    all_of(modes_out_ref, modes_in_ref, 2, GROUPS - 1).wait_recv()
    spare, carries = spectral_stage(first, grid_loss, modes_in_ref, legendre_ref, wide_ref, lhs_ref)
    held = BANDS * PARTS
    for y_step in FAR_FIRST:
        block = lax.rem(y + y_step, 4)
        for part in range(4):
            member = block * 4 + part
            value = wide_ref[pl.ds(pl.multiple_of(member * held, held), held), :]
            value = jnp.where(carries, spare, value.reshape(BANDS, ORDERS, 2, LANES))
            back_out_ref[pl.ds(member * BANDS, BANDS)] = value.astype(BF16)
        to_groups(back_out_ref, back_in_ref, 4, y_step)
    back_in_ref[mine] = back_out_ref[mine]

    all_of(counts_out_ref, counts_in_ref, 3, MEMBERS - 1).wait_recv()
    all_of(back_out_ref, back_in_ref, 4, GROUPS - 1).wait_recv()
    total = jnp.zeros((2, LANES), F32)
    for block in range(16):
        total = total + jnp.sum(back_in_ref[8 * block : 8 * block + 8, 0].astype(F32), axis=0)
    row, column = iota((2, LANES), 0), iota((2, LANES), 1)
    total = jnp.where((row == 0) & (column >= LANES - 8) & (column < LANES - 5), total, 0.0)
    loss_ref[...] = jnp.sum(jnp.sum(total, axis=0, keepdims=True), axis=1, keepdims=True)

    all_of(blocks_out_ref, blocks_in_ref, 0, MEMBERS - 1).wait_send()
    all_of(rows_out_ref, rows_in_ref, 1, MEMBERS - 1).wait_send()
    all_of(modes_out_ref, modes_in_ref, 2, GROUPS - 1).wait_send()
    all_of(counts_out_ref, counts_in_ref, 3, MEMBERS - 1).wait_send()
    all_of(back_out_ref, back_in_ref, 4, GROUPS - 1).wait_send()


def exchange(own, target):
    rows = (MEMBERS, PACKED_TILES, 8, LANES)
    blocks = (MEMBERS, 8, LANES)
    modes = (GROUPS, ORDERS, 2, LANES)
    return pl.pallas_call(
        exchange_kernel,
        out_shape=(
            jax.ShapeDtypeStruct((SPECTRAL_ROWS, LON_PADDED), BF16),
            jax.ShapeDtypeStruct(modes, BF16),
            jax.ShapeDtypeStruct(rows, BF16),
            jax.ShapeDtypeStruct((1, 1), F32),
        ),
        in_specs=[pl.BlockSpec(memory_space=pltpu.HBM)] * 2,
        out_specs=tuple([pl.BlockSpec(memory_space=VMEM)] * 4),
        scratch_shapes=[
            VMEM((BAND_ROWS, AZIMUTH_STEPS), BF16),
            VMEM((BAND_ROWS, LON_BLOCK), BF16),
            VMEM((PACKED_ROWS, LANES), F32),
            VMEM((PACKED_ROWS, LANES), F32),
            VMEM((96, LON_PADDED), F32),
            VMEM(rows, BF16),
            VMEM(rows, BF16),
            VMEM(blocks, BF16),
            VMEM(blocks, BF16),
            VMEM((8, LON_PADDED), F32),
            VMEM((LANES, LON_PADDED), BF16),
            VMEM(modes, BF16),
            VMEM(modes, BF16),
            VMEM((16, DEGREE_CUTOFF), F32),
            pltpu.SMEM((16, DEGREE_CUTOFF), F32),
            VMEM((ORDERS * DEGREE_CUTOFF * 8, LANES), F32),
            VMEM((ORDERS, DEGREE_CUTOFF, BANDS * LANES), BF16),
            VMEM(rows, BF16),
            VMEM(modes, BF16),
            VMEM((SPECTRAL_ROWS, LANES), F32),
            VMEM((ORDERS, 48, BANDS * LANES), BF16),
            pltpu.SemaphoreType.DMA((5,)),
            pltpu.SemaphoreType.DMA((5,)),
            pltpu.SemaphoreType.DMA((3,)),
        ],
        compiler_params=params(collective_id=0, has_side_effects=True),
        cost_estimate=pl.CostEstimate(flops=800_000_000, bytes_accessed=8 << 20, transcendentals=0),
    )(own, target)


def final_kernel(table_ref, modes_ref, counts_ref, out_ref, packed_ref):
    row = iota((LANES, LANES), 0)
    line = BAND_ROWS * lax.axis_index("lat") + GROUP_ROWS * (row >> 3) + (row & 7)
    weight = cos_sin(line.astype(F32) + 0.5)[1] / (MEMBERS - 1)
    for group in range(ROW_GROUPS):
        packed_ref[PACKED_ROWS * group : PACKED_ROWS * (group + 1), :] = (
            counts_ref[group].astype(F32).reshape(PACKED_ROWS, LANES)
        )
    for chunk in range(LON_CHUNKS):
        lanes = slice(LANES * chunk, LANES * (chunk + 1))
        width = min(LANES, AZIMUTH_STEPS - LANES * chunk)
        wave = lax.dot_general(
            modes_ref[...],
            table_ref[:, lanes],
            (((0,), (0,)), ((), ())),
            preferred_element_type=F32,
        )
        for group in range(ROW_GROUPS):
            first = PACKED_ROWS * group + GROUP_ROWS * chunk
            rows = slice(8 * group, 8 * group + GROUP_ROWS)
            total = weight[rows] * packed_ref[first : first + GROUP_ROWS, :] + wave[rows]
            out_ref[
                GROUP_ROWS * group : GROUP_ROWS * (group + 1), 0, LANES * chunk : LANES * chunk + width
            ] = total[:, 0:width]


def final(table, modes, counts):
    return pl.pallas_call(
        final_kernel,
        out_shape=jax.ShapeDtypeStruct((BAND_ROWS, 1, AZIMUTH_STEPS), F32),
        in_specs=[pl.BlockSpec(memory_space=VMEM)] * 3,
        out_specs=pl.BlockSpec(memory_space=VMEM),
        scratch_shapes=[VMEM((ROW_GROUPS * PACKED_ROWS, LANES), F32)],
        compiler_params=params(),
        cost_estimate=pl.CostEstimate(flops=400_000_000, bytes_accessed=4 << 20, transcendentals=0),
    )(table, modes, counts)


def local(model_outputs, verifying_truth):
    table, back, counts, shared = exchange(pltpu.with_memory_space_constraint(model_outputs[0, 0], pltpu.HBM), pltpu.with_memory_space_constraint(verifying_truth[0], pltpu.HBM))
    other = lax.ppermute(shared, "chan", [(0, 1), (1, 0)])
    slope = final(table, back.reshape(SPECTRAL_ROWS, LANES), counts)
    return (slope.reshape(1, 1, BAND_ROWS, AZIMUTH_STEPS), (shared + other)[0, 0])


def solution(mesh):
    return jax.shard_map(
        local,
        mesh=mesh,
        in_specs=(P("ens", "chan", "lat", None), P("chan", "lat", "ens")),
        out_specs=(P("ens", "chan", "lat", None), P()),
        check_vma=False,
    )
```

```python
import functools
import math

import jax
import jax.numpy as jnp
from jax import lax
from jax.experimental import pallas as pl
from jax.experimental.pallas import tpu as pltpu
from jax.sharding import PartitionSpec as P

PARALLEL_LINES = 720
AZIMUTH_STEPS = 1440
DEGREE_CUTOFF = 384
SOFTENING_EPS = 0.25
SPECTRAL_WEIGHT = 0.1

MEMBERS = 16
BANDS = 8
GROUPS = MEMBERS * BANDS
ORDERS = DEGREE_CUTOFF // GROUPS
BAND_ROWS = PARALLEL_LINES // BANDS
LON_BLOCK = AZIMUTH_STEPS // MEMBERS
ROW_GROUPS = 15
GROUP_ROWS = 6
LANES = 128
LON_CHUNKS = 12
LON_PADDED = LON_CHUNKS * LANES
SPECTRAL_ROWS = 2 * DEGREE_CUTOFF
BLOCK = 16
DFT_BLOCK = 64
PACKED_ROWS = GROUP_ROWS * LON_CHUNKS
PACKED_TILES = PACKED_ROWS // 8
PARTS = 2 * ORDERS
FAR_FIRST = (2, 1, 3, 0)

VMEM = pltpu.VMEM
MESH = pl.DeviceIdType.MESH
F32 = jnp.float32
BF16 = jnp.bfloat16


def params(**kw):
    return pltpu.CompilerParams(vmem_limit_bytes=48 << 20, **kw)


def iota(shape, dim):
    return lax.broadcasted_iota(jnp.int32, shape, dim)


def cos_sin(steps):
    quarter = jnp.floor(steps * (1.0 / 360.0) + 0.5)
    rest = (steps - 360.0 * quarter) * (2.0 * math.pi / AZIMUTH_STEPS)
    quadrant = quarter - 4.0 * jnp.floor(quarter * 0.25)
    square = rest * rest
    sine = rest * (
        1.0
        + square
        * (-1.0 / 6.0 + square * (1.0 / 120.0 + square * (-1.0 / 5040.0 + square * (1.0 / 362880.0))))
    )
    cosine = 1.0 + square * (
        -0.5
        + square
        * (1.0 / 24.0 + square * (-1.0 / 720.0 + square * (1.0 / 40320.0 - square * (1.0 / 3628800.0))))
    )
    odd = (quadrant == 1.0) | (quadrant == 3.0)
    cos_part = jnp.where(odd, sine, cosine)
    sin_part = jnp.where(odd, cosine, sine)
    cos_part = jnp.where((quadrant == 1.0) | (quadrant == 2.0), -cos_part, cos_part)
    sin_part = jnp.where(quadrant >= 2.0, -sin_part, sin_part)
    return cos_part, sin_part


def fill_dft(out_ref):
    def body(block, carry):
        row = block * DFT_BLOCK + iota((DFT_BLOCK, LANES), 0)
        lane = iota((DFT_BLOCK, LANES), 1)
        order = (row >> 1).astype(F32)
        turn = (360 * (row & 1)).astype(F32)
        cosine, sine = cos_sin(order * lane.astype(F32) + turn)
        cos_step, sin_step = cos_sin(order * float(LANES))
        rows = pl.ds(pl.multiple_of(block * DFT_BLOCK, DFT_BLOCK), DFT_BLOCK)
        for chunk in range(LON_CHUNKS):
            value = cosine
            if chunk == LON_CHUNKS - 1:
                value = jnp.where(lane < AZIMUTH_STEPS - LANES * chunk, value, 0.0)
            out_ref[rows, LANES * chunk : LANES * (chunk + 1)] = value.astype(BF16)
            cosine, sine = (
                cosine * cos_step - sine * sin_step,
                sine * cos_step + cosine * sin_step,
            )
        return carry

    lax.fori_loop(0, SPECTRAL_ROWS // DFT_BLOCK, body, 0)


def fill_recurrence(first, out_ref):
    order = (first + iota((8, DEGREE_CUTOFF), 0)).astype(F32)
    degree = iota((8, DEGREE_CUTOFF), 1).astype(F32)
    growing = degree > order
    denominator = jnp.where(growing, degree * degree - order * order, 1.0)
    leading = jnp.sqrt(jnp.maximum(4.0 * degree * degree - 1.0, 0.0) / denominator)
    trailing = jnp.sqrt(
        jnp.maximum(
            ((degree - 1.0) * (degree - 1.0) - order * order)
            * (2.0 * degree + 1.0)
            / ((2.0 * degree - 3.0) * denominator),
            0.0,
        )
    )
    out_ref[0:8, :] = jnp.where(growing, leading, 0.0)
    out_ref[8:16, :] = jnp.where(growing, trailing, 0.0)


def seed_logs(first):
    order = (first + iota((8, DEGREE_CUTOFF), 0)).astype(F32)
    factor = (1 + iota((8, DEGREE_CUTOFF), 1)).astype(F32)
    summands = jnp.where(factor <= order, jnp.log(1.0 - 0.5 / factor), 0.0)
    return 0.5 * jnp.log(order[:, 0:1] + 0.5) + 0.5 * jnp.sum(summands, axis=1, keepdims=True)


def fill_legendre(first, coef_ref, table_ref, out_ref):
    band, lane = iota((8, LANES), 0), iota((8, LANES), 1)
    group, part = lane >> 3, lane & 7
    valid = (group < ROW_GROUPS) & (part < GROUP_ROWS)
    row = jnp.where(valid, BAND_ROWS * band + GROUP_ROWS * group + part, 0)
    cos_lat, sin_lat = cos_sin(row.astype(F32) + 0.5)
    weight = jnp.where(valid, math.pi / PARALLEL_LINES * sin_lat, 0.0)
    log_sin = jnp.log(sin_lat)
    seeds = seed_logs(first)

    def body(block, carry):
        state = list(carry)
        for step in range(BLOCK):
            degree = block * BLOCK + step
            for index in range(ORDERS):
                latest, before, log_scale, factor = state[4 * index : 4 * index + 4]
                leading = coef_ref[index, degree]
                trailing = coef_ref[8 + index, degree]
                begin = jnp.where(degree == first + index, 1.0, 0.0)
                advanced = (leading * cos_lat) * latest + (begin - trailing * before)
                row = (index * DEGREE_CUTOFF + degree) * 8
                table_ref[pl.ds(pl.multiple_of(row, 8), 8), :] = advanced * factor
                state[4 * index : 4 * index + 4] = [advanced, latest, log_scale, factor]
        for index in range(ORDERS):
            latest, before, log_scale, factor = state[4 * index : 4 * index + 4]
            largest = jnp.maximum(jnp.abs(latest), jnp.abs(before))
            largest = jnp.where(largest > 0.0, largest, 1.0)
            shrink = 1.0 / largest
            log_scale = log_scale + jnp.log(largest)
            state[4 * index : 4 * index + 4] = [
                latest * shrink,
                before * shrink,
                log_scale,
                jnp.exp(log_scale) * weight,
            ]
        return tuple(state)

    state = []
    for index in range(ORDERS):
        order = jnp.broadcast_to((first + index).astype(F32), (8, LANES))
        start = jnp.broadcast_to(seeds[index : index + 1, :], (8, LANES)) + order * log_sin
        state += [jnp.zeros((8, LANES), F32), jnp.zeros((8, LANES), F32), start, jnp.exp(start) * weight]
    lax.fori_loop(0, DEGREE_CUTOFF // BLOCK, body, tuple(state))
    for index in range(ORDERS):
        for band in range(BANDS):
            rows = table_ref[pl.ds(index * DEGREE_CUTOFF * 8 + band, DEGREE_CUTOFF, stride=8), :]
            out_ref[index, :, LANES * band : LANES * (band + 1)] = rows.astype(BF16)


def fill_truth(blocks_ref, out_ref, packed_ref):
    lane = iota((8, LANES), 1)
    chunks = [jnp.zeros((8, LANES), F32) for _ in range(LON_CHUNKS)]
    for block in range(MEMBERS):
        first = LON_BLOCK * block
        value = blocks_ref[block].astype(F32)
        shift = first % LANES
        if shift:
            value = pltpu.roll(value, shift, 1)
        for chunk in range(first // LANES, (first + LON_BLOCK - 1) // LANES + 1):
            place = lane + chunk * LANES
            inside = (place >= first) & (place < first + LON_BLOCK)
            chunks[chunk] = jnp.where(inside, value, chunks[chunk])
    for chunk in range(LON_CHUNKS):
        out_ref[:, LANES * chunk : LANES * (chunk + 1)] = chunks[chunk]
        packed_ref[GROUP_ROWS * chunk : GROUP_ROWS * (chunk + 1), :] = chunks[chunk][0:GROUP_ROWS]


def grid_stage(ens, lat, draws_ref, truth_ref, counts_ref):
    row, lane = iota((8, LANES), 0), iota((8, LANES), 1)

    def body(tile, total):
        place = 8 * tile + row
        chunk = (place * 43) >> 8
        part = place - GROUP_ROWS * chunk
        line = (BAND_ROWS * lat + GROUP_ROWS * ens + part).astype(F32)
        kept = (lane + chunk * LANES < AZIMUTH_STEPS) & (ens < ROW_GROUPS)
        weight = jnp.where(kept, cos_sin(line + 0.5)[1], 0.0)
        draws = [draws_ref[i, tile].astype(F32) for i in range(MEMBERS)]
        target = truth_ref[pl.ds(pl.multiple_of(8 * tile, 8), 8), :]
        counts = [None] * MEMBERS
        for i in range(MEMBERS):
            for k in range(i + 1, MEMBERS):
                above = jnp.where(draws[i] > draws[k], 1.0, 0.0)
                turn = jnp.where(draws[i] < draws[k], -1.0, above)
                counts[i] = turn if counts[i] is None else counts[i] + turn
                counts[k] = -turn if counts[k] is None else counts[k] - turn
        spread = jnp.zeros((8, LANES), F32)
        for i in range(MEMBERS):
            gap = draws[i] - target
            above = jnp.where(draws[i] > target, float(MEMBERS - 1), 0.0)
            side = jnp.where(draws[i] < target, -float(MEMBERS - 1), above)
            counts_ref[i, tile] = (side - counts[i]).astype(BF16)
            spread = spread + (jnp.abs(gap) - (draws[i] * counts[i]) * (1.0 / (MEMBERS - 1)))
        return total + jnp.where(kept, weight * spread, 0.0)

    return lax.fori_loop(0, PACKED_TILES, body, jnp.zeros((8, LANES), F32))


def spectral_stage(first, grid_loss, modes_ref, table_ref, wide_ref, lhs_ref, result_ref):
    draws = MEMBERS
    scale = SPECTRAL_WEIGHT * PARALLEL_LINES * AZIMUTH_STEPS / (DEGREE_CUTOFF * (DEGREE_CUTOFF + 1) / 2)
    held = BANDS * PARTS
    lane = iota((held, LANES), 1)
    target = jnp.zeros((held, LANES), F32)
    for member in range(draws):
        value = modes_ref[8 * member : 8 * member + 8].astype(F32).reshape(held, LANES)
        wide_ref[held * member : held * (member + 1), :] = value
        if member < ROW_GROUPS:
            moved = pltpu.roll(value, (8 * member + 8) % LANES, 1)
            target = jnp.where((lane >> 3) == member, moved, target)
    loss = jnp.zeros((1, DEGREE_CUTOFF), F32)
    degree = iota((1, DEGREE_CUTOFF), 1)
    pad = jnp.zeros((14, LANES), F32)
    for index in range(ORDERS):
        for band in range(BANDS):
            lanes = slice(LANES * band, LANES * (band + 1))
            parts = [
                wide_ref[pl.ds(PARTS * band + 2 * index + r, draws, stride=held), :] for r in range(2)
            ]
            aim = PARTS * band + 2 * index
            aims = [target[aim + r : aim + r + 1, :] for r in range(2)]
            lhs_ref[index, :, lanes] = jnp.concatenate(parts + aims + [pad], axis=0).astype(BF16)
    for index in range(ORDERS):
        terms = lax.dot_general(
            lhs_ref[index],
            table_ref[index],
            (((1,), (1,)), ((), ())),
            preferred_element_type=F32,
        )
        real, imag = terms[0:draws], terms[draws : 2 * draws]
        real_aim, imag_aim = terms[2 * draws : 2 * draws + 1], terms[2 * draws + 1 : 2 * draws + 2]
        gap_real, gap_imag = real - real_aim, imag - imag_aim
        square = gap_real * gap_real + gap_imag * gap_imag + SOFTENING_EPS**2
        inverse = lax.rsqrt(square)
        near = square * inverse
        step_real, step_imag = gap_real * inverse, gap_imag * inverse
        pair = jnp.zeros_like(real)
        pull_real, pull_imag = jnp.zeros_like(real), jnp.zeros_like(real)
        for other in range(draws):
            gap_real, gap_imag = real - real[other : other + 1], imag - imag[other : other + 1]
            square = gap_real * gap_real + gap_imag * gap_imag + SOFTENING_EPS**2
            inverse = lax.rsqrt(square)
            pair = pair + square * inverse
            pull_real = pull_real + gap_real * inverse
            pull_imag = pull_imag + gap_imag * inverse
        kept = degree >= first + index
        score = jnp.sum(near, axis=0, keepdims=True) - (
            jnp.sum(pair, axis=0, keepdims=True) - draws * SOFTENING_EPS
        ) / (2.0 * (draws - 1))
        loss = loss + jnp.where(kept, score, 0.0)
        down = jnp.concatenate(
            [step_real - pull_real / (draws - 1), step_imag - pull_imag / (draws - 1)], axis=0
        )
        grad = jnp.where(kept, scale * down, 0.0).astype(BF16)
        back = jnp.dot(grad, table_ref[index], preferred_element_type=F32)
        for band in range(BANDS):
            for r in range(2):
                result_ref[pl.ds(PARTS * band + 2 * index + r, draws, stride=held), :] = back[
                    draws * r : draws * (r + 1), LANES * band : LANES * (band + 1)
                ]
    local = jnp.sum(jnp.sum(grid_loss, axis=0, keepdims=True), axis=1, keepdims=True) / (
        PARALLEL_LINES * AZIMUTH_STEPS
    ) + SPECTRAL_WEIGHT / (DEGREE_CUTOFF * (DEGREE_CUTOFF + 1) / 2) * jnp.sum(loss, axis=1, keepdims=True)
    high = local.astype(BF16).astype(F32)
    middle = (local - high).astype(BF16).astype(F32)
    low = local - high - middle
    row = iota((BANDS, ORDERS, 2, LANES), 1) + iota((BANDS, ORDERS, 2, LANES), 2)
    column = iota((BANDS, ORDERS, 2, LANES), 3)
    high, middle, low = (v.reshape(1, 1, 1, 1) for v in (high, middle, low))
    spare = jnp.where(column == LANES - 8, high, jnp.where(column == LANES - 7, middle, low))
    carries = (row == 0) & (column >= LANES - 8) & (column < LANES - 5)
    return spare, carries


def exchange_kernel(
    own_hbm_ref,
    truth_hbm_ref,
    dft_ref,
    back_in_ref,
    base_ref,
    loss_ref,
    own_ref,
    truth_in_ref,
    packed_ref,
    truth_packed_ref,
    wide_own_ref,
    rows_out_ref,
    rows_in_ref,
    blocks_out_ref,
    blocks_in_ref,
    truth_ref,
    field_ref,
    modes_out_ref,
    modes_in_ref,
    coef_vector_ref,
    coef_ref,
    table_ref,
    legendre_ref,
    counts_out_ref,
    counts_in_ref,
    back_out_ref,
    wide_ref,
    lhs_ref,
    result_ref,
    send_sem,
    recv_sem,
    local_sem,
):
    chan, ens, lat = lax.axis_index("chan"), lax.axis_index("ens"), lax.axis_index("lat")
    mine = ens * BANDS + lat
    first = ORDERS * mine
    y, x = lax.div(ens, 4), lax.rem(lat, 4)
    z = lax.div(lat, 4) * 4 + lax.rem(ens, 4)
    truth_copy = pltpu.make_async_copy(truth_hbm_ref, truth_in_ref, local_sem.at[0])
    truth_copy.start()
    own_copy = pltpu.make_async_copy(own_hbm_ref, own_ref, local_sem.at[1])
    own_copy.start()

    barrier = pltpu.get_barrier_semaphore()

    def each_group(y_step, visit):
        peer_y = lax.rem(y + y_step, 4)

        def one(z_step, x_step):
            peer_z, peer_x = lax.rem(z + z_step, 8), lax.rem(x + x_step, 4)
            visit(peer_y * 4 + lax.rem(peer_z, 4), lax.div(peer_z, 4) * 4 + peer_x)

        def body(step, carry):
            z_step = 4 + lax.div(step + 1, 2) * (1 - 2 * lax.rem(step, 2))
            for x_step in FAR_FIRST:
                one(z_step, x_step)
            return carry

        lax.fori_loop(0, 8 if y_step else 7, body, 0)
        if y_step == 0:
            for x_step in FAR_FIRST[:3]:
                one(0, x_step)

    def greet(peer_ens, peer_lat):
        pl.semaphore_signal(
            barrier, inc=1, device_id=(chan, peer_ens, peer_lat), device_id_type=MESH
        )

    for y_step in FAR_FIRST:
        each_group(y_step, greet)

    def copy(source, target, kind, peer_ens, peer_lat):
        return pltpu.make_async_remote_copy(
            src_ref=source,
            dst_ref=target,
            send_sem=send_sem.at[kind],
            recv_sem=recv_sem.at[kind],
            device_id=(chan, peer_ens, peer_lat),
            device_id_type=MESH,
        )

    def to_members(source, target, kind):
        def body(step, carry):
            peer_y = lax.rem(y + FAR_FIRST[0] + lax.div(step, 4), 4)
            peer = peer_y * 4 + lax.rem(ens + 2 + step, 4)

            @pl.when(peer != ens)
            def _():
                copy(source.at[peer], target.at[ens], kind, peer, lat).start()

            return carry

        lax.fori_loop(0, MEMBERS, body, 0)
        target[ens] = source[ens]

    def to_groups(source, target, kind, y_step):
        def send(peer_ens, peer_lat):
            copy(
                source.at[peer_ens * BANDS + peer_lat], target.at[mine], kind, peer_ens, peer_lat
            ).start()

        each_group(y_step, send)

    def all_of(source, target, kind, count):
        return copy(source.at[pl.ds(0, count)], target.at[pl.ds(0, count)], kind, ens, lat)

    wide_own_ref[88:96, :] = jnp.zeros((8, LON_PADDED), F32)
    wide_own_ref[:, LON_PADDED - LANES :] = jnp.zeros((96, LANES), F32)
    truth_copy.wait()
    wide_own_ref[0:BAND_ROWS, 0:LON_BLOCK] = truth_in_ref[...].astype(F32)
    for group in range(ROW_GROUPS):
        blocks_out_ref[group] = wide_own_ref[GROUP_ROWS * group : GROUP_ROWS * group + 8, 0:LANES].astype(BF16)
    blocks_out_ref[ROW_GROUPS] = jnp.zeros((8, LANES), BF16)

    own_copy.wait()
    wide_own_ref[0:BAND_ROWS, 0:AZIMUTH_STEPS] = own_ref[...].astype(F32)
    for group in range(ROW_GROUPS):
        for chunk in range(LON_CHUNKS):
            packed_ref[GROUP_ROWS * chunk : GROUP_ROWS * (chunk + 1), :] = wide_own_ref[
                GROUP_ROWS * group : GROUP_ROWS * (group + 1), LANES * chunk : LANES * (chunk + 1)
            ]
        rows_out_ref[group] = packed_ref[...].reshape(PACKED_TILES, 8, LANES).astype(BF16)
    rows_out_ref[ROW_GROUPS] = jnp.zeros((PACKED_TILES, 8, LANES), BF16)

    fill_recurrence(first, coef_vector_ref)
    coef_copy = pltpu.make_async_copy(coef_vector_ref, coef_ref, local_sem.at[2])
    coef_copy.start()
    for pair in range(7):
        both = [
            wide_own_ref[GROUP_ROWS * group : GROUP_ROWS * group + 8, :] for group in (2 * pair, 2 * pair + 1)
        ]
        field_ref[16 * pair : 16 * pair + 16, :] = jnp.concatenate(both, axis=0).astype(BF16)
    fill_dft(dft_ref)

    pl.semaphore_wait(barrier, GROUPS - 1)
    to_members(blocks_out_ref, blocks_in_ref, 0)
    to_members(rows_out_ref, rows_in_ref, 1)

    all_of(blocks_out_ref, blocks_in_ref, 0, MEMBERS - 1).wait_recv()
    fill_truth(blocks_in_ref, truth_ref, truth_packed_ref)
    both = [wide_own_ref[84:92, :], truth_ref[...]]
    field_ref[112:128, :] = jnp.concatenate(both, axis=0).astype(BF16)

    for y_step in FAR_FIRST:
        block = lax.rem(y + y_step, 4)
        modes = lax.dot_general(
            dft_ref[pl.ds(pl.multiple_of(block * 192, 192), 192), :],
            field_ref[...],
            (((1,), (1,)), ((), ())),
            preferred_element_type=F32,
        )
        modes_out_ref[pl.ds(block * 32, 32)] = modes.reshape(32, ORDERS, 2, LANES).astype(BF16)
        to_groups(modes_out_ref, modes_in_ref, 2, y_step)
    modes_in_ref[mine] = modes_out_ref[mine]

    coef_copy.wait()
    fill_legendre(first, coef_ref, table_ref, legendre_ref)

    all_of(rows_out_ref, rows_in_ref, 1, MEMBERS - 1).wait_recv()
    grid_loss = grid_stage(ens, lat, rows_in_ref, truth_packed_ref, counts_out_ref)
    to_members(counts_out_ref, counts_in_ref, 3)

    all_of(modes_out_ref, modes_in_ref, 2, GROUPS - 1).wait_recv()
    spare, carries = spectral_stage(
        first, grid_loss, modes_in_ref, legendre_ref, wide_ref, lhs_ref, result_ref
    )
    held = BANDS * PARTS
    for y_step in FAR_FIRST:
        block = lax.rem(y + y_step, 4)
        for part in range(4):
            member = block * 4 + part
            value = result_ref[pl.ds(pl.multiple_of(member * held, held), held), :]
            value = jnp.where(carries, spare, value.reshape(BANDS, ORDERS, 2, LANES))
            back_out_ref[pl.ds(member * BANDS, BANDS)] = value.astype(BF16)
        to_groups(back_out_ref, back_in_ref, 4, y_step)
    back_in_ref[mine] = back_out_ref[mine]

    all_of(counts_out_ref, counts_in_ref, 3, MEMBERS - 1).wait_recv()
    for group in range(ROW_GROUPS):
        packed_ref[...] = counts_in_ref[group].astype(F32).reshape(PACKED_ROWS, LANES)
        line = BAND_ROWS * lat + GROUP_ROWS * group + iota((8, LANES), 0)
        weight = (cos_sin(line.astype(F32) + 0.5)[1] / (MEMBERS - 1))[0:GROUP_ROWS]
        for chunk in range(LON_CHUNKS):
            base_ref[8 * group : 8 * group + GROUP_ROWS, LANES * chunk : LANES * (chunk + 1)] = (
                weight * packed_ref[GROUP_ROWS * chunk : GROUP_ROWS * (chunk + 1), :]
            )
    all_of(back_out_ref, back_in_ref, 4, GROUPS - 1).wait_recv()
    total = jnp.zeros((2, LANES), F32)
    for block in range(16):
        total = total + jnp.sum(back_in_ref[8 * block : 8 * block + 8, 0].astype(F32), axis=0)
    row, column = iota((2, LANES), 0), iota((2, LANES), 1)
    total = jnp.where((row == 0) & (column >= LANES - 8) & (column < LANES - 5), total, 0.0)
    loss_ref[...] = jnp.sum(jnp.sum(total, axis=0, keepdims=True), axis=1, keepdims=True)

    all_of(blocks_out_ref, blocks_in_ref, 0, MEMBERS - 1).wait_send()
    all_of(rows_out_ref, rows_in_ref, 1, MEMBERS - 1).wait_send()
    all_of(modes_out_ref, modes_in_ref, 2, GROUPS - 1).wait_send()
    all_of(counts_out_ref, counts_in_ref, 3, MEMBERS - 1).wait_send()
    all_of(back_out_ref, back_in_ref, 4, GROUPS - 1).wait_send()


def exchange(own, target):
    rows = (MEMBERS, PACKED_TILES, 8, LANES)
    blocks = (MEMBERS, 8, LANES)
    modes = (GROUPS, ORDERS, 2, LANES)
    return pl.pallas_call(
        exchange_kernel,
        out_shape=(
            jax.ShapeDtypeStruct((SPECTRAL_ROWS, LON_PADDED), BF16),
            jax.ShapeDtypeStruct(modes, BF16),
            jax.ShapeDtypeStruct((LANES, LON_PADDED), F32),
            jax.ShapeDtypeStruct((1, 1), F32),
        ),
        in_specs=[pl.BlockSpec(memory_space=pltpu.HBM)] * 2,
        out_specs=tuple([pl.BlockSpec(memory_space=VMEM)] * 4),
        scratch_shapes=[
            VMEM((BAND_ROWS, AZIMUTH_STEPS), BF16),
            VMEM((BAND_ROWS, LON_BLOCK), BF16),
            VMEM((PACKED_ROWS, LANES), F32),
            VMEM((PACKED_ROWS, LANES), F32),
            VMEM((96, LON_PADDED), F32),
            VMEM(rows, BF16),
            VMEM(rows, BF16),
            VMEM(blocks, BF16),
            VMEM(blocks, BF16),
            VMEM((8, LON_PADDED), F32),
            VMEM((LANES, LON_PADDED), BF16),
            VMEM(modes, BF16),
            VMEM(modes, BF16),
            VMEM((16, DEGREE_CUTOFF), F32),
            pltpu.SMEM((16, DEGREE_CUTOFF), F32),
            VMEM((ORDERS * DEGREE_CUTOFF * 8, LANES), F32),
            VMEM((ORDERS, DEGREE_CUTOFF, BANDS * LANES), BF16),
            VMEM(rows, BF16),
            VMEM(rows, BF16),
            VMEM(modes, BF16),
            VMEM((SPECTRAL_ROWS, LANES), F32),
            VMEM((ORDERS, 48, BANDS * LANES), BF16),
            VMEM((SPECTRAL_ROWS, LANES), F32),
            pltpu.SemaphoreType.DMA((5,)),
            pltpu.SemaphoreType.DMA((5,)),
            pltpu.SemaphoreType.DMA((3,)),
        ],
        compiler_params=params(collective_id=0, has_side_effects=True),
        cost_estimate=pl.CostEstimate(flops=800_000_000, bytes_accessed=8 << 20, transcendentals=0),
    )(own, target)


def final_kernel(table_ref, modes_ref, base_ref, out_ref):
    for chunk in range(LON_CHUNKS):
        lanes = slice(LANES * chunk, LANES * (chunk + 1))
        width = min(LANES, AZIMUTH_STEPS - LANES * chunk)
        wave = lax.dot_general(
            modes_ref[...],
            table_ref[:, lanes],
            (((0,), (0,)), ((), ())),
            preferred_element_type=F32,
        )
        for group in range(ROW_GROUPS):
            rows = slice(8 * group, 8 * group + GROUP_ROWS)
            total = base_ref[rows, lanes] + wave[rows]
            out_ref[
                GROUP_ROWS * group : GROUP_ROWS * (group + 1), 0, LANES * chunk : LANES * chunk + width
            ] = total[:, 0:width]


def final(table, modes, base):
    return pl.pallas_call(
        final_kernel,
        out_shape=jax.ShapeDtypeStruct((BAND_ROWS, 1, AZIMUTH_STEPS), F32),
        in_specs=[pl.BlockSpec(memory_space=VMEM)] * 3,
        out_specs=pl.BlockSpec(memory_space=VMEM),
        compiler_params=params(),
        cost_estimate=pl.CostEstimate(flops=400_000_000, bytes_accessed=4 << 20, transcendentals=0),
    )(table, modes, base)


def local(model_outputs, verifying_truth):
    table, back, base, shared = exchange(pltpu.with_memory_space_constraint(model_outputs[0, 0], pltpu.HBM), pltpu.with_memory_space_constraint(verifying_truth[0], pltpu.HBM))
    other = lax.ppermute(shared, "chan", [(0, 1), (1, 0)])
    slope = final(table, back.reshape(SPECTRAL_ROWS, LANES), base)
    return (slope.reshape(1, 1, BAND_ROWS, AZIMUTH_STEPS), (shared + other)[0, 0])


def solution(mesh):
    return jax.shard_map(
        local,
        mesh=mesh,
        in_specs=(P("ens", "chan", "lat", None), P("chan", "lat", "ens")),
        out_specs=(P("ens", "chan", "lat", None), P()),
        check_vma=False,
    )
```

```python
import functools
import math

import jax
import jax.numpy as jnp
from jax import lax
from jax.experimental import pallas as pl
from jax.experimental.pallas import tpu as pltpu
from jax.sharding import PartitionSpec as P

PARALLEL_LINES = 720
AZIMUTH_STEPS = 1440
DEGREE_CUTOFF = 384
SOFTENING_EPS = 0.25
SPECTRAL_WEIGHT = 0.1

MEMBERS = 16
BANDS = 8
GROUPS = MEMBERS * BANDS
ORDERS = DEGREE_CUTOFF // GROUPS
BAND_ROWS = PARALLEL_LINES // BANDS
LON_BLOCK = AZIMUTH_STEPS // MEMBERS
ROW_GROUPS = 15
GROUP_ROWS = 6
LANES = 128
LON_CHUNKS = 12
LON_PADDED = LON_CHUNKS * LANES
SPECTRAL_ROWS = 2 * DEGREE_CUTOFF
BLOCK = 16
DFT_BLOCK = 64
PACKED_ROWS = GROUP_ROWS * LON_CHUNKS
PACKED_TILES = PACKED_ROWS // 8
PARTS = 2 * ORDERS
FAR_FIRST = (2, 1, 3, 0)

VMEM = pltpu.VMEM
MESH = pl.DeviceIdType.MESH
F32 = jnp.float32
BF16 = jnp.bfloat16


def params(**kw):
    return pltpu.CompilerParams(vmem_limit_bytes=48 << 20, **kw)


def iota(shape, dim):
    return lax.broadcasted_iota(jnp.int32, shape, dim)


def cos_sin(steps):
    quarter = jnp.floor(steps * (1.0 / 360.0) + 0.5)
    rest = (steps - 360.0 * quarter) * (2.0 * math.pi / AZIMUTH_STEPS)
    quadrant = quarter - 4.0 * jnp.floor(quarter * 0.25)
    square = rest * rest
    sine = rest * (
        1.0
        + square
        * (-1.0 / 6.0 + square * (1.0 / 120.0 + square * (-1.0 / 5040.0 + square * (1.0 / 362880.0))))
    )
    cosine = 1.0 + square * (
        -0.5
        + square
        * (1.0 / 24.0 + square * (-1.0 / 720.0 + square * (1.0 / 40320.0 - square * (1.0 / 3628800.0))))
    )
    odd = (quadrant == 1.0) | (quadrant == 3.0)
    cos_part = jnp.where(odd, sine, cosine)
    sin_part = jnp.where(odd, cosine, sine)
    cos_part = jnp.where((quadrant == 1.0) | (quadrant == 2.0), -cos_part, cos_part)
    sin_part = jnp.where(quadrant >= 2.0, -sin_part, sin_part)
    return cos_part, sin_part


def fill_dft(out_ref):
    def body(block, carry):
        row = block * DFT_BLOCK + iota((DFT_BLOCK, LANES), 0)
        lane = iota((DFT_BLOCK, LANES), 1)
        order = (row >> 1).astype(F32)
        turn = (360 * (row & 1)).astype(F32)
        cosine, sine = cos_sin(order * lane.astype(F32) + turn)
        cos_step, sin_step = cos_sin(order * float(LANES))
        rows = pl.ds(pl.multiple_of(block * DFT_BLOCK, DFT_BLOCK), DFT_BLOCK)
        for chunk in range(LON_CHUNKS):
            value = cosine
            if chunk == LON_CHUNKS - 1:
                value = jnp.where(lane < AZIMUTH_STEPS - LANES * chunk, value, 0.0)
            out_ref[rows, LANES * chunk : LANES * (chunk + 1)] = value.astype(BF16)
            cosine, sine = (
                cosine * cos_step - sine * sin_step,
                sine * cos_step + cosine * sin_step,
            )
        return carry

    lax.fori_loop(0, SPECTRAL_ROWS // DFT_BLOCK, body, 0)


def fill_recurrence(first, out_ref):
    order = (first + iota((8, DEGREE_CUTOFF), 0)).astype(F32)
    degree = iota((8, DEGREE_CUTOFF), 1).astype(F32)
    growing = degree > order
    denominator = jnp.where(growing, degree * degree - order * order, 1.0)
    leading = jnp.sqrt(jnp.maximum(4.0 * degree * degree - 1.0, 0.0) / denominator)
    trailing = jnp.sqrt(
        jnp.maximum(
            ((degree - 1.0) * (degree - 1.0) - order * order)
            * (2.0 * degree + 1.0)
            / ((2.0 * degree - 3.0) * denominator),
            0.0,
        )
    )
    out_ref[0:8, :] = jnp.where(growing, leading, 0.0)
    out_ref[8:16, :] = jnp.where(growing, trailing, 0.0)


def seed_logs(first):
    order = (first + iota((8, DEGREE_CUTOFF), 0)).astype(F32)
    factor = (1 + iota((8, DEGREE_CUTOFF), 1)).astype(F32)
    summands = jnp.where(factor <= order, jnp.log(1.0 - 0.5 / factor), 0.0)
    return 0.5 * jnp.log(order[:, 0:1] + 0.5) + 0.5 * jnp.sum(summands, axis=1, keepdims=True)


def legendre_recurrence(first, coef_ref, table_ref):
    band, lane = iota((8, LANES), 0), iota((8, LANES), 1)
    group, part = lane >> 3, lane & 7
    valid = (group < ROW_GROUPS) & (part < GROUP_ROWS)
    row = jnp.where(valid, BAND_ROWS * band + GROUP_ROWS * group + part, 0)
    cos_lat, sin_lat = cos_sin(row.astype(F32) + 0.5)
    weight = jnp.where(valid, math.pi / PARALLEL_LINES * sin_lat, 0.0)
    log_sin = jnp.log(sin_lat)
    seeds = seed_logs(first)

    def body(block, carry):
        state = list(carry)
        for step in range(BLOCK):
            degree = block * BLOCK + step
            for index in range(ORDERS):
                latest, before, log_scale, factor = state[4 * index : 4 * index + 4]
                leading = coef_ref[index, degree]
                trailing = coef_ref[8 + index, degree]
                begin = jnp.where(degree == first + index, 1.0, 0.0)
                advanced = (leading * cos_lat) * latest + (begin - trailing * before)
                row = (index * DEGREE_CUTOFF + degree) * 8
                table_ref[pl.ds(pl.multiple_of(row, 8), 8), :] = advanced * factor
                state[4 * index : 4 * index + 4] = [advanced, latest, log_scale, factor]
        for index in range(ORDERS):
            latest, before, log_scale, factor = state[4 * index : 4 * index + 4]
            largest = jnp.maximum(jnp.abs(latest), jnp.abs(before))
            largest = jnp.where(largest > 0.0, largest, 1.0)
            shrink = 1.0 / largest
            log_scale = log_scale + jnp.log(largest)
            state[4 * index : 4 * index + 4] = [
                latest * shrink,
                before * shrink,
                log_scale,
                jnp.exp(log_scale) * weight,
            ]
        return tuple(state)

    state = []
    for index in range(ORDERS):
        order = jnp.broadcast_to((first + index).astype(F32), (8, LANES))
        start = jnp.broadcast_to(seeds[index : index + 1, :], (8, LANES)) + order * log_sin
        state += [jnp.zeros((8, LANES), F32), jnp.zeros((8, LANES), F32), start, jnp.exp(start) * weight]
    lax.fori_loop(0, DEGREE_CUTOFF // BLOCK, body, tuple(state))


def fill_legendre(table_ref, out_ref):
    for index in range(ORDERS):
        for band in range(BANDS):
            rows = table_ref[pl.ds(index * DEGREE_CUTOFF * 8 + band, DEGREE_CUTOFF, stride=8), :]
            out_ref[index, :, LANES * band : LANES * (band + 1)] = rows.astype(BF16)


def fill_truth(blocks_ref, out_ref, packed_ref):
    lane = iota((8, LANES), 1)
    chunks = [jnp.zeros((8, LANES), F32) for _ in range(LON_CHUNKS)]
    for block in range(MEMBERS):
        first = LON_BLOCK * block
        value = blocks_ref[block].astype(F32)
        shift = first % LANES
        if shift:
            value = pltpu.roll(value, shift, 1)
        for chunk in range(first // LANES, (first + LON_BLOCK - 1) // LANES + 1):
            place = lane + chunk * LANES
            inside = (place >= first) & (place < first + LON_BLOCK)
            chunks[chunk] = jnp.where(inside, value, chunks[chunk])
    for chunk in range(LON_CHUNKS):
        out_ref[:, LANES * chunk : LANES * (chunk + 1)] = chunks[chunk]
        packed_ref[GROUP_ROWS * chunk : GROUP_ROWS * (chunk + 1), :] = chunks[chunk][0:GROUP_ROWS]


def grid_stage(ens, lat, draws_ref, truth_ref, counts_ref):
    row, lane = iota((8, LANES), 0), iota((8, LANES), 1)

    def body(tile, total):
        place = 8 * tile + row
        chunk = (place * 43) >> 8
        part = place - GROUP_ROWS * chunk
        line = (BAND_ROWS * lat + GROUP_ROWS * ens + part).astype(F32)
        kept = (lane + chunk * LANES < AZIMUTH_STEPS) & (ens < ROW_GROUPS)
        weight = jnp.where(kept, cos_sin(line + 0.5)[1], 0.0)
        draws = [draws_ref[i, tile].astype(F32) for i in range(MEMBERS)]
        target = truth_ref[pl.ds(pl.multiple_of(8 * tile, 8), 8), :]
        counts = [None] * MEMBERS
        for i in range(MEMBERS):
            for k in range(i + 1, MEMBERS):
                above = jnp.where(draws[i] > draws[k], 1.0, 0.0)
                turn = jnp.where(draws[i] < draws[k], -1.0, above)
                counts[i] = turn if counts[i] is None else counts[i] + turn
                counts[k] = -turn if counts[k] is None else counts[k] - turn
        spread = jnp.zeros((8, LANES), F32)
        for i in range(MEMBERS):
            gap = draws[i] - target
            above = jnp.where(draws[i] > target, float(MEMBERS - 1), 0.0)
            side = jnp.where(draws[i] < target, -float(MEMBERS - 1), above)
            counts_ref[i, tile] = (side - counts[i]).astype(BF16)
            spread = spread + (jnp.abs(gap) - (draws[i] * counts[i]) * (1.0 / (MEMBERS - 1)))
        return total + jnp.where(kept, weight * spread, 0.0)

    return lax.fori_loop(0, PACKED_TILES, body, jnp.zeros((8, LANES), F32))


def spectral_stage(first, grid_loss, modes_ref, table_ref, wide_ref, lhs_ref, result_ref):
    draws = MEMBERS
    scale = SPECTRAL_WEIGHT * PARALLEL_LINES * AZIMUTH_STEPS / (DEGREE_CUTOFF * (DEGREE_CUTOFF + 1) / 2)
    held = BANDS * PARTS
    lane = iota((held, LANES), 1)
    target = jnp.zeros((held, LANES), F32)
    for member in range(draws):
        value = modes_ref[8 * member : 8 * member + 8].astype(F32).reshape(held, LANES)
        wide_ref[held * member : held * (member + 1), :] = value
        if member < ROW_GROUPS:
            moved = pltpu.roll(value, (8 * member + 8) % LANES, 1)
            target = jnp.where((lane >> 3) == member, moved, target)
    loss = jnp.zeros((1, DEGREE_CUTOFF), F32)
    degree = iota((1, DEGREE_CUTOFF), 1)
    pad = jnp.zeros((14, LANES), F32)
    for index in range(ORDERS):
        for band in range(BANDS):
            lanes = slice(LANES * band, LANES * (band + 1))
            parts = [
                wide_ref[pl.ds(PARTS * band + 2 * index + r, draws, stride=held), :] for r in range(2)
            ]
            aim = PARTS * band + 2 * index
            aims = [target[aim + r : aim + r + 1, :] for r in range(2)]
            lhs_ref[index, :, lanes] = jnp.concatenate(parts + aims + [pad], axis=0).astype(BF16)
    for index in range(ORDERS):
        terms = lax.dot_general(
            lhs_ref[index],
            table_ref[index],
            (((1,), (1,)), ((), ())),
            preferred_element_type=F32,
        )
        real, imag = terms[0:draws], terms[draws : 2 * draws]
        real_aim, imag_aim = terms[2 * draws : 2 * draws + 1], terms[2 * draws + 1 : 2 * draws + 2]
        gap_real, gap_imag = real - real_aim, imag - imag_aim
        square = gap_real * gap_real + gap_imag * gap_imag + SOFTENING_EPS**2
        inverse = lax.rsqrt(square)
        near = square * inverse
        step_real, step_imag = gap_real * inverse, gap_imag * inverse
        pair = jnp.zeros_like(real)
        pull_real, pull_imag = jnp.zeros_like(real), jnp.zeros_like(real)
        for other in range(draws):
            gap_real, gap_imag = real - real[other : other + 1], imag - imag[other : other + 1]
            square = gap_real * gap_real + gap_imag * gap_imag + SOFTENING_EPS**2
            inverse = lax.rsqrt(square)
            pair = pair + square * inverse
            pull_real = pull_real + gap_real * inverse
            pull_imag = pull_imag + gap_imag * inverse
        kept = degree >= first + index
        score = jnp.sum(near, axis=0, keepdims=True) - (
            jnp.sum(pair, axis=0, keepdims=True) - draws * SOFTENING_EPS
        ) / (2.0 * (draws - 1))
        loss = loss + jnp.where(kept, score, 0.0)
        down = jnp.concatenate(
            [step_real - pull_real / (draws - 1), step_imag - pull_imag / (draws - 1)], axis=0
        )
        grad = jnp.where(kept, scale * down, 0.0).astype(BF16)
        back = jnp.dot(grad, table_ref[index], preferred_element_type=F32)
        for band in range(BANDS):
            for r in range(2):
                result_ref[pl.ds(PARTS * band + 2 * index + r, draws, stride=held), :] = back[
                    draws * r : draws * (r + 1), LANES * band : LANES * (band + 1)
                ]
    local = jnp.sum(jnp.sum(grid_loss, axis=0, keepdims=True), axis=1, keepdims=True) / (
        PARALLEL_LINES * AZIMUTH_STEPS
    ) + SPECTRAL_WEIGHT / (DEGREE_CUTOFF * (DEGREE_CUTOFF + 1) / 2) * jnp.sum(loss, axis=1, keepdims=True)
    high = local.astype(BF16).astype(F32)
    middle = (local - high).astype(BF16).astype(F32)
    low = local - high - middle
    row = iota((BANDS, ORDERS, 2, LANES), 1) + iota((BANDS, ORDERS, 2, LANES), 2)
    column = iota((BANDS, ORDERS, 2, LANES), 3)
    high, middle, low = (v.reshape(1, 1, 1, 1) for v in (high, middle, low))
    spare = jnp.where(column == LANES - 8, high, jnp.where(column == LANES - 7, middle, low))
    carries = (row == 0) & (column >= LANES - 8) & (column < LANES - 5)
    return spare, carries


def exchange_kernel(
    own_hbm_ref,
    truth_hbm_ref,
    dft_ref,
    back_in_ref,
    base_ref,
    loss_ref,
    own_ref,
    truth_in_ref,
    packed_ref,
    truth_packed_ref,
    wide_own_ref,
    rows_out_ref,
    rows_in_ref,
    blocks_out_ref,
    blocks_in_ref,
    truth_ref,
    field_ref,
    modes_out_ref,
    modes_in_ref,
    coef_vector_ref,
    coef_ref,
    table_ref,
    legendre_ref,
    counts_out_ref,
    counts_in_ref,
    back_out_ref,
    wide_ref,
    lhs_ref,
    result_ref,
    send_sem,
    recv_sem,
    local_sem,
):
    chan, ens, lat = lax.axis_index("chan"), lax.axis_index("ens"), lax.axis_index("lat")
    mine = ens * BANDS + lat
    first = ORDERS * mine
    y, x = lax.div(ens, 4), lax.rem(lat, 4)
    z = lax.div(lat, 4) * 4 + lax.rem(ens, 4)
    truth_copy = pltpu.make_async_copy(truth_hbm_ref, truth_in_ref, local_sem.at[0])
    truth_copy.start()
    own_copy = pltpu.make_async_copy(own_hbm_ref, own_ref, local_sem.at[1])
    own_copy.start()

    barrier = pltpu.get_barrier_semaphore()

    def each_group(y_step, visit):
        peer_y = lax.rem(y + y_step, 4)

        def one(z_step, x_step):
            peer_z, peer_x = lax.rem(z + z_step, 8), lax.rem(x + x_step, 4)
            visit(peer_y * 4 + lax.rem(peer_z, 4), lax.div(peer_z, 4) * 4 + peer_x)

        def body(step, carry):
            z_step = 4 + lax.div(step + 1, 2) * (1 - 2 * lax.rem(step, 2))
            for x_step in FAR_FIRST:
                one(z_step, x_step)
            return carry

        lax.fori_loop(0, 8 if y_step else 7, body, 0)
        if y_step == 0:
            for x_step in FAR_FIRST[:3]:
                one(0, x_step)

    def greet(peer_ens, peer_lat):
        pl.semaphore_signal(
            barrier, inc=1, device_id=(chan, peer_ens, peer_lat), device_id_type=MESH
        )

    for y_step in FAR_FIRST:
        each_group(y_step, greet)

    def copy(source, target, kind, peer_ens, peer_lat):
        return pltpu.make_async_remote_copy(
            src_ref=source,
            dst_ref=target,
            send_sem=send_sem.at[kind],
            recv_sem=recv_sem.at[kind],
            device_id=(chan, peer_ens, peer_lat),
            device_id_type=MESH,
        )

    def to_members(source, target, kind):
        def body(step, carry):
            peer_y = lax.rem(y + FAR_FIRST[0] + lax.div(step, 4), 4)
            peer = peer_y * 4 + lax.rem(ens + 2 + step, 4)

            @pl.when(peer != ens)
            def _():
                copy(source.at[peer], target.at[ens], kind, peer, lat).start()

            return carry

        lax.fori_loop(0, MEMBERS, body, 0)
        target[ens] = source[ens]

    def to_groups(source, target, kind, y_step):
        def send(peer_ens, peer_lat):
            copy(
                source.at[peer_ens * BANDS + peer_lat], target.at[mine], kind, peer_ens, peer_lat
            ).start()

        each_group(y_step, send)

    def all_of(source, target, kind, count):
        return copy(source.at[pl.ds(0, count)], target.at[pl.ds(0, count)], kind, ens, lat)

    wide_own_ref[88:96, :] = jnp.zeros((8, LON_PADDED), F32)
    wide_own_ref[:, LON_PADDED - LANES :] = jnp.zeros((96, LANES), F32)
    truth_copy.wait()
    wide_own_ref[0:BAND_ROWS, 0:LON_BLOCK] = truth_in_ref[...].astype(F32)
    for group in range(ROW_GROUPS):
        blocks_out_ref[group] = wide_own_ref[GROUP_ROWS * group : GROUP_ROWS * group + 8, 0:LANES].astype(BF16)
    blocks_out_ref[ROW_GROUPS] = jnp.zeros((8, LANES), BF16)

    own_copy.wait()
    wide_own_ref[0:BAND_ROWS, 0:AZIMUTH_STEPS] = own_ref[...].astype(F32)
    for group in range(ROW_GROUPS):
        for chunk in range(LON_CHUNKS):
            packed_ref[GROUP_ROWS * chunk : GROUP_ROWS * (chunk + 1), :] = wide_own_ref[
                GROUP_ROWS * group : GROUP_ROWS * (group + 1), LANES * chunk : LANES * (chunk + 1)
            ]
        rows_out_ref[group] = packed_ref[...].reshape(PACKED_TILES, 8, LANES).astype(BF16)
    rows_out_ref[ROW_GROUPS] = jnp.zeros((PACKED_TILES, 8, LANES), BF16)

    pl.semaphore_wait(barrier, GROUPS - 1)
    to_members(blocks_out_ref, blocks_in_ref, 0)
    to_members(rows_out_ref, rows_in_ref, 1)
    fill_recurrence(first, coef_vector_ref)
    coef_copy = pltpu.make_async_copy(coef_vector_ref, coef_ref, local_sem.at[2])
    coef_copy.start()
    for pair in range(7):
        both = [
            wide_own_ref[GROUP_ROWS * group : GROUP_ROWS * group + 8, :] for group in (2 * pair, 2 * pair + 1)
        ]
        field_ref[16 * pair : 16 * pair + 16, :] = jnp.concatenate(both, axis=0).astype(BF16)
    fill_dft(dft_ref)

    all_of(blocks_out_ref, blocks_in_ref, 0, MEMBERS - 1).wait_recv()
    fill_truth(blocks_in_ref, truth_ref, truth_packed_ref)
    both = [wide_own_ref[84:92, :], truth_ref[...]]
    field_ref[112:128, :] = jnp.concatenate(both, axis=0).astype(BF16)

    for y_step in FAR_FIRST:
        block = lax.rem(y + y_step, 4)
        modes = lax.dot_general(
            dft_ref[pl.ds(pl.multiple_of(block * 192, 192), 192), :],
            field_ref[...],
            (((1,), (1,)), ((), ())),
            preferred_element_type=F32,
        )
        modes_out_ref[pl.ds(block * 32, 32)] = modes.reshape(32, ORDERS, 2, LANES).astype(BF16)
        to_groups(modes_out_ref, modes_in_ref, 2, y_step)
    modes_in_ref[mine] = modes_out_ref[mine]

    coef_copy.wait()
    legendre_recurrence(first, coef_ref, table_ref)
    fill_legendre(table_ref, legendre_ref)

    all_of(rows_out_ref, rows_in_ref, 1, MEMBERS - 1).wait_recv()
    grid_loss = grid_stage(ens, lat, rows_in_ref, truth_packed_ref, counts_out_ref)
    to_members(counts_out_ref, counts_in_ref, 3)

    all_of(modes_out_ref, modes_in_ref, 2, GROUPS - 1).wait_recv()
    spare, carries = spectral_stage(
        first, grid_loss, modes_in_ref, legendre_ref, wide_ref, lhs_ref, result_ref
    )
    held = BANDS * PARTS
    for y_step in FAR_FIRST:
        block = lax.rem(y + y_step, 4)
        for part in range(4):
            member = block * 4 + part
            value = result_ref[pl.ds(pl.multiple_of(member * held, held), held), :]
            value = jnp.where(carries, spare, value.reshape(BANDS, ORDERS, 2, LANES))
            back_out_ref[pl.ds(member * BANDS, BANDS)] = value.astype(BF16)
        to_groups(back_out_ref, back_in_ref, 4, y_step)
    back_in_ref[mine] = back_out_ref[mine]

    all_of(counts_out_ref, counts_in_ref, 3, MEMBERS - 1).wait_recv()
    for group in range(ROW_GROUPS):
        packed_ref[...] = counts_in_ref[group].astype(F32).reshape(PACKED_ROWS, LANES)
        line = BAND_ROWS * lat + GROUP_ROWS * group + iota((8, LANES), 0)
        weight = (cos_sin(line.astype(F32) + 0.5)[1] / (MEMBERS - 1))[0:GROUP_ROWS]
        for chunk in range(LON_CHUNKS):
            base_ref[8 * group : 8 * group + GROUP_ROWS, LANES * chunk : LANES * (chunk + 1)] = (
                weight * packed_ref[GROUP_ROWS * chunk : GROUP_ROWS * (chunk + 1), :]
            )
    all_of(back_out_ref, back_in_ref, 4, GROUPS - 1).wait_recv()
    total = jnp.zeros((2, LANES), F32)
    for block in range(16):
        total = total + jnp.sum(back_in_ref[8 * block : 8 * block + 8, 0].astype(F32), axis=0)
    row, column = iota((2, LANES), 0), iota((2, LANES), 1)
    total = jnp.where((row == 0) & (column >= LANES - 8) & (column < LANES - 5), total, 0.0)
    loss_ref[...] = jnp.sum(jnp.sum(total, axis=0, keepdims=True), axis=1, keepdims=True)

    all_of(blocks_out_ref, blocks_in_ref, 0, MEMBERS - 1).wait_send()
    all_of(rows_out_ref, rows_in_ref, 1, MEMBERS - 1).wait_send()
    all_of(modes_out_ref, modes_in_ref, 2, GROUPS - 1).wait_send()
    all_of(counts_out_ref, counts_in_ref, 3, MEMBERS - 1).wait_send()
    all_of(back_out_ref, back_in_ref, 4, GROUPS - 1).wait_send()


def exchange(own, target):
    rows = (MEMBERS, PACKED_TILES, 8, LANES)
    blocks = (MEMBERS, 8, LANES)
    modes = (GROUPS, ORDERS, 2, LANES)
    return pl.pallas_call(
        exchange_kernel,
        out_shape=(
            jax.ShapeDtypeStruct((SPECTRAL_ROWS, LON_PADDED), BF16),
            jax.ShapeDtypeStruct(modes, BF16),
            jax.ShapeDtypeStruct((LANES, LON_PADDED), F32),
            jax.ShapeDtypeStruct((1, 1), F32),
        ),
        in_specs=[pl.BlockSpec(memory_space=pltpu.HBM)] * 2,
        out_specs=tuple([pl.BlockSpec(memory_space=VMEM)] * 4),
        scratch_shapes=[
            VMEM((BAND_ROWS, AZIMUTH_STEPS), BF16),
            VMEM((BAND_ROWS, LON_BLOCK), BF16),
            VMEM((PACKED_ROWS, LANES), F32),
            VMEM((PACKED_ROWS, LANES), F32),
            VMEM((96, LON_PADDED), F32),
            VMEM(rows, BF16),
            VMEM(rows, BF16),
            VMEM(blocks, BF16),
            VMEM(blocks, BF16),
            VMEM((8, LON_PADDED), F32),
            VMEM((LANES, LON_PADDED), BF16),
            VMEM(modes, BF16),
            VMEM(modes, BF16),
            VMEM((16, DEGREE_CUTOFF), F32),
            pltpu.SMEM((16, DEGREE_CUTOFF), F32),
            VMEM((ORDERS * DEGREE_CUTOFF * 8, LANES), F32),
            VMEM((ORDERS, DEGREE_CUTOFF, BANDS * LANES), BF16),
            VMEM(rows, BF16),
            VMEM(rows, BF16),
            VMEM(modes, BF16),
            VMEM((SPECTRAL_ROWS, LANES), F32),
            VMEM((ORDERS, 48, BANDS * LANES), BF16),
            VMEM((SPECTRAL_ROWS, LANES), F32),
            pltpu.SemaphoreType.DMA((5,)),
            pltpu.SemaphoreType.DMA((5,)),
            pltpu.SemaphoreType.DMA((3,)),
        ],
        compiler_params=params(collective_id=0, has_side_effects=True),
        cost_estimate=pl.CostEstimate(flops=800_000_000, bytes_accessed=8 << 20, transcendentals=0),
    )(own, target)


def final_kernel(table_ref, modes_ref, base_ref, out_ref):
    modes = modes_ref[...].astype(F32).T.astype(BF16)
    for chunk in range(LON_CHUNKS // 2):
        first = 2 * LANES * chunk
        lanes = slice(first, first + 2 * LANES)
        width = min(2 * LANES, AZIMUTH_STEPS - first)
        wave = jnp.dot(modes, table_ref[:, lanes], preferred_element_type=F32)
        for group in range(ROW_GROUPS):
            rows = slice(8 * group, 8 * group + GROUP_ROWS)
            total = base_ref[rows, lanes] + wave[rows]
            out_ref[GROUP_ROWS * group : GROUP_ROWS * (group + 1), 0, first : first + width] = total[
                :, 0:width
            ]


def final(table, modes, base):
    return pl.pallas_call(
        final_kernel,
        out_shape=jax.ShapeDtypeStruct((BAND_ROWS, 1, AZIMUTH_STEPS), F32),
        in_specs=[pl.BlockSpec(memory_space=VMEM)] * 3,
        out_specs=pl.BlockSpec(memory_space=VMEM),
        compiler_params=params(),
        cost_estimate=pl.CostEstimate(flops=400_000_000, bytes_accessed=4 << 20, transcendentals=0),
    )(table, modes, base)


def local(model_outputs, verifying_truth):
    table, back, base, shared = exchange(pltpu.with_memory_space_constraint(model_outputs[0, 0], pltpu.HBM), pltpu.with_memory_space_constraint(verifying_truth[0], pltpu.HBM))
    other = lax.ppermute(shared, "chan", [(0, 1), (1, 0)])
    slope = final(table, back.reshape(SPECTRAL_ROWS, LANES), base)
    return (slope.reshape(1, 1, BAND_ROWS, AZIMUTH_STEPS), (shared + other)[0, 0])


def solution(mesh):
    return jax.shard_map(
        local,
        mesh=mesh,
        in_specs=(P("ens", "chan", "lat", None), P("chan", "lat", "ens")),
        out_specs=(P("ens", "chan", "lat", None), P()),
        check_vma=False,
    )
```

```python
import functools
import math

import jax
import jax.numpy as jnp
from jax import lax
from jax.experimental import pallas as pl
from jax.experimental.pallas import tpu as pltpu
from jax.sharding import PartitionSpec as P

PARALLEL_LINES = 720
AZIMUTH_STEPS = 1440
DEGREE_CUTOFF = 384
SOFTENING_EPS = 0.25
SPECTRAL_WEIGHT = 0.1

MEMBERS = 16
BANDS = 8
GROUPS = MEMBERS * BANDS
ORDERS = DEGREE_CUTOFF // GROUPS
BAND_ROWS = PARALLEL_LINES // BANDS
LON_BLOCK = AZIMUTH_STEPS // MEMBERS
ROW_GROUPS = 15
GROUP_ROWS = 6
LANES = 128
LON_CHUNKS = 12
LON_PADDED = LON_CHUNKS * LANES
SPECTRAL_ROWS = 2 * DEGREE_CUTOFF
BLOCK = 16
DFT_BLOCK = 64
PACKED_ROWS = GROUP_ROWS * LON_CHUNKS
PACKED_TILES = PACKED_ROWS // 8
PARTS = 2 * ORDERS
FAR_FIRST = (2, 1, 3, 0)

VMEM = pltpu.VMEM
MESH = pl.DeviceIdType.MESH
F32 = jnp.float32
BF16 = jnp.bfloat16


def params(**kw):
    return pltpu.CompilerParams(vmem_limit_bytes=48 << 20, **kw)


def iota(shape, dim):
    return lax.broadcasted_iota(jnp.int32, shape, dim)


def cos_sin(steps):
    quarter = jnp.floor(steps * (1.0 / 360.0) + 0.5)
    rest = (steps - 360.0 * quarter) * (2.0 * math.pi / AZIMUTH_STEPS)
    quadrant = quarter - 4.0 * jnp.floor(quarter * 0.25)
    square = rest * rest
    sine = rest * (
        1.0
        + square
        * (-1.0 / 6.0 + square * (1.0 / 120.0 + square * (-1.0 / 5040.0 + square * (1.0 / 362880.0))))
    )
    cosine = 1.0 + square * (
        -0.5
        + square
        * (1.0 / 24.0 + square * (-1.0 / 720.0 + square * (1.0 / 40320.0 - square * (1.0 / 3628800.0))))
    )
    odd = (quadrant == 1.0) | (quadrant == 3.0)
    cos_part = jnp.where(odd, sine, cosine)
    sin_part = jnp.where(odd, cosine, sine)
    cos_part = jnp.where((quadrant == 1.0) | (quadrant == 2.0), -cos_part, cos_part)
    sin_part = jnp.where(quadrant >= 2.0, -sin_part, sin_part)
    return cos_part, sin_part


def fill_dft(out_ref):
    def body(block, carry):
        row = block * DFT_BLOCK + iota((DFT_BLOCK, LANES), 0)
        lane = iota((DFT_BLOCK, LANES), 1)
        order = (row >> 1).astype(F32)
        turn = (360 * (row & 1)).astype(F32)
        cosine, sine = cos_sin(order * lane.astype(F32) + turn)
        cos_step, sin_step = cos_sin(order * float(LANES))
        rows = pl.ds(pl.multiple_of(block * DFT_BLOCK, DFT_BLOCK), DFT_BLOCK)
        for chunk in range(LON_CHUNKS):
            value = cosine
            if chunk == LON_CHUNKS - 1:
                value = jnp.where(lane < AZIMUTH_STEPS - LANES * chunk, value, 0.0)
            out_ref[rows, LANES * chunk : LANES * (chunk + 1)] = value.astype(BF16)
            cosine, sine = (
                cosine * cos_step - sine * sin_step,
                sine * cos_step + cosine * sin_step,
            )
        return carry

    lax.fori_loop(0, SPECTRAL_ROWS // DFT_BLOCK, body, 0)


def fill_recurrence(first, out_ref):
    order = (first + iota((8, DEGREE_CUTOFF), 0)).astype(F32)
    degree = iota((8, DEGREE_CUTOFF), 1).astype(F32)
    growing = degree > order
    denominator = jnp.where(growing, degree * degree - order * order, 1.0)
    leading = jnp.sqrt(jnp.maximum(4.0 * degree * degree - 1.0, 0.0) / denominator)
    trailing = jnp.sqrt(
        jnp.maximum(
            ((degree - 1.0) * (degree - 1.0) - order * order)
            * (2.0 * degree + 1.0)
            / ((2.0 * degree - 3.0) * denominator),
            0.0,
        )
    )
    out_ref[0:8, :] = jnp.where(growing, leading, 0.0)
    out_ref[8:16, :] = jnp.where(growing, trailing, 0.0)


def seed_logs(first):
    order = (first + iota((8, DEGREE_CUTOFF), 0)).astype(F32)
    factor = (1 + iota((8, DEGREE_CUTOFF), 1)).astype(F32)
    summands = jnp.where(factor <= order, jnp.log(1.0 - 0.5 / factor), 0.0)
    return 0.5 * jnp.log(order[:, 0:1] + 0.5) + 0.5 * jnp.sum(summands, axis=1, keepdims=True)


def legendre_recurrence(first, coef_ref, table_ref):
    band, lane = iota((8, LANES), 0), iota((8, LANES), 1)
    group, part = lane >> 3, lane & 7
    valid = (group < ROW_GROUPS) & (part < GROUP_ROWS)
    row = jnp.where(valid, BAND_ROWS * band + GROUP_ROWS * group + part, 0)
    cos_lat, sin_lat = cos_sin(row.astype(F32) + 0.5)
    weight = jnp.where(valid, math.pi / PARALLEL_LINES * sin_lat, 0.0)
    log_sin = jnp.log(sin_lat)
    seeds = seed_logs(first)

    def body(block, carry):
        state = list(carry)
        for step in range(BLOCK):
            degree = block * BLOCK + step
            for index in range(ORDERS):
                latest, before, log_scale, factor = state[4 * index : 4 * index + 4]
                leading = coef_ref[index, degree]
                trailing = coef_ref[8 + index, degree]
                begin = jnp.where(degree == first + index, 1.0, 0.0)
                advanced = (leading * cos_lat) * latest + (begin - trailing * before)
                row = (index * DEGREE_CUTOFF + degree) * 8
                table_ref[pl.ds(pl.multiple_of(row, 8), 8), :] = advanced * factor
                state[4 * index : 4 * index + 4] = [advanced, latest, log_scale, factor]
        for index in range(ORDERS):
            latest, before, log_scale, factor = state[4 * index : 4 * index + 4]
            largest = jnp.maximum(jnp.abs(latest), jnp.abs(before))
            largest = jnp.where(largest > 0.0, largest, 1.0)
            shrink = 1.0 / largest
            log_scale = log_scale + jnp.log(largest)
            state[4 * index : 4 * index + 4] = [
                latest * shrink,
                before * shrink,
                log_scale,
                jnp.exp(log_scale) * weight,
            ]
        return tuple(state)

    state = []
    for index in range(ORDERS):
        order = jnp.broadcast_to((first + index).astype(F32), (8, LANES))
        start = jnp.broadcast_to(seeds[index : index + 1, :], (8, LANES)) + order * log_sin
        state += [jnp.zeros((8, LANES), F32), jnp.zeros((8, LANES), F32), start, jnp.exp(start) * weight]
    lax.fori_loop(0, DEGREE_CUTOFF // BLOCK, body, tuple(state))


def fill_legendre(table_ref, out_ref):
    for index in range(ORDERS):
        for band in range(BANDS):
            rows = table_ref[pl.ds(index * DEGREE_CUTOFF * 8 + band, DEGREE_CUTOFF, stride=8), :]
            out_ref[index, :, LANES * band : LANES * (band + 1)] = rows.astype(BF16)


def fill_truth(blocks_ref, out_ref, packed_ref):
    lane = iota((8, LANES), 1)
    chunks = [jnp.zeros((8, LANES), F32) for _ in range(LON_CHUNKS)]
    for block in range(MEMBERS):
        first = LON_BLOCK * block
        value = blocks_ref[block].astype(F32)
        shift = first % LANES
        if shift:
            value = pltpu.roll(value, shift, 1)
        for chunk in range(first // LANES, (first + LON_BLOCK - 1) // LANES + 1):
            place = lane + chunk * LANES
            inside = (place >= first) & (place < first + LON_BLOCK)
            chunks[chunk] = jnp.where(inside, value, chunks[chunk])
    for chunk in range(LON_CHUNKS):
        out_ref[:, LANES * chunk : LANES * (chunk + 1)] = chunks[chunk]
        packed_ref[GROUP_ROWS * chunk : GROUP_ROWS * (chunk + 1), :] = chunks[chunk][0:GROUP_ROWS]


def grid_stage(ens, lat, draws_ref, truth_ref, counts_ref):
    row, lane = iota((8, LANES), 0), iota((8, LANES), 1)

    def body(tile, total):
        place = 8 * tile + row
        chunk = (place * 43) >> 8
        part = place - GROUP_ROWS * chunk
        line = (BAND_ROWS * lat + GROUP_ROWS * ens + part).astype(F32)
        kept = (lane + chunk * LANES < AZIMUTH_STEPS) & (ens < ROW_GROUPS)
        weight = jnp.where(kept, cos_sin(line + 0.5)[1], 0.0)
        draws = [draws_ref[i, tile].astype(F32) for i in range(MEMBERS)]
        target = truth_ref[pl.ds(pl.multiple_of(8 * tile, 8), 8), :]
        counts = [None] * MEMBERS
        for i in range(MEMBERS):
            for k in range(i + 1, MEMBERS):
                above = jnp.where(draws[i] > draws[k], 1.0, 0.0)
                turn = jnp.where(draws[i] < draws[k], -1.0, above)
                counts[i] = turn if counts[i] is None else counts[i] + turn
                counts[k] = -turn if counts[k] is None else counts[k] - turn
        spread = jnp.zeros((8, LANES), F32)
        for i in range(MEMBERS):
            gap = draws[i] - target
            above = jnp.where(draws[i] > target, float(MEMBERS - 1), 0.0)
            side = jnp.where(draws[i] < target, -float(MEMBERS - 1), above)
            counts_ref[i, tile] = (side - counts[i]).astype(BF16)
            spread = spread + (jnp.abs(gap) - (draws[i] * counts[i]) * (1.0 / (MEMBERS - 1)))
        return total + jnp.where(kept, weight * spread, 0.0)

    return lax.fori_loop(0, PACKED_TILES, body, jnp.zeros((8, LANES), F32))


def spectral_stage(first, grid_loss, modes_ref, table_ref, wide_ref, lhs_ref, result_ref):
    draws = MEMBERS
    scale = SPECTRAL_WEIGHT * PARALLEL_LINES * AZIMUTH_STEPS / (DEGREE_CUTOFF * (DEGREE_CUTOFF + 1) / 2)
    held = BANDS * PARTS
    lane = iota((held, LANES), 1)
    target = jnp.zeros((held, LANES), F32)
    for member in range(draws):
        value = modes_ref[8 * member : 8 * member + 8].astype(F32).reshape(held, LANES)
        wide_ref[held * member : held * (member + 1), :] = value
        if member < ROW_GROUPS:
            moved = pltpu.roll(value, (8 * member + 8) % LANES, 1)
            target = jnp.where((lane >> 3) == member, moved, target)
    loss = jnp.zeros((1, DEGREE_CUTOFF), F32)
    degree = iota((1, DEGREE_CUTOFF), 1)
    pad = jnp.zeros((14, LANES), F32)
    for index in range(ORDERS):
        for band in range(BANDS):
            lanes = slice(LANES * band, LANES * (band + 1))
            parts = [
                wide_ref[pl.ds(PARTS * band + 2 * index + r, draws, stride=held), :] for r in range(2)
            ]
            aim = PARTS * band + 2 * index
            aims = [target[aim + r : aim + r + 1, :] for r in range(2)]
            lhs_ref[index, :, lanes] = jnp.concatenate(parts + aims + [pad], axis=0).astype(BF16)
    for index in range(ORDERS):
        terms = lax.dot_general(
            lhs_ref[index],
            table_ref[index],
            (((1,), (1,)), ((), ())),
            preferred_element_type=F32,
        )
        real, imag = terms[0:draws], terms[draws : 2 * draws]
        real_aim, imag_aim = terms[2 * draws : 2 * draws + 1], terms[2 * draws + 1 : 2 * draws + 2]
        gap_real, gap_imag = real - real_aim, imag - imag_aim
        square = gap_real * gap_real + gap_imag * gap_imag + SOFTENING_EPS**2
        inverse = lax.rsqrt(square)
        near = square * inverse
        step_real, step_imag = gap_real * inverse, gap_imag * inverse
        pair = jnp.zeros_like(real)
        pull_real, pull_imag = jnp.zeros_like(real), jnp.zeros_like(real)
        for other in range(draws):
            gap_real, gap_imag = real - real[other : other + 1], imag - imag[other : other + 1]
            square = gap_real * gap_real + gap_imag * gap_imag + SOFTENING_EPS**2
            inverse = lax.rsqrt(square)
            pair = pair + square * inverse
            pull_real = pull_real + gap_real * inverse
            pull_imag = pull_imag + gap_imag * inverse
        kept = degree >= first + index
        score = jnp.sum(near, axis=0, keepdims=True) - (
            jnp.sum(pair, axis=0, keepdims=True) - draws * SOFTENING_EPS
        ) / (2.0 * (draws - 1))
        loss = loss + jnp.where(kept, score, 0.0)
        down = jnp.concatenate(
            [step_real - pull_real / (draws - 1), step_imag - pull_imag / (draws - 1)], axis=0
        )
        grad = jnp.where(kept, scale * down, 0.0).astype(BF16)
        back = jnp.dot(grad, table_ref[index], preferred_element_type=F32)
        for band in range(BANDS):
            for r in range(2):
                result_ref[pl.ds(PARTS * band + 2 * index + r, draws, stride=held), :] = back[
                    draws * r : draws * (r + 1), LANES * band : LANES * (band + 1)
                ]
    local = jnp.sum(jnp.sum(grid_loss, axis=0, keepdims=True), axis=1, keepdims=True) / (
        PARALLEL_LINES * AZIMUTH_STEPS
    ) + SPECTRAL_WEIGHT / (DEGREE_CUTOFF * (DEGREE_CUTOFF + 1) / 2) * jnp.sum(loss, axis=1, keepdims=True)
    high = local.astype(BF16).astype(F32)
    middle = (local - high).astype(BF16).astype(F32)
    low = local - high - middle
    row = iota((BANDS, ORDERS, 2, LANES), 1) + iota((BANDS, ORDERS, 2, LANES), 2)
    column = iota((BANDS, ORDERS, 2, LANES), 3)
    high, middle, low = (v.reshape(1, 1, 1, 1) for v in (high, middle, low))
    spare = jnp.where(column == LANES - 8, high, jnp.where(column == LANES - 7, middle, low))
    carries = (row == 0) & (column >= LANES - 8) & (column < LANES - 5)
    return spare, carries


def exchange_kernel(
    own_hbm_ref,
    truth_hbm_ref,
    dft_ref,
    back_in_ref,
    base_ref,
    loss_ref,
    own_ref,
    truth_in_ref,
    packed_ref,
    truth_packed_ref,
    wide_own_ref,
    rows_out_ref,
    rows_in_ref,
    blocks_out_ref,
    blocks_in_ref,
    truth_ref,
    field_ref,
    modes_out_ref,
    modes_in_ref,
    coef_vector_ref,
    coef_ref,
    table_ref,
    legendre_ref,
    counts_out_ref,
    counts_in_ref,
    back_out_ref,
    wide_ref,
    lhs_ref,
    result_ref,
    send_sem,
    recv_sem,
    local_sem,
):
    chan, ens, lat = lax.axis_index("chan"), lax.axis_index("ens"), lax.axis_index("lat")
    mine = ens * BANDS + lat
    first = ORDERS * mine
    y, x = lax.div(ens, 4), lax.rem(lat, 4)
    z = lax.div(lat, 4) * 4 + lax.rem(ens, 4)
    truth_copy = pltpu.make_async_copy(truth_hbm_ref, truth_in_ref, local_sem.at[0])
    truth_copy.start()
    own_copy = pltpu.make_async_copy(own_hbm_ref, own_ref, local_sem.at[1])
    own_copy.start()

    barrier = pltpu.get_barrier_semaphore()

    def each_group(y_step, visit):
        peer_y = lax.rem(y + y_step, 4)

        def one(z_step, x_step):
            peer_z, peer_x = lax.rem(z + z_step, 8), lax.rem(x + x_step, 4)
            visit(peer_y * 4 + lax.rem(peer_z, 4), lax.div(peer_z, 4) * 4 + peer_x)

        def body(step, carry):
            z_step = 4 + lax.div(step + 1, 2) * (1 - 2 * lax.rem(step, 2))
            for x_step in FAR_FIRST:
                one(z_step, x_step)
            return carry

        lax.fori_loop(0, 8 if y_step else 7, body, 0)
        if y_step == 0:
            for x_step in FAR_FIRST[:3]:
                one(0, x_step)

    def greet(peer_ens, peer_lat):
        pl.semaphore_signal(
            barrier, inc=1, device_id=(chan, peer_ens, peer_lat), device_id_type=MESH
        )

    for y_step in FAR_FIRST:
        each_group(y_step, greet)

    def copy(source, target, kind, peer_ens, peer_lat):
        return pltpu.make_async_remote_copy(
            src_ref=source,
            dst_ref=target,
            send_sem=send_sem.at[kind],
            recv_sem=recv_sem.at[kind],
            device_id=(chan, peer_ens, peer_lat),
            device_id_type=MESH,
        )

    def to_members(source, target, kind):
        def body(step, carry):
            peer_y = lax.rem(y + FAR_FIRST[0] + lax.div(step, 4), 4)
            peer = peer_y * 4 + lax.rem(ens + 2 + step, 4)

            @pl.when(peer != ens)
            def _():
                copy(source.at[peer], target.at[ens], kind, peer, lat).start()

            return carry

        lax.fori_loop(0, MEMBERS, body, 0)
        target[ens] = source[ens]

    def to_groups(source, target, kind, y_step):
        def send(peer_ens, peer_lat):
            copy(
                source.at[peer_ens * BANDS + peer_lat], target.at[mine], kind, peer_ens, peer_lat
            ).start()

        each_group(y_step, send)

    def all_of(source, target, kind, count):
        return copy(source.at[pl.ds(0, count)], target.at[pl.ds(0, count)], kind, ens, lat)

    wide_own_ref[88:96, :] = jnp.zeros((8, LON_PADDED), F32)
    wide_own_ref[:, LON_PADDED - LANES :] = jnp.zeros((96, LANES), F32)
    truth_copy.wait()
    wide_own_ref[0:BAND_ROWS, 0:LON_BLOCK] = truth_in_ref[...].astype(F32)
    for group in range(ROW_GROUPS):
        blocks_out_ref[group] = wide_own_ref[GROUP_ROWS * group : GROUP_ROWS * group + 8, 0:LANES].astype(BF16)
    blocks_out_ref[ROW_GROUPS] = jnp.zeros((8, LANES), BF16)

    pl.semaphore_wait(barrier, GROUPS - 1)
    to_members(blocks_out_ref, blocks_in_ref, 0)
    own_copy.wait()
    wide_own_ref[0:BAND_ROWS, 0:AZIMUTH_STEPS] = own_ref[...].astype(F32)
    for group in range(ROW_GROUPS):
        for chunk in range(LON_CHUNKS):
            packed_ref[GROUP_ROWS * chunk : GROUP_ROWS * (chunk + 1), :] = wide_own_ref[
                GROUP_ROWS * group : GROUP_ROWS * (group + 1), LANES * chunk : LANES * (chunk + 1)
            ]
        rows_out_ref[group] = packed_ref[...].reshape(PACKED_TILES, 8, LANES).astype(BF16)
    rows_out_ref[ROW_GROUPS] = jnp.zeros((PACKED_TILES, 8, LANES), BF16)
    to_members(rows_out_ref, rows_in_ref, 1)
    fill_recurrence(first, coef_vector_ref)
    coef_copy = pltpu.make_async_copy(coef_vector_ref, coef_ref, local_sem.at[2])
    coef_copy.start()
    for pair in range(7):
        both = [
            wide_own_ref[GROUP_ROWS * group : GROUP_ROWS * group + 8, :] for group in (2 * pair, 2 * pair + 1)
        ]
        field_ref[16 * pair : 16 * pair + 16, :] = jnp.concatenate(both, axis=0).astype(BF16)
    fill_dft(dft_ref)

    all_of(blocks_out_ref, blocks_in_ref, 0, MEMBERS - 1).wait_recv()
    fill_truth(blocks_in_ref, truth_ref, truth_packed_ref)
    both = [wide_own_ref[84:92, :], truth_ref[...]]
    field_ref[112:128, :] = jnp.concatenate(both, axis=0).astype(BF16)

    for y_step in FAR_FIRST:
        block = lax.rem(y + y_step, 4)
        modes = lax.dot_general(
            dft_ref[pl.ds(pl.multiple_of(block * 192, 192), 192), :],
            field_ref[...],
            (((1,), (1,)), ((), ())),
            preferred_element_type=F32,
        )
        modes_out_ref[pl.ds(block * 32, 32)] = modes.reshape(32, ORDERS, 2, LANES).astype(BF16)
        to_groups(modes_out_ref, modes_in_ref, 2, y_step)
    modes_in_ref[mine] = modes_out_ref[mine]

    coef_copy.wait()
    legendre_recurrence(first, coef_ref, table_ref)
    fill_legendre(table_ref, legendre_ref)

    all_of(rows_out_ref, rows_in_ref, 1, MEMBERS - 1).wait_recv()
    grid_loss = grid_stage(ens, lat, rows_in_ref, truth_packed_ref, counts_out_ref)
    to_members(counts_out_ref, counts_in_ref, 3)

    all_of(modes_out_ref, modes_in_ref, 2, GROUPS - 1).wait_recv()
    spare, carries = spectral_stage(
        first, grid_loss, modes_in_ref, legendre_ref, wide_ref, lhs_ref, result_ref
    )
    held = BANDS * PARTS
    for y_step in FAR_FIRST:
        block = lax.rem(y + y_step, 4)
        for part in range(4):
            member = block * 4 + part
            value = result_ref[pl.ds(pl.multiple_of(member * held, held), held), :]
            value = jnp.where(carries, spare, value.reshape(BANDS, ORDERS, 2, LANES))
            back_out_ref[pl.ds(member * BANDS, BANDS)] = value.astype(BF16)
        to_groups(back_out_ref, back_in_ref, 4, y_step)
    back_in_ref[mine] = back_out_ref[mine]

    all_of(counts_out_ref, counts_in_ref, 3, MEMBERS - 1).wait_recv()
    for group in range(ROW_GROUPS):
        packed_ref[...] = counts_in_ref[group].astype(F32).reshape(PACKED_ROWS, LANES)
        line = BAND_ROWS * lat + GROUP_ROWS * group + iota((8, LANES), 0)
        weight = (cos_sin(line.astype(F32) + 0.5)[1] / (MEMBERS - 1))[0:GROUP_ROWS]
        for chunk in range(LON_CHUNKS):
            base_ref[8 * group : 8 * group + GROUP_ROWS, LANES * chunk : LANES * (chunk + 1)] = (
                weight * packed_ref[GROUP_ROWS * chunk : GROUP_ROWS * (chunk + 1), :]
            )
    all_of(back_out_ref, back_in_ref, 4, GROUPS - 1).wait_recv()
    total = jnp.zeros((2, LANES), F32)
    for block in range(16):
        total = total + jnp.sum(back_in_ref[8 * block : 8 * block + 8, 0].astype(F32), axis=0)
    row, column = iota((2, LANES), 0), iota((2, LANES), 1)
    total = jnp.where((row == 0) & (column >= LANES - 8) & (column < LANES - 5), total, 0.0)
    loss_ref[...] = jnp.sum(jnp.sum(total, axis=0, keepdims=True), axis=1, keepdims=True)

    all_of(blocks_out_ref, blocks_in_ref, 0, MEMBERS - 1).wait_send()
    all_of(rows_out_ref, rows_in_ref, 1, MEMBERS - 1).wait_send()
    all_of(modes_out_ref, modes_in_ref, 2, GROUPS - 1).wait_send()
    all_of(counts_out_ref, counts_in_ref, 3, MEMBERS - 1).wait_send()
    all_of(back_out_ref, back_in_ref, 4, GROUPS - 1).wait_send()


def exchange(own, target):
    rows = (MEMBERS, PACKED_TILES, 8, LANES)
    blocks = (MEMBERS, 8, LANES)
    modes = (GROUPS, ORDERS, 2, LANES)
    return pl.pallas_call(
        exchange_kernel,
        out_shape=(
            jax.ShapeDtypeStruct((SPECTRAL_ROWS, LON_PADDED), BF16),
            jax.ShapeDtypeStruct(modes, BF16),
            jax.ShapeDtypeStruct((LANES, LON_PADDED), F32),
            jax.ShapeDtypeStruct((1, 1), F32),
        ),
        in_specs=[pl.BlockSpec(memory_space=pltpu.HBM)] * 2,
        out_specs=tuple([pl.BlockSpec(memory_space=VMEM)] * 4),
        scratch_shapes=[
            VMEM((BAND_ROWS, AZIMUTH_STEPS), BF16),
            VMEM((BAND_ROWS, LON_BLOCK), BF16),
            VMEM((PACKED_ROWS, LANES), F32),
            VMEM((PACKED_ROWS, LANES), F32),
            VMEM((96, LON_PADDED), F32),
            VMEM(rows, BF16),
            VMEM(rows, BF16),
            VMEM(blocks, BF16),
            VMEM(blocks, BF16),
            VMEM((8, LON_PADDED), F32),
            VMEM((LANES, LON_PADDED), BF16),
            VMEM(modes, BF16),
            VMEM(modes, BF16),
            VMEM((16, DEGREE_CUTOFF), F32),
            pltpu.SMEM((16, DEGREE_CUTOFF), F32),
            VMEM((ORDERS * DEGREE_CUTOFF * 8, LANES), F32),
            VMEM((ORDERS, DEGREE_CUTOFF, BANDS * LANES), BF16),
            VMEM(rows, BF16),
            VMEM(rows, BF16),
            VMEM(modes, BF16),
            VMEM((SPECTRAL_ROWS, LANES), F32),
            VMEM((ORDERS, 48, BANDS * LANES), BF16),
            VMEM((SPECTRAL_ROWS, LANES), F32),
            pltpu.SemaphoreType.DMA((5,)),
            pltpu.SemaphoreType.DMA((5,)),
            pltpu.SemaphoreType.DMA((3,)),
        ],
        compiler_params=params(collective_id=0, has_side_effects=True),
        cost_estimate=pl.CostEstimate(flops=800_000_000, bytes_accessed=8 << 20, transcendentals=0),
    )(own, target)


def final_kernel(table_ref, modes_ref, base_ref, out_ref):
    modes = modes_ref[...].astype(F32).T.astype(BF16)
    for chunk in range(LON_CHUNKS // 2):
        first = 2 * LANES * chunk
        lanes = slice(first, first + 2 * LANES)
        width = min(2 * LANES, AZIMUTH_STEPS - first)
        wave = jnp.dot(modes, table_ref[:, lanes], preferred_element_type=F32)
        for group in range(ROW_GROUPS):
            rows = slice(8 * group, 8 * group + GROUP_ROWS)
            total = base_ref[rows, lanes] + wave[rows]
            out_ref[GROUP_ROWS * group : GROUP_ROWS * (group + 1), 0, first : first + width] = total[
                :, 0:width
            ]


def final(table, modes, base):
    return pl.pallas_call(
        final_kernel,
        out_shape=jax.ShapeDtypeStruct((BAND_ROWS, 1, AZIMUTH_STEPS), F32),
        in_specs=[pl.BlockSpec(memory_space=VMEM)] * 3,
        out_specs=pl.BlockSpec(memory_space=VMEM),
        compiler_params=params(),
        cost_estimate=pl.CostEstimate(flops=400_000_000, bytes_accessed=4 << 20, transcendentals=0),
    )(table, modes, base)


def local(model_outputs, verifying_truth):
    table, back, base, shared = exchange(pltpu.with_memory_space_constraint(model_outputs[0, 0], pltpu.HBM), pltpu.with_memory_space_constraint(verifying_truth[0], pltpu.HBM))
    other = lax.ppermute(shared, "chan", [(0, 1), (1, 0)])
    slope = final(table, back.reshape(SPECTRAL_ROWS, LANES), base)
    return (slope.reshape(1, 1, BAND_ROWS, AZIMUTH_STEPS), (shared + other)[0, 0])


def solution(mesh):
    return jax.shard_map(
        local,
        mesh=mesh,
        in_specs=(P("ens", "chan", "lat", None), P("chan", "lat", "ens")),
        out_specs=(P("ens", "chan", "lat", None), P()),
        check_vma=False,
    )
```
